32 devices in a mesh: groups: 2 (over x), seq: 8 (over z, y), chan: 2 (over core).
Axes of the slice: x: 2, y: 2, z: 4, core: 2. Of those that a mesh axis runs over, the one named last changes fastest.
Arguments:
- inputs: bfloat16 [8192, 768], P(('groups', 'seq')), parts along dimension 0, may hold values from -6 to 6
- enc_weight: bfloat16 [768, 5, 1536], P('seq', None, 'chan'), may hold values from -0.09375 to 0.09375
- dec_weight: bfloat16 [768, 5, 1536], P('seq', None, 'chan'), may hold values from -0.0625 to 0.0625
- cotangent: bfloat16 [8192, 768], P(('groups', 'seq'), 'chan'), parts along dimension 0, may hold values from -6 to 6
Outputs:
- mixed_out: bfloat16 [8192, 768], P(('groups', 'seq'), 'chan'), parts along dimension 0
- input_grad: bfloat16 [8192, 768], P(('groups', 'seq'), 'chan'), parts along dimension 0
- enc_grad: bfloat16 [1536, 5, 1536], P(('groups', 'seq'), None, 'chan'), parts along dimension 0
- dec_grad: bfloat16 [1536, 5, 1536], P(('groups', 'seq'), None, 'chan'), parts along dimension 0
The draws below stay inside these ranges and needn't reach their ends.
There are 2 independent parts, one for each index of `groups`. The reference program is written for one: setup_inputs(seed, part) draws one part's arguments, and reference() takes and returns one part's arrays. A program takes and returns all parts, laid end to end along the dimension named above; an argument that names none is the same for every part. Nothing has to cross between parts.
All inputs are finite; a program needn't handle non-finite values.
Results may differ from the reference program's by a relative error of at most 0.012.
Values may be sent and summed in bfloat16 or wider, within the bound.
A program may use at most 128 MiB of HBM per device.

```python
import jax
import jax.numpy as jnp
from jax import lax

C1 = 768
C2 = 1536
K = 5
R1 = 256
R0 = 512
L1 = 2048
L0 = 4096
N_SEQ = 8


def spiked(array, key, source, target, shards_of, factor):
    owner, partner = [(jnp.arange(array.shape[dim]) // (array.shape[dim] // shards_of)).reshape([-1 if axis == dim else 1 for axis in range(array.ndim)]) for dim in (source, target)]
    chosen = jax.random.permutation(key, shards_of)[partner]
    strong = (owner == chosen) | (owner == (partner + shards_of // 2) % shards_of)
    return jnp.where(strong, factor * array, array)


def block_levels(stream_key, shape, shards, smallest, top_value):
    level = 1.0
    for position, parts in shards:
        steps = jax.random.uniform(jax.random.fold_in(jax.random.fold_in(stream_key, 6), position), (parts,), jnp.float32, smallest / len(shards), top_value / len(shards))
        level = level * jnp.repeat(jnp.exp(steps), shape[position] // parts).reshape((-1,) + (1,) * (len(shape) - 1 - position))
    return level


def noise(stream_key, extent, deviation, bound, cuts=(), held_as=jnp.bfloat16):
    entries = deviation * jax.random.normal(stream_key, extent, jnp.float32)
    if cuts:
        entries = entries * block_levels(stream_key, extent, cuts, -0.22, 0.18)
    return jnp.clip(entries, -bound, bound).astype(held_as)


def bell_draw_with(key, extent, scale, bound, split, heavy, kind=jnp.bfloat16):
    drawn = scale * jax.random.normal(key, extent, jnp.float32)
    if split:
        drawn = drawn * block_levels(key, extent, split, -0.22, 0.18)
    return jnp.clip(spiked(drawn, jax.random.fold_in(key, 3), *heavy), -bound, bound).astype(kind)


def setup_inputs(seed: int = 0, part: int = 0) -> dict:
    key_of = jax.random.split(jax.random.key(seed), 5)
    part_splits = jax.random.split(jax.random.fold_in(key_of[4], part), 5)
    return {
        "inputs": bell_draw_with(part_splits[0], (L0, C1), 1.0, 6.0, ((0, 8),), (0, 1, 8, 2.0)),
        "enc_weight": noise(key_of[1], (C1, K, C2), (K * C1) ** -0.5, 0.09375, ((0, 8), (2, 2))),
        "dec_weight": noise(key_of[2], (C1, K, C2), (K * C2) ** -0.5, 0.0625, ((0, 8), (2, 2))),
        "cotangent": bell_draw_with(part_splits[3], (L0, C1), 1.0, 6.0, ((0, 8), (1, 2)), (0, 1, 8, 2.0)),
    }


def gelu_fn(values):
    return jax.nn.gelu(values, approximate=True)

def reference(inputs, enc_weight, dec_weight, cotangent):
    pooled = (inputs.astype(jnp.float32).reshape(L1, 2, C1).sum(axis=1) * 0.5).astype(jnp.bfloat16)
    pad_pool = jnp.pad(pooled, ((2, 2), (0, 0)))
    pre_act = jnp.zeros((L1, C2), jnp.float32)
    for tap_index in range(K):
        pre_act = pre_act + jnp.dot(pad_pool[tap_index:tap_index + L1], enc_weight[:, tap_index, :], preferred_element_type=jnp.float32)
    hidden = gelu_fn(pre_act).astype(jnp.bfloat16)
    upsampled = jnp.repeat(hidden, 2, axis=0)
    pad_up = jnp.pad(upsampled, ((2, 2), (0, 0)))
    decoded = jnp.zeros((L0, C1), jnp.float32)
    for tap_index in range(K):
        decoded = decoded + lax.dot_general(pad_up[tap_index:tap_index + L0], dec_weight[:, tap_index, :], (((1,), (1,)), ((), ())), preferred_element_type=jnp.float32)
    mixed_out = (inputs.astype(jnp.float32) + decoded).astype(jnp.bfloat16)
    pad_cot = jnp.pad(cotangent, ((2, 2), (0, 0)))
    up_grad = jnp.zeros((L0, C2), jnp.float32)
    for tap_index in range(K):
        up_grad = up_grad + jnp.dot(pad_cot[4 - tap_index:4 - tap_index + L0], dec_weight[:, tap_index, :], preferred_element_type=jnp.float32)
    hid_grad = up_grad.reshape(L1, 2, C2).sum(axis=1)
    _, pullback = jax.vjp(gelu_fn, pre_act)
    pre_grad = pullback(hid_grad)[0].astype(jnp.bfloat16)
    pad_grad = jnp.pad(pre_grad, ((2, 2), (0, 0)))
    pool_grad = jnp.zeros((L1, C1), jnp.float32)
    for tap_index in range(K):
        pool_grad = pool_grad + lax.dot_general(pad_grad[4 - tap_index:4 - tap_index + L1], enc_weight[:, tap_index, :], (((1,), (1,)), ((), ())), preferred_element_type=jnp.float32)
    input_grad = (cotangent.astype(jnp.float32) + 0.5 * jnp.repeat(pool_grad, 2, axis=0)).astype(jnp.bfloat16)

    def add_block(carry, block_index):
        enc_total, dec_total = carry
        coarse_start = (block_index * R1).astype(jnp.int32)
        fine_start = (block_index * R0).astype(jnp.int32)
        block_pool = lax.dynamic_slice_in_dim(pad_pool, coarse_start, R1 + 4, 0)
        block_grad = lax.dynamic_slice_in_dim(pre_grad, coarse_start, R1, 0)
        block_up = lax.dynamic_slice_in_dim(pad_up, fine_start, R0 + 4, 0)
        block_cot = lax.dynamic_slice_in_dim(cotangent, fine_start, R0, 0)
        enc_terms = jnp.stack([jnp.dot(block_pool[tap_index:tap_index + R1].T, block_grad, preferred_element_type=jnp.float32) for tap_index in range(K)], axis=1)
        dec_terms = jnp.stack([jnp.dot(block_cot.T, block_up[tap_index:tap_index + R0], preferred_element_type=jnp.float32) for tap_index in range(K)], axis=1)
        enc_total = enc_total + enc_terms.astype(jnp.bfloat16).astype(jnp.float32)
        dec_total = dec_total + dec_terms.astype(jnp.bfloat16).astype(jnp.float32)
        return ((enc_total, dec_total), None)
    zeros_init = (jnp.zeros((C1, K, C2), jnp.float32), jnp.zeros((C1, K, C2), jnp.float32))
    (enc_total, dec_total), _ = lax.scan(add_block, zeros_init, jnp.arange(N_SEQ, dtype=jnp.int32))
    return (mixed_out, input_grad, enc_total.astype(jnp.bfloat16), dec_total.astype(jnp.bfloat16))
```

```python
import functools
import math

import jax
import jax.numpy as jnp
from jax import lax
from jax.experimental import pallas as pl
from jax.experimental.pallas import tpu as pltpu
from jax.sharding import PartitionSpec as P

BF16 = jnp.bfloat16
F32 = jnp.float32


def shift(array, by):
    length = array.shape[0]
    if by == 0:
        return array
    pad = jnp.zeros((abs(by),) + array.shape[1:], array.dtype)
    if by > 0:
        return jnp.concatenate([array[by:], pad], axis=0)
    return jnp.concatenate([pad, array[: length + by]], axis=0)


def to_columns(array, parts):
    rows, cols = array.shape
    blocks = array.reshape(rows, parts, cols // parts).transpose(1, 0, 2)
    return lax.all_to_all(blocks, "seq", 0, 0, tiled=True)


def to_rows(blocks):
    parts, rows, cols = blocks.shape
    got = lax.all_to_all(blocks, "seq", 0, 0, tiled=True)
    return got.transpose(1, 0, 2).reshape(rows, parts * cols)


PIECES = 2


def ring_place(index, n):
    if n != 8:
        return index
    y = lax.rem(index, 2)
    z = index // 2
    return z + y * (n - 1 - 2 * z)


def ring_index(place, n):
    place = lax.rem(place + 2 * n, n)
    if n != 8:
        return place
    back = place // (n // 2)
    return 2 * place + back * (2 * n - 1 - 4 * place)


def gelu_and_slope(v):
    scale = math.sqrt(2.0 / math.pi)
    square = v * v
    th = jnp.tanh(scale * (v + 0.044715 * square * v))
    up = 0.5 * (1.0 + th)
    slope = up + 0.5 * v * (1.0 - th * th) * (scale * (1.0 + 3.0 * 0.044715 * square))
    return v * up, slope


def ring_kernel(
    n, x_ref, y_ref, enc_ref, dec_ref, out_ref, slots, term, mine,
    rs_send, rs_recv, ag_send, ag_recv, local_sem,
):
    me = lax.axis_index("seq")
    place = ring_place(me, n)
    nexts = (ring_index(place + 1, n), ring_index(place - 1, n))
    half = x_ref.shape[1]
    share = enc_ref.shape[1]
    side = half // 2
    piece = side // PIECES

    barrier = pltpu.get_barrier_semaphore()
    for other in nexts:
        pl.semaphore_signal(
            barrier, inc=1, device_id={"seq": other}, device_id_type=pl.DeviceIdType.MESH
        )
    pl.semaphore_wait(barrier, 2)

    def signed(d, steps):
        return place - steps if d == 0 else place + steps

    def own_term(d, steps):
        chunk = ring_index(signed(d, steps), n)
        at = pl.ds(d * side, side)
        a = jnp.dot(x_ref[chunk, at, :], enc_ref[...], preferred_element_type=jnp.float32)
        b = jnp.dot(y_ref[chunk, at, :], dec_ref[...], preferred_element_type=jnp.float32)
        return a, b

    def rs_copy(d, s, q):
        at = pl.ds(q * piece, piece)
        return pltpu.make_async_remote_copy(
            src_ref=slots.at[d, s, at],
            dst_ref=slots.at[d, s + 1, at],
            send_sem=rs_send.at[d, s, q],
            recv_sem=rs_recv.at[d, s, q],
            device_id={"seq": nexts[d]},
            device_id_type=pl.DeviceIdType.MESH,
        )

    def ag_copy(d, s, q, first):
        at = pl.ds(d * side + q * piece, piece)
        owner = ring_index(signed(d, s), n)
        return pltpu.make_async_remote_copy(
            src_ref=mine.at[at] if first else out_ref.at[owner, at],
            dst_ref=out_ref.at[owner, at],
            send_sem=ag_send.at[d, s, q],
            recv_sem=ag_recv.at[d, s, q],
            device_id={"seq": nexts[d]},
            device_id_type=pl.DeviceIdType.MESH,
        )

    for d in range(2):
        a, b = own_term(d, 1)
        slots[d, 0, :, :share] = a.astype(BF16)
        slots[d, 0, :, share:] = b.astype(BF16)
        for q in range(PIECES):
            rs_copy(d, 0, q).start()

    def fill(s):
        for d in range(2):
            a, b = own_term(d, s + 2)
            term[d, :, :share] = a
            term[d, :, share:] = b

    def rs_step(s, carry):
        fill(s)
        for q in range(PIECES):
            at = pl.ds(q * piece, piece)
            for d in range(2):
                rs_copy(d, s, q).wait_recv()
                total = slots[d, s + 1, at, :].astype(F32) + term[d, at, :]
                slots[d, s + 1, at, :] = total.astype(BF16)
                rs_copy(d, s + 1, q).start()
        return carry

    lax.fori_loop(0, n - 2, rs_step, 0)
    fill(n - 2)
    for q in range(PIECES):
        at = pl.ds(q * piece, piece)
        for d in range(2):
            rs_copy(d, n - 2, q).wait_recv()
            rows = pl.ds(d * side + q * piece, piece)
            pre = slots[d, n - 1, at, :share].astype(F32) + term[d, at, :share]
            grad = slots[d, n - 1, at, share:].astype(F32) + term[d, at, share:]
            value, slope = gelu_and_slope(pre)
            mine[rows, :share] = value.astype(BF16)
            mine[rows, share:] = (grad * slope).astype(BF16)
            ag_copy(d, 0, q, True).start()
    local = pltpu.make_async_copy(mine, out_ref.at[me], local_sem)
    local.start()

    def ag_step(s, carry):
        for q in range(PIECES):
            for d in range(2):
                incoming(d, s, q).wait_recv()
                ag_copy(d, s + 1, q, False).start()
        return carry

    def incoming(d, s, q):
        at = pl.ds(d * side + q * piece, piece)
        owner = ring_index(signed(d, s + 1), n)
        return pltpu.make_async_remote_copy(
            src_ref=mine.at[at],
            dst_ref=out_ref.at[owner, at],
            send_sem=ag_send.at[d, s, q],
            recv_sem=ag_recv.at[d, s, q],
            device_id={"seq": nexts[d]},
            device_id_type=pl.DeviceIdType.MESH,
        )

    lax.fori_loop(0, n - 2, ag_step, 0)
    for q in range(PIECES):
        for d in range(2):
            incoming(d, n - 2, q).wait_recv()

    def drain(s, carry):
        for q in range(PIECES):
            for d in range(2):
                rs_copy(d, s, q).wait_send()
                ag_copy(d, s, q, True).wait_send()
        return carry

    lax.fori_loop(0, n - 1, drain, 0)
    local.wait()


def ring(pool_taps, cot_taps, enc_mat, dec_mat, n):
    half = pool_taps.shape[1]
    share = enc_mat.shape[1]
    depth = enc_mat.shape[0]
    vmem = pl.BlockSpec(memory_space=pltpu.VMEM)
    steps = (2, n - 1, PIECES)
    return pl.pallas_call(
        functools.partial(ring_kernel, n),
        out_shape=jax.ShapeDtypeStruct((n, half, 2 * share), BF16),
        in_specs=[vmem] * 4,
        out_specs=pl.BlockSpec(memory_space=pl.ANY),
        scratch_shapes=[
            pltpu.VMEM((2, n, half // 2, 2 * share), BF16),
            pltpu.VMEM((2, half // 2, 2 * share), F32),
            pltpu.VMEM((half, 2 * share), BF16),
            pltpu.SemaphoreType.DMA(steps),
            pltpu.SemaphoreType.DMA(steps),
            pltpu.SemaphoreType.DMA(steps),
            pltpu.SemaphoreType.DMA(steps),
            pltpu.SemaphoreType.DMA,
        ],
        compiler_params=pltpu.CompilerParams(
            collective_id=0, has_side_effects=True, vmem_limit_bytes=48 * 2**20
        ),
        cost_estimate=pl.CostEstimate(
            flops=4 * n * half * depth * share,
            bytes_accessed=4 * n * half * share * 2,
            transcendentals=half * share,
        ),
    )(pool_taps, cot_taps, enc_mat, dec_mat)


def wide_shards(inputs, enc_weight, dec_weight, cotangent):
    parts = lax.axis_size("seq")
    rows, width = inputs.shape
    half = rows // 2
    total = half * parts
    block, taps, share = enc_weight.shape
    half_width = cotangent.shape[1]

    pooled = (inputs.astype(F32).reshape(half, 2, width).sum(axis=1) * 0.5).astype(BF16)
    cot_full = lax.all_gather(cotangent, "chan", axis=1, tiled=True)
    core = lax.axis_index("chan")
    cores = lax.axis_size("chan")
    few = half // cores
    leaving = jnp.concatenate(
        [
            lax.dynamic_slice_in_dim(pooled, core * few, few, 0),
            lax.dynamic_slice_in_dim(cot_full, core * 2 * few, 2 * few, 0),
        ],
        axis=0,
    )
    columns = to_columns(leaving, parts).reshape(parts, 1, 3 * few, block)
    columns = lax.all_gather(columns, "chan", axis=1, tiled=True)
    pool_col = columns[:, :, :few].reshape(total, block)
    cot_col = columns[:, :, few:].reshape(total, 2, block).astype(F32)
    even = cot_col[:, 0]
    odd = cot_col[:, 1]
    pair = (even + odd).astype(BF16)
    cross = (odd + shift(even, 1)).astype(BF16)
    before = jnp.concatenate([even[:1].astype(BF16), cross[:-1]], axis=0)
    pool_taps = jnp.concatenate([shift(pool_col, t - 2) for t in range(taps)], axis=1)
    cot_taps = jnp.concatenate([shift(pair, 1), cross, pair, before, shift(pair, -1)], axis=1)
    enc_mat = enc_weight.transpose(1, 0, 2).reshape(taps * block, share)
    dec_mat = dec_weight.transpose(1, 0, 2).reshape(taps * block, share)

    joint = ring(
        pool_taps.reshape(parts, half, taps * block),
        cot_taps.reshape(parts, half, taps * block),
        enc_mat,
        dec_mat,
        parts,
    ).reshape(total, 2 * share)
    hidden_all = joint[:, :share]
    grad_all = joint[:, share:]

    contract_rows = (((0,), (0,)), ((), ()))
    contract_last = (((1,), (1,)), ((), ()))
    dec_grad = lax.dot_general(cot_taps, hidden_all, contract_rows, preferred_element_type=F32)
    enc_grad = lax.dot_general(pool_taps, grad_all, contract_rows, preferred_element_type=F32)
    dec_grad = dec_grad.astype(BF16).reshape(taps, block, share).transpose(1, 0, 2)
    enc_grad = enc_grad.astype(BF16).reshape(taps, block, share).transpose(1, 0, 2)

    dec_out = lax.dot_general(hidden_all, dec_mat, contract_last, preferred_element_type=F32)
    p0, p1, p2, p3, p4 = [dec_out[:, t * block : (t + 1) * block] for t in range(taps)]
    after4 = shift(p4, 1)
    before0 = shift(p0, -1)
    dec_even = before0 + shift(p1, -1) + p2 + p3 + after4
    dec_odd = before0 + p1 + p2 + shift(p3, 1) + after4
    decoded = jnp.stack([dec_even, dec_odd], axis=1).astype(BF16).reshape(parts, rows, block)
    enc_out = lax.dot_general(grad_all, enc_mat, contract_last, preferred_element_type=F32)
    pool_grad = sum(shift(enc_out[:, t * block : (t + 1) * block], 2 - t) for t in range(taps))
    pool_grad = pool_grad.astype(BF16).reshape(parts, half, block)
    mine = jnp.concatenate([decoded, pool_grad], axis=1)
    mine = lax.psum_scatter(mine, "chan", scatter_dimension=1, tiled=True)
    mine = lax.all_gather(to_rows(mine), "chan", axis=0, tiled=True)
    col_start = core * half_width
    mine = lax.dynamic_slice_in_dim(mine, col_start, half_width, 1).astype(F32)

    skip = lax.dynamic_slice_in_dim(inputs, col_start, half_width, 1)
    mixed_out = (skip.astype(F32) + mine[:rows]).astype(BF16)
    input_grad = (cotangent.astype(F32) + 0.5 * jnp.repeat(mine[rows:], 2, axis=0)).astype(BF16)
    return mixed_out, input_grad, enc_grad, dec_grad


LANES = 128
HALO = 16
EDGE = 8


def pair_kernel(
    pc_ref, enc_ref, dec_ref, grad_ref, out_ref,
    rows_all, weights, folded, z_enc, z_dec, hid, pre_grad, g_taps, h_taps,
    enc_sum, dec_sum, part, give, take, give_y, take_y, grad_give,
    local_sem, wy_send, wy_recv, wz_send, wz_recv, wx_send, wx_recv,
    edge_send, edge_z, edge_y, edge_c, edge_fwd, edge_ysend, edge_csend,
    own_send, pz_send, pz_recv, py_send, py_recv, pc_send, pc_recv,
    give_sem, take_sem, grad_sem,
):
    g = lax.axis_index("groups")
    s = lax.axis_index("seq")
    c = lax.axis_index("chan")
    z, y = s // 2, lax.rem(s, 2)
    last = lax.axis_size("seq") // 2 - 1
    chunk, wide = pc_ref.shape[1], pc_ref.shape[2]
    cell = 2 * chunk
    taps, block = enc_ref.shape[0], enc_ref.shape[1]
    share = enc_ref.shape[2] // 2
    half = block // 2
    inner = chunk - HALO
    ids = pl.DeviceIdType.MESH
    to_y, to_x, to_c = {"seq": s + 1 - 2 * y}, {"groups": 1 - g}, {"chan": 1 - c}
    to_left, to_right = {"seq": s - 2}, {"seq": s + 2}
    has_left, has_right = z > 0, z < last

    barrier = pltpu.get_barrier_semaphore()
    for where in (to_y, to_x, to_c):
        pl.semaphore_signal(barrier, inc=1, device_id=where, device_id_type=ids)

    @pl.when(has_left)
    def _():
        pl.semaphore_signal(barrier, inc=1, device_id=to_left, device_id_type=ids)

    @pl.when(has_right)
    def _():
        pl.semaphore_signal(barrier, inc=1, device_id=to_right, device_id_type=ids)

    inside = jnp.where(has_left, 1, 0) + jnp.where(has_right, 1, 0)
    pl.semaphore_wait(barrier, 3 + inside)

    def remote(src, dst, send, recv, where):
        return pltpu.make_async_remote_copy(
            src_ref=src, dst_ref=dst, send_sem=send, recv_sem=recv,
            device_id=where, device_id_type=ids,
        )

    def lanes(index, width):
        return pl.ds(pl.multiple_of(index * width, LANES), width)

    sources = (enc_ref, dec_ref)

    def own_weight(w, t):
        return pltpu.make_async_copy(
            sources[w].at[t, :, lanes(y, share)],
            weights.at[w, pl.ds(pl.multiple_of(s * block, HALO), block), pl.ds(t * share, share)],
            local_sem.at[w, t],
        )

    def weight_to_y(w, t, side):
        at = pl.ds(pl.multiple_of(side * half, HALO), half)
        row = pl.multiple_of(s * block + side * half, HALO)
        return remote(
            sources[w].at[t, at, lanes(1 - y, share)],
            weights.at[w, pl.ds(row, half), pl.ds(t * share, share)],
            wy_send.at[w, t, side], wy_recv.at[w, t, side], to_y,
        )

    def slab(w, b, side):
        return weights.at[w, pl.ds(pl.multiple_of(b * block + side * half, HALO), half), :]

    def weight_z(w, zz, b, d, where):
        ref = slab(w, 2 * zz + b, g)
        return remote(ref, ref, wz_send.at[d, w, zz, b], wz_recv.at[w, zz, b], where)

    def weight_x(w, zz, b, side):
        ref = slab(w, 2 * zz + b, side)
        return remote(ref, ref, wx_send.at[w, zz, b], wx_recv.at[w, zz, b], to_x)

    def edge_of(zz, yy, cc):
        at = pl.multiple_of(HALO + (2 * zz + yy) * chunk + yy * inner, HALO)
        return rows_all.at[:, pl.ds(at, HALO), lanes(cc, wide)]

    def inner_of(i, zz, yy, cc):
        at = pl.multiple_of(HALO + (2 * zz + yy) * chunk + (1 - yy) * HALO, HALO)
        return rows_all.at[i, pl.ds(at, inner), lanes(cc, wide)]

    own_edge = pc_ref.at[:, pl.ds(pl.multiple_of(y * inner, HALO), HALO), :]

    def own_inner(i):
        return pc_ref.at[i, pl.ds(pl.multiple_of((1 - y) * HALO, HALO), inner), :]

    local_edge = pltpu.make_async_copy(own_edge, edge_of(z, y, c), local_sem.at[0, taps])
    local_inner = [
        pltpu.make_async_copy(own_inner(i), inner_of(i, z, y, c), local_sem.at[1, taps + i])
        for i in range(3)
    ]

    for w in range(2):
        for t in range(taps):
            own_weight(w, t).start()
            weight_to_y(w, t, g).start()

    def edge_out(d, where):
        return remote(own_edge, edge_of(z, y, c), edge_send.at[d], edge_z.at[z], where)

    def edge_forward(zz, where):
        ref = edge_of(zz, y, c)
        return remote(ref, ref, edge_fwd.at[zz], edge_z.at[zz], where)

    def edge_to_y(zz):
        src = edge_of(zz, y, c)
        return remote(src, src, edge_ysend.at[zz], edge_y.at[zz], to_y)

    def edge_to_c(zz, yy):
        ref = edge_of(zz, yy, c)
        return remote(ref, ref, edge_csend.at[zz, yy], edge_c.at[zz, yy], to_c)

    local_edge.start()

    @pl.when(has_left)
    def _():
        edge_out(0, to_left).start()

    @pl.when(has_right)
    def _():
        edge_out(1, to_right).start()

    for copy in local_inner:
        copy.start()
    rows_all[:, :HALO, :] = jnp.zeros((3, HALO, 2 * wide), BF16)
    bottom = rows_all.shape[1] - HALO
    rows_all[:, bottom:, :] = jnp.zeros((3, HALO, 2 * wide), BF16)
    local_edge.wait()
    edge_to_y(z).start()
    edge_to_c(z, y).start()

    for w in range(2):
        for t in range(taps):
            own_weight(w, t).wait()

        @pl.when(has_left)
        def _():
            weight_z(w, z, y, 0, to_left).start()

        @pl.when(has_right)
        def _():
            weight_z(w, z, y, 1, to_right).start()

    for w in range(2):
        for t in range(taps):
            weight_from_y(
                weights, sources, wy_send, wy_recv, w, t, g, s, y, half, block, share, to_y, lanes
            ).wait_recv()

        @pl.when(has_left)
        def _():
            weight_z(w, z, 1 - y, 0, to_left).start()

        @pl.when(has_right)
        def _():
            weight_z(w, z, 1 - y, 1, to_right).start()

    for w in range(2):
        for t in range(taps):
            weight_to_y(w, t, 1 - g).start()

    def inner_to_y(i, zz):
        ref = inner_of(i, zz, y, c)
        return remote(ref, ref, py_send.at[zz, i], py_recv.at[zz, i], to_y)

    def inner_to_c(i, zz, yy):
        ref = inner_of(i, zz, yy, c)
        return remote(ref, ref, pc_send.at[zz, yy, i], pc_recv.at[zz, yy, i], to_c)

    def inner_out(i, d, where):
        return remote(own_inner(i), inner_of(i, z, y, c), own_send.at[d, i], pz_recv.at[z, i], where)

    for i in range(3):
        local_inner[i].wait()
        inner_to_y(i, z).start()
        inner_to_c(i, z, y).start()

    def order(k):
        low = jnp.minimum(z, last - z)
        near = jnp.where(low == 0, k, jnp.where(k < 2, 1 - k, k))
        return jnp.where(z * 2 < last, near, last - near)

    def edge_step(k, carry):
        zz = order(k)
        edge_forward(zz, to_y).wait_recv()

        @pl.when((zz < z) & has_right)
        def _():
            edge_forward(zz, to_right).start()

        @pl.when((zz > z) & has_left)
        def _():
            edge_forward(zz, to_left).start()

        edge_to_y(zz).start()
        edge_to_c(zz, y).start()
        return carry

    lax.fori_loop(1, last + 1, edge_step, 0)

    def edge_end(zz, carry):
        edge_arrives_y(zz).wait_recv()
        edge_to_c(zz, 1 - y).start()
        return carry

    def edge_arrives_y(zz):
        ref = edge_of(zz, 1 - y, c)
        return remote(ref, ref, edge_ysend.at[zz], edge_y.at[zz], to_y)

    lax.fori_loop(0, last + 1, edge_end, 0)
    for zz in range(last + 1):
        for yy in range(2):
            ref = edge_of(zz, yy, 1 - c)
            remote(ref, ref, edge_csend.at[zz, yy], edge_c.at[zz, yy], to_c).wait_recv()

    def send_own_rows(d, where):
        for i in range(3):
            inner_out(i, d, where).start()

    @pl.when(z == 0)
    def _():
        send_own_rows(1, to_right)

    @pl.when(z == last)
    def _():
        send_own_rows(0, to_left)

    def weight_step(k, carry):
        for sign in (-1, 1):
            zz = z + sign * k

            @pl.when((zz >= 0) & (zz <= last))
            def _():
                for w in range(2):
                    for b in range(2):
                        weight_z(w, zz, b, 0, to_y).wait_recv()

                        if sign < 0:
                            @pl.when(has_right)
                            def _():
                                weight_z(w, zz, b, 1, to_right).start()
                        else:
                            @pl.when(has_left)
                            def _():
                                weight_z(w, zz, b, 0, to_left).start()

                        weight_x(w, zz, b, g).start()

        @pl.when((z == k) & has_right)
        def _():
            send_own_rows(1, to_right)

        @pl.when((last - z == k) & has_left)
        def _():
            send_own_rows(0, to_left)

        return carry

    lax.fori_loop(1, last + 1, weight_step, 0)

    def each_other_cell(body):
        def step(k, carry):
            body(order(k))
            return carry

        lax.fori_loop(1, last + 1, step, 0)

    for w in range(2):
        for t in range(taps):
            weight_from_y(
                weights, sources, wy_send, wy_recv, w, t, 1 - g, s, y, half, block, share, to_y, lanes
            ).wait_recv()

    def wait_x(zz):
        for w in range(2):
            for b in range(2):
                weight_x(w, zz, b, 1 - g).wait_recv()

    each_other_cell(wait_x)

    step_rows = 64

    def fold(i, carry):
        at = pl.ds(pl.multiple_of(i * step_rows, HALO), step_rows)
        w = [weights[1, at, t * share : (t + 1) * share].astype(F32) for t in range(5)]
        folded[0, at, :share] = (w[0] + w[1]).astype(BF16)
        folded[0, at, share : 2 * share] = (w[2] + w[3]).astype(BF16)
        folded[0, at, 2 * share :] = weights[1, at, 4 * share :]
        folded[1, at, :share] = weights[1, at, :share]
        folded[1, at, share : 2 * share] = (w[1] + w[2]).astype(BF16)
        folded[1, at, 2 * share :] = (w[3] + w[4]).astype(BF16)
        return carry

    lax.fori_loop(0, weights.shape[1] // step_rows, fold, 0)

    contract_rows = (((0,), (0,)), ((), ()))
    contract_last = (((1,), (1,)), ((), ()))
    wide_rows = cell + 2 * HALO
    mid_rows = cell + 2 * EDGE
    window = pl.ds(pl.multiple_of((2 * block * z) // LANES * LANES, LANES), 2 * LANES)
    offset = 2 * block * z - (2 * block * z) // LANES * LANES

    enc_sum[...] = jnp.zeros_like(enc_sum)
    dec_sum[...] = jnp.zeros_like(dec_sum)

    def sums_over_cores():
        for i in range(3):
            total = part[i] + take[i].astype(F32)
            part[i] = total
            rows = pl.ds(pl.multiple_of((1 - y) * chunk, HALO), chunk)
            give_y[i] = part[i, rows, :].astype(BF16)

    give_copy = remote(give, take, give_sem.at[0], take_sem.at[0], to_c)
    give_y_copy = remote(give_y, take_y, give_sem.at[1], take_sem.at[1], to_y)

    def cell_step(k, carry):
        zz = order(k)

        @pl.when(k > 0)
        def _():
            for i in range(3):
                inner_forward(i, zz, to_y).wait_recv()

                @pl.when((zz < z) & has_right)
                def _():
                    inner_forward(i, zz, to_right).start()

                @pl.when((zz > z) & has_left)
                def _():
                    inner_forward(i, zz, to_left).start()

                inner_to_y(i, zz).start()
                inner_to_c(i, zz, y).start()

        for i in range(3):
            ref = inner_of(i, zz, 1 - y, c)
            remote(ref, ref, py_send.at[zz, i], py_recv.at[zz, i], to_y).wait_recv()
            inner_to_c(i, zz, 1 - y).start()
        for yy in range(2):
            for i in range(3):
                ref = inner_of(i, zz, yy, 1 - c)
                remote(ref, ref, pc_send.at[zz, yy, i], pc_recv.at[zz, yy, i], to_c).wait_recv()

        base = pl.multiple_of(zz * cell, HALO)
        at = pl.ds(base, wide_rows)
        z_enc[...] = jnp.dot(rows_all[0, at, :], weights[0], preferred_element_type=F32)
        z_dec[...] = jnp.dot(
            rows_all[1, at, :], folded[0], preferred_element_type=F32
        ) + jnp.dot(rows_all[2, at, :], folded[1], preferred_element_type=F32)

        piece = mid_rows // 6

        def activate(r, carry):
            start = pl.multiple_of(r * piece, EDGE)
            near = pl.ds(start, piece + 2 * EDGE)

            def enc_tap(t):
                return z_enc[near, t * share : (t + 1) * share][6 + t : 6 + t + piece]

            def dec_tap(t):
                return z_dec[near, t * share : (t + 1) * share][9 - t : 9 - t + piece]

            pre = enc_tap(0) + enc_tap(1) + enc_tap(2) + enc_tap(3) + enc_tap(4)
            grad = dec_tap(0) + dec_tap(1) + dec_tap(2)
            value, slope = gelu_and_slope(pre)
            hid[pl.ds(start, piece), :] = value
            pre_grad[pl.ds(start, piece), :] = grad * slope
            return carry

        lax.fori_loop(0, 6, activate, 0)

        @pl.when(zz == 0)
        def _():
            hid[:EDGE, :] = jnp.zeros((EDGE, share), F32)
            pre_grad[:EDGE, :] = jnp.zeros((EDGE, share), F32)

        @pl.when(zz == last)
        def _():
            hid[mid_rows - EDGE :, :] = jnp.zeros((EDGE, share), F32)
            pre_grad[mid_rows - EDGE :, :] = jnp.zeros((EDGE, share), F32)

        def shifted(r, carry):
            start = pl.multiple_of(r * LANES, HALO)
            to = pl.ds(start, LANES)
            grad = pre_grad[pl.ds(start, LANES + 2 * EDGE), :]
            value = hid[pl.ds(start, LANES + 2 * EDGE), :]
            for t in range(5):
                by = EDGE + 2 - t
                g_taps[to, t * share : (t + 1) * share] = grad[by : by + LANES].astype(BF16)
            for t in range(3):
                by = EDGE - 1 + t
                h_taps[to, t * share : (t + 1) * share] = value[by : by + LANES].astype(BF16)
            return carry

        lax.fori_loop(0, cell // LANES, shifted, 0)

        body = pl.ds(base + HALO, cell)
        enc_sum[...] += lax.dot_general(
            rows_all[0, body, window], g_taps[...], contract_rows, preferred_element_type=F32
        )
        for i in range(2):
            dec_sum[i] += lax.dot_general(
                rows_all[1 + i, body, window], h_taps[...], contract_rows,
                preferred_element_type=F32,
            )

        @pl.when(k == 0)
        def _():
            for i in range(3):
                for h in range(2):
                    cols = pl.ds(pl.multiple_of((c if h == 0 else 1 - c) * wide, LANES), wide)
                    rhs = weights[0, cols, :] if i == 0 else folded[i - 1, cols, :]
                    lhs = g_taps[...] if i == 0 else h_taps[...]
                    value = lax.dot_general(lhs, rhs, contract_last, preferred_element_type=F32)
                    if h == 0:
                        part[i] = value
                    else:
                        give[i] = value.astype(BF16)
            give_copy.start()

        @pl.when(k == 1)
        def _():
            give_copy.wait_recv()
            sums_over_cores()
            give_y_copy.start()

        return carry

    def inner_forward(i, zz, where):
        ref = inner_of(i, zz, y, c)
        return remote(ref, ref, pz_send.at[zz, i], pz_recv.at[zz, i], where)

    lax.fori_loop(0, last + 1, cell_step, 0)

    def grad_copy(w):
        return remote(
            grad_give.at[w], grad_ref.at[w, :, :, lanes(y, share)], grad_sem.at[0, w], grad_sem.at[1, w], to_y
        )

    def grads(w, who):
        at = pl.ds(pl.multiple_of(offset + who * block, HALO), block)
        if w == 0:
            return [enc_sum[at, t * share : (t + 1) * share].astype(BF16) for t in range(5)]
        e = [dec_sum[0, at, k * share : (k + 1) * share] for k in range(3)]
        o = [dec_sum[1, at, k * share : (k + 1) * share] for k in range(3)]
        both = (e[0] + o[0], e[0] + o[1], e[1] + o[1], e[1] + o[2], e[2] + o[2])
        return [v.astype(BF16) for v in both]

    for w in range(2):
        for t, value in enumerate(grads(w, 1 - y)):
            grad_give[w, t] = value
        grad_copy(w).start()
    for w in range(2):
        for t, value in enumerate(grads(w, y)):
            grad_ref[w, t, :, lanes(y, share)] = value

    give_y_copy.wait_recv()
    for i in range(3):
        own = pl.ds(pl.multiple_of(y * chunk, HALO), chunk)
        out_ref[i] = part[i, own, :] + take_y[i].astype(F32)

    give_copy.wait_send()
    give_y_copy.wait_send()
    for w in range(2):
        for t in range(taps):
            weight_to_y(w, t, g).wait_send()
            weight_to_y(w, t, 1 - g).wait_send()

    @pl.when(has_left)
    def _():
        edge_out(0, to_left).wait_send()
        for i in range(3):
            inner_out(i, 0, to_left).wait_send()
        for w in range(2):
            for b in range(2):
                weight_z(w, z, b, 0, to_left).wait_send()

    @pl.when(has_right)
    def _():
        edge_out(1, to_right).wait_send()
        for i in range(3):
            inner_out(i, 1, to_right).wait_send()
        for w in range(2):
            for b in range(2):
                weight_z(w, z, b, 1, to_right).wait_send()

    def drain(k, carry):
        zz = order(k)
        edge_to_y(zz).wait_send()
        for yy in range(2):
            edge_to_c(zz, yy).wait_send()
        for i in range(3):
            inner_to_y(i, zz).wait_send()
            for yy in range(2):
                inner_to_c(i, zz, yy).wait_send()

        @pl.when(k > 0)
        def _():
            for w in range(2):
                for b in range(2):
                    weight_x(w, zz, b, g).wait_send()

        @pl.when((zz < z) & has_right)
        def _():
            edge_forward(zz, to_right).wait_send()
            for i in range(3):
                inner_forward(i, zz, to_right).wait_send()
            for w in range(2):
                for b in range(2):
                    weight_z(w, zz, b, 1, to_right).wait_send()

        @pl.when((zz > z) & has_left)
        def _():
            edge_forward(zz, to_left).wait_send()
            for i in range(3):
                inner_forward(i, zz, to_left).wait_send()
            for w in range(2):
                for b in range(2):
                    weight_z(w, zz, b, 0, to_left).wait_send()

        return carry

    lax.fori_loop(0, last + 1, drain, 0)
    for w in range(2):
        grad_copy(w).wait_send()
    for w in range(2):
        grad_arrives = remote(
            grad_give.at[w], grad_ref.at[w, :, :, lanes(1 - y, share)],
            grad_sem.at[0, w], grad_sem.at[1, w], to_y,
        )
        grad_arrives.wait_recv()


def weight_from_y(weights, sources, send, recv, w, t, side, s, y, half, block, share, to_y, lanes):
    other = s + 1 - 2 * y
    row = pl.multiple_of(other * block + side * half, HALO)
    return pltpu.make_async_remote_copy(
        src_ref=sources[w].at[t, pl.ds(pl.multiple_of(side * half, HALO), half), lanes(1 - y, share)],
        dst_ref=weights.at[w, pl.ds(row, half), pl.ds(t * share, share)],
        send_sem=send.at[w, t, side],
        recv_sem=recv.at[w, t, side],
        device_id=to_y,
        device_id_type=pl.DeviceIdType.MESH,
    )


def pair_call(own, enc_taps, dec_taps, cells):
    _, chunk, wide = own.shape
    taps, block, both = enc_taps.shape
    share = both // 2
    cell = 2 * chunk
    vmem = pl.BlockSpec(memory_space=pltpu.VMEM)
    anywhere = pl.BlockSpec(memory_space=pl.ANY)
    dma = pltpu.SemaphoreType.DMA
    tall = cells * cell + 2 * HALO
    width = 2 * wide
    return pl.pallas_call(
        pair_kernel,
        out_shape=[
            jax.ShapeDtypeStruct((2, taps, block, both), BF16),
            jax.ShapeDtypeStruct((3, chunk, wide), F32),
        ],
        in_specs=[vmem, anywhere, anywhere],
        out_specs=[vmem, vmem],
        scratch_shapes=[
            pltpu.VMEM((3, tall, width), BF16),
            pltpu.VMEM((2, width, taps * share), BF16),
            pltpu.VMEM((2, width, 3 * share), BF16),
            pltpu.VMEM((cell + 2 * HALO, taps * share), F32),
            pltpu.VMEM((cell + 2 * HALO, 3 * share), F32),
            pltpu.VMEM((cell + 2 * EDGE, share), F32),
            pltpu.VMEM((cell + 2 * EDGE, share), F32),
            pltpu.VMEM((cell, taps * share), BF16),
            pltpu.VMEM((cell, 3 * share), BF16),
            pltpu.VMEM((2 * LANES, taps * share), F32),
            pltpu.VMEM((2, 2 * LANES, 3 * share), F32),
            pltpu.VMEM((3, cell, wide), F32),
            pltpu.VMEM((3, cell, wide), BF16),
            pltpu.VMEM((3, cell, wide), BF16),
            pltpu.VMEM((3, chunk, wide), BF16),
            pltpu.VMEM((3, chunk, wide), BF16),
            pltpu.VMEM((2, taps, block, share), BF16),
            dma((2, taps + 3)),
            dma((2, taps, 2)), dma((2, taps, 2)),
            dma((2, 2, cells, 2)), dma((2, cells, 2)), dma((2, cells, 2)), dma((2, cells, 2)),
            dma((2,)), dma((cells,)), dma((cells,)), dma((cells, 2)), dma((cells,)), dma((cells,)),
            dma((cells, 2)),
            dma((2, 3)), dma((cells, 3)), dma((cells, 3)), dma((cells, 3)), dma((cells, 3)),
            dma((cells, 2, 3)), dma((cells, 2, 3)),
            dma((2,)), dma((2,)), dma((2, 2)),
        ],
        compiler_params=pltpu.CompilerParams(
            collective_id=0, has_side_effects=True, vmem_limit_bytes=58 * 2**20
        ),
        cost_estimate=pl.CostEstimate(
            flops=2 * 11 * cells * cell * width * share + 4 * 11 * cells * cell * block * share,
            bytes_accessed=4 * taps * block * both * 2,
            transcendentals=cells * cell * share,
        ),
    )(own, enc_taps, dec_taps)


def shards(inputs, enc_weight, dec_weight, cotangent):
    parts = lax.axis_size("seq")
    cores = lax.axis_size("chan")
    rows, width = inputs.shape
    chunk = rows // 2
    block, taps, share = enc_weight.shape
    wide = cotangent.shape[1]
    fits = parts == 8 and cores == 2 and lax.axis_size("groups") == 2 and taps == 5
    fits = fits and block == 96 and share % (2 * LANES) == 0 and wide % LANES == 0 and chunk == 256
    if not fits:
        return wide_shards(inputs, enc_weight, dec_weight, cotangent)
    core = lax.axis_index("chan")

    skip = lax.dynamic_slice_in_dim(inputs, core * wide, wide, 1)
    pooled = (skip.astype(F32).reshape(chunk, 2, wide).sum(axis=1) * 0.5).astype(BF16)
    cot = cotangent.reshape(chunk, 2, wide)
    own = jnp.stack([pooled, cot[:, 0], cot[:, 1]])
    grads, back = pair_call(own, enc_weight.transpose(1, 0, 2), dec_weight.transpose(1, 0, 2), parts // 2)
    decoded = jnp.stack([back[1], back[2]], axis=1).reshape(rows, wide)
    mixed_out = (skip.astype(F32) + decoded).astype(BF16)
    input_grad = (cotangent.astype(F32) + 0.5 * jnp.repeat(back[0], 2, axis=0)).astype(BF16)
    return mixed_out, input_grad, grads[0].transpose(1, 0, 2), grads[1].transpose(1, 0, 2)


def solution(mesh):
    return jax.shard_map(
        shards,
        mesh=mesh,
        in_specs=(
            P(("groups", "seq"), None),
            P("seq", None, "chan"),
            P("seq", None, "chan"),
            P(("groups", "seq"), "chan"),
        ),
        out_specs=(
            P(("groups", "seq"), "chan"),
            P(("groups", "seq"), "chan"),
            P(("groups", "seq"), None, "chan"),
            P(("groups", "seq"), None, "chan"),
        ),
        check_vma=False,
    )
```

```python
import functools
import math

import jax
import jax.numpy as jnp
from jax import lax
from jax.experimental import pallas as pl
from jax.experimental.pallas import tpu as pltpu
from jax.sharding import PartitionSpec as P

BF16 = jnp.bfloat16
F32 = jnp.float32


def shift(array, by):
    length = array.shape[0]
    if by == 0:
        return array
    pad = jnp.zeros((abs(by),) + array.shape[1:], array.dtype)
    if by > 0:
        return jnp.concatenate([array[by:], pad], axis=0)
    return jnp.concatenate([pad, array[: length + by]], axis=0)


def to_columns(array, parts):
    rows, cols = array.shape
    blocks = array.reshape(rows, parts, cols // parts).transpose(1, 0, 2)
    return lax.all_to_all(blocks, "seq", 0, 0, tiled=True)


def to_rows(blocks):
    parts, rows, cols = blocks.shape
    got = lax.all_to_all(blocks, "seq", 0, 0, tiled=True)
    return got.transpose(1, 0, 2).reshape(rows, parts * cols)


PIECES = 2


def ring_place(index, n):
    if n != 8:
        return index
    y = lax.rem(index, 2)
    z = index // 2
    return z + y * (n - 1 - 2 * z)


def ring_index(place, n):
    place = lax.rem(place + 2 * n, n)
    if n != 8:
        return place
    back = place // (n // 2)
    return 2 * place + back * (2 * n - 1 - 4 * place)


def gelu_and_slope(v):
    scale = math.sqrt(2.0 / math.pi)
    square = v * v
    th = jnp.tanh(scale * (v + 0.044715 * square * v))
    up = 0.5 * (1.0 + th)
    slope = up + 0.5 * v * (1.0 - th * th) * (scale * (1.0 + 3.0 * 0.044715 * square))
    return v * up, slope


def ring_kernel(
    n, x_ref, y_ref, enc_ref, dec_ref, out_ref, slots, term, mine,
    rs_send, rs_recv, ag_send, ag_recv, local_sem,
):
    me = lax.axis_index("seq")
    place = ring_place(me, n)
    nexts = (ring_index(place + 1, n), ring_index(place - 1, n))
    half = x_ref.shape[1]
    share = enc_ref.shape[1]
    side = half // 2
    piece = side // PIECES

    barrier = pltpu.get_barrier_semaphore()
    for other in nexts:
        pl.semaphore_signal(
            barrier, inc=1, device_id={"seq": other}, device_id_type=pl.DeviceIdType.MESH
        )
    pl.semaphore_wait(barrier, 2)

    def signed(d, steps):
        return place - steps if d == 0 else place + steps

    def own_term(d, steps):
        chunk = ring_index(signed(d, steps), n)
        at = pl.ds(d * side, side)
        a = jnp.dot(x_ref[chunk, at, :], enc_ref[...], preferred_element_type=jnp.float32)
        b = jnp.dot(y_ref[chunk, at, :], dec_ref[...], preferred_element_type=jnp.float32)
        return a, b

    def rs_copy(d, s, q):
        at = pl.ds(q * piece, piece)
        return pltpu.make_async_remote_copy(
            src_ref=slots.at[d, s, at],
            dst_ref=slots.at[d, s + 1, at],
            send_sem=rs_send.at[d, s, q],
            recv_sem=rs_recv.at[d, s, q],
            device_id={"seq": nexts[d]},
            device_id_type=pl.DeviceIdType.MESH,
        )

    def ag_copy(d, s, q, first):
        at = pl.ds(d * side + q * piece, piece)
        owner = ring_index(signed(d, s), n)
        return pltpu.make_async_remote_copy(
            src_ref=mine.at[at] if first else out_ref.at[owner, at],
            dst_ref=out_ref.at[owner, at],
            send_sem=ag_send.at[d, s, q],
            recv_sem=ag_recv.at[d, s, q],
            device_id={"seq": nexts[d]},
            device_id_type=pl.DeviceIdType.MESH,
        )

    for d in range(2):
        a, b = own_term(d, 1)
        slots[d, 0, :, :share] = a.astype(BF16)
        slots[d, 0, :, share:] = b.astype(BF16)
        for q in range(PIECES):
            rs_copy(d, 0, q).start()

    def fill(s):
        for d in range(2):
            a, b = own_term(d, s + 2)
            term[d, :, :share] = a
            term[d, :, share:] = b

    def rs_step(s, carry):
        fill(s)
        for q in range(PIECES):
            at = pl.ds(q * piece, piece)
            for d in range(2):
                rs_copy(d, s, q).wait_recv()
                total = slots[d, s + 1, at, :].astype(F32) + term[d, at, :]
                slots[d, s + 1, at, :] = total.astype(BF16)
                rs_copy(d, s + 1, q).start()
        return carry

    lax.fori_loop(0, n - 2, rs_step, 0)
    fill(n - 2)
    for q in range(PIECES):
        at = pl.ds(q * piece, piece)
        for d in range(2):
            rs_copy(d, n - 2, q).wait_recv()
            rows = pl.ds(d * side + q * piece, piece)
            pre = slots[d, n - 1, at, :share].astype(F32) + term[d, at, :share]
            grad = slots[d, n - 1, at, share:].astype(F32) + term[d, at, share:]
            value, slope = gelu_and_slope(pre)
            mine[rows, :share] = value.astype(BF16)
            mine[rows, share:] = (grad * slope).astype(BF16)
            ag_copy(d, 0, q, True).start()
    local = pltpu.make_async_copy(mine, out_ref.at[me], local_sem)
    local.start()

    def ag_step(s, carry):
        for q in range(PIECES):
            for d in range(2):
                incoming(d, s, q).wait_recv()
                ag_copy(d, s + 1, q, False).start()
        return carry

    def incoming(d, s, q):
        at = pl.ds(d * side + q * piece, piece)
        owner = ring_index(signed(d, s + 1), n)
        return pltpu.make_async_remote_copy(
            src_ref=mine.at[at],
            dst_ref=out_ref.at[owner, at],
            send_sem=ag_send.at[d, s, q],
            recv_sem=ag_recv.at[d, s, q],
            device_id={"seq": nexts[d]},
            device_id_type=pl.DeviceIdType.MESH,
        )

    lax.fori_loop(0, n - 2, ag_step, 0)
    for q in range(PIECES):
        for d in range(2):
            incoming(d, n - 2, q).wait_recv()

    def drain(s, carry):
        for q in range(PIECES):
            for d in range(2):
                rs_copy(d, s, q).wait_send()
                ag_copy(d, s, q, True).wait_send()
        return carry

    lax.fori_loop(0, n - 1, drain, 0)
    local.wait()


def ring(pool_taps, cot_taps, enc_mat, dec_mat, n):
    half = pool_taps.shape[1]
    share = enc_mat.shape[1]
    depth = enc_mat.shape[0]
    vmem = pl.BlockSpec(memory_space=pltpu.VMEM)
    steps = (2, n - 1, PIECES)
    return pl.pallas_call(
        functools.partial(ring_kernel, n),
        out_shape=jax.ShapeDtypeStruct((n, half, 2 * share), BF16),
        in_specs=[vmem] * 4,
        out_specs=pl.BlockSpec(memory_space=pl.ANY),
        scratch_shapes=[
            pltpu.VMEM((2, n, half // 2, 2 * share), BF16),
            pltpu.VMEM((2, half // 2, 2 * share), F32),
            pltpu.VMEM((half, 2 * share), BF16),
            pltpu.SemaphoreType.DMA(steps),
            pltpu.SemaphoreType.DMA(steps),
            pltpu.SemaphoreType.DMA(steps),
            pltpu.SemaphoreType.DMA(steps),
            pltpu.SemaphoreType.DMA,
        ],
        compiler_params=pltpu.CompilerParams(
            collective_id=0, has_side_effects=True, vmem_limit_bytes=48 * 2**20
        ),
        cost_estimate=pl.CostEstimate(
            flops=4 * n * half * depth * share,
            bytes_accessed=4 * n * half * share * 2,
            transcendentals=half * share,
        ),
    )(pool_taps, cot_taps, enc_mat, dec_mat)


def wide_shards(inputs, enc_weight, dec_weight, cotangent):
    parts = lax.axis_size("seq")
    rows, width = inputs.shape
    half = rows // 2
    total = half * parts
    block, taps, share = enc_weight.shape
    half_width = cotangent.shape[1]

    pooled = (inputs.astype(F32).reshape(half, 2, width).sum(axis=1) * 0.5).astype(BF16)
    cot_full = lax.all_gather(cotangent, "chan", axis=1, tiled=True)
    core = lax.axis_index("chan")
    cores = lax.axis_size("chan")
    few = half // cores
    leaving = jnp.concatenate(
        [
            lax.dynamic_slice_in_dim(pooled, core * few, few, 0),
            lax.dynamic_slice_in_dim(cot_full, core * 2 * few, 2 * few, 0),
        ],
        axis=0,
    )
    columns = to_columns(leaving, parts).reshape(parts, 1, 3 * few, block)
    columns = lax.all_gather(columns, "chan", axis=1, tiled=True)
    pool_col = columns[:, :, :few].reshape(total, block)
    cot_col = columns[:, :, few:].reshape(total, 2, block).astype(F32)
    even = cot_col[:, 0]
    odd = cot_col[:, 1]
    pair = (even + odd).astype(BF16)
    cross = (odd + shift(even, 1)).astype(BF16)
    before = jnp.concatenate([even[:1].astype(BF16), cross[:-1]], axis=0)
    pool_taps = jnp.concatenate([shift(pool_col, t - 2) for t in range(taps)], axis=1)
    cot_taps = jnp.concatenate([shift(pair, 1), cross, pair, before, shift(pair, -1)], axis=1)
    enc_mat = enc_weight.transpose(1, 0, 2).reshape(taps * block, share)
    dec_mat = dec_weight.transpose(1, 0, 2).reshape(taps * block, share)

    joint = ring(
        pool_taps.reshape(parts, half, taps * block),
        cot_taps.reshape(parts, half, taps * block),
        enc_mat,
        dec_mat,
        parts,
    ).reshape(total, 2 * share)
    hidden_all = joint[:, :share]
    grad_all = joint[:, share:]

    contract_rows = (((0,), (0,)), ((), ()))
    contract_last = (((1,), (1,)), ((), ()))
    dec_grad = lax.dot_general(cot_taps, hidden_all, contract_rows, preferred_element_type=F32)
    enc_grad = lax.dot_general(pool_taps, grad_all, contract_rows, preferred_element_type=F32)
    dec_grad = dec_grad.astype(BF16).reshape(taps, block, share).transpose(1, 0, 2)
    enc_grad = enc_grad.astype(BF16).reshape(taps, block, share).transpose(1, 0, 2)

    dec_out = lax.dot_general(hidden_all, dec_mat, contract_last, preferred_element_type=F32)
    p0, p1, p2, p3, p4 = [dec_out[:, t * block : (t + 1) * block] for t in range(taps)]
    after4 = shift(p4, 1)
    before0 = shift(p0, -1)
    dec_even = before0 + shift(p1, -1) + p2 + p3 + after4
    dec_odd = before0 + p1 + p2 + shift(p3, 1) + after4
    decoded = jnp.stack([dec_even, dec_odd], axis=1).astype(BF16).reshape(parts, rows, block)
    enc_out = lax.dot_general(grad_all, enc_mat, contract_last, preferred_element_type=F32)
    pool_grad = sum(shift(enc_out[:, t * block : (t + 1) * block], 2 - t) for t in range(taps))
    pool_grad = pool_grad.astype(BF16).reshape(parts, half, block)
    mine = jnp.concatenate([decoded, pool_grad], axis=1)
    mine = lax.psum_scatter(mine, "chan", scatter_dimension=1, tiled=True)
    mine = lax.all_gather(to_rows(mine), "chan", axis=0, tiled=True)
    col_start = core * half_width
    mine = lax.dynamic_slice_in_dim(mine, col_start, half_width, 1).astype(F32)

    skip = lax.dynamic_slice_in_dim(inputs, col_start, half_width, 1)
    mixed_out = (skip.astype(F32) + mine[:rows]).astype(BF16)
    input_grad = (cotangent.astype(F32) + 0.5 * jnp.repeat(mine[rows:], 2, axis=0)).astype(BF16)
    return mixed_out, input_grad, enc_grad, dec_grad


LANES = 128
HALO = 16
EDGE = 8


def pair_kernel(
    pc_ref, enc_ref, dec_ref, grad_ref, out_ref,
    rows_all, weights, folded, z_enc, z_dec, hid, pre_grad, g_taps, h_taps,
    enc_sum, dec_sum, part, give, take, give_y, take_y, grad_give,
    local_sem, wy_send, wy_recv, wz_send, wz_recv, wx_send, wx_recv,
    edge_send, edge_z, edge_y, edge_c, edge_fwd, edge_ysend, edge_csend,
    own_send, pz_send, pz_recv, py_send, py_recv, pc_send, pc_recv,
    give_sem, take_sem, grad_sem,
):
    g = lax.axis_index("groups")
    s = lax.axis_index("seq")
    c = lax.axis_index("chan")
    z, y = s // 2, lax.rem(s, 2)
    last = lax.axis_size("seq") // 2 - 1
    chunk, wide = pc_ref.shape[1], pc_ref.shape[2]
    cell = 2 * chunk
    taps, block = enc_ref.shape[0], enc_ref.shape[1]
    share = enc_ref.shape[2] // 2
    half = block // 2
    inner = chunk - HALO
    ids = pl.DeviceIdType.MESH
    to_y, to_x, to_c = {"seq": s + 1 - 2 * y}, {"groups": 1 - g}, {"chan": 1 - c}
    to_left, to_right = {"seq": s - 2}, {"seq": s + 2}
    has_left, has_right = z > 0, z < last

    barrier = pltpu.get_barrier_semaphore()
    for where in (to_y, to_x, to_c):
        pl.semaphore_signal(barrier, inc=1, device_id=where, device_id_type=ids)

    @pl.when(has_left)
    def _():
        pl.semaphore_signal(barrier, inc=1, device_id=to_left, device_id_type=ids)

    @pl.when(has_right)
    def _():
        pl.semaphore_signal(barrier, inc=1, device_id=to_right, device_id_type=ids)

    inside = jnp.where(has_left, 1, 0) + jnp.where(has_right, 1, 0)
    pl.semaphore_wait(barrier, 3 + inside)

    def remote(src, dst, send, recv, where):
        return pltpu.make_async_remote_copy(
            src_ref=src, dst_ref=dst, send_sem=send, recv_sem=recv,
            device_id=where, device_id_type=ids,
        )

    def lanes(index, width):
        return pl.ds(pl.multiple_of(index * width, LANES), width)

    sources = (enc_ref, dec_ref)

    def own_weight(w, t):
        return pltpu.make_async_copy(
            sources[w].at[t, :, lanes(y, share)],
            weights.at[w, pl.ds(pl.multiple_of(s * block, HALO), block), pl.ds(t * share, share)],
            local_sem.at[w, t],
        )

    def weight_to_y(w, t, side):
        at = pl.ds(pl.multiple_of(side * half, HALO), half)
        row = pl.multiple_of(s * block + side * half, HALO)
        return remote(
            sources[w].at[t, at, lanes(1 - y, share)],
            weights.at[w, pl.ds(row, half), pl.ds(t * share, share)],
            wy_send.at[w, t, side], wy_recv.at[w, t, side], to_y,
        )

    def slab(w, b, side):
        return weights.at[w, pl.ds(pl.multiple_of(b * block + side * half, HALO), half), :]

    def weight_z(w, zz, b, d, where):
        ref = slab(w, 2 * zz + b, g)
        return remote(ref, ref, wz_send.at[d, w, zz, b], wz_recv.at[w, zz, b], where)

    def weight_x(w, zz, b, side):
        ref = slab(w, 2 * zz + b, side)
        return remote(ref, ref, wx_send.at[w, zz, b], wx_recv.at[w, zz, b], to_x)

    def edge_of(zz, yy, cc):
        at = pl.multiple_of(HALO + (2 * zz + yy) * chunk + yy * inner, HALO)
        return rows_all.at[:, pl.ds(at, HALO), lanes(cc, wide)]

    def inner_of(i, zz, yy, cc):
        at = pl.multiple_of(HALO + (2 * zz + yy) * chunk + (1 - yy) * HALO, HALO)
        return rows_all.at[i, pl.ds(at, inner), lanes(cc, wide)]

    own_edge = pc_ref.at[:, pl.ds(pl.multiple_of(y * inner, HALO), HALO), :]

    def own_inner(i):
        return pc_ref.at[i, pl.ds(pl.multiple_of((1 - y) * HALO, HALO), inner), :]

    local_edge = pltpu.make_async_copy(own_edge, edge_of(z, y, c), local_sem.at[0, taps])
    local_inner = [
        pltpu.make_async_copy(own_inner(i), inner_of(i, z, y, c), local_sem.at[1, taps + i])
        for i in range(3)
    ]

    for w in range(2):
        for t in range(taps):
            own_weight(w, t).start()
            weight_to_y(w, t, g).start()

    def edge_out(d, where):
        return remote(own_edge, edge_of(z, y, c), edge_send.at[d], edge_z.at[z], where)

    def edge_forward(zz, where):
        ref = edge_of(zz, y, c)
        return remote(ref, ref, edge_fwd.at[zz], edge_z.at[zz], where)

    def edge_to_y(zz):
        src = edge_of(zz, y, c)
        return remote(src, src, edge_ysend.at[zz], edge_y.at[zz], to_y)

    def edge_to_c(zz, yy):
        ref = edge_of(zz, yy, c)
        return remote(ref, ref, edge_csend.at[zz, yy], edge_c.at[zz, yy], to_c)

    local_edge.start()

    @pl.when(has_left)
    def _():
        edge_out(0, to_left).start()

    @pl.when(has_right)
    def _():
        edge_out(1, to_right).start()

    for copy in local_inner:
        copy.start()
    rows_all[:, :HALO, :] = jnp.zeros((3, HALO, 2 * wide), BF16)
    bottom = rows_all.shape[1] - HALO
    rows_all[:, bottom:, :] = jnp.zeros((3, HALO, 2 * wide), BF16)
    local_edge.wait()
    edge_to_y(z).start()
    edge_to_c(z, y).start()

    for w in range(2):
        for t in range(taps):
            own_weight(w, t).wait()

        @pl.when(has_left)
        def _():
            weight_z(w, z, y, 0, to_left).start()

        @pl.when(has_right)
        def _():
            weight_z(w, z, y, 1, to_right).start()

    for w in range(2):
        for t in range(taps):
            weight_from_y(
                weights, sources, wy_send, wy_recv, w, t, g, s, y, half, block, share, to_y, lanes
            ).wait_recv()

        @pl.when(has_left)
        def _():
            weight_z(w, z, 1 - y, 0, to_left).start()

        @pl.when(has_right)
        def _():
            weight_z(w, z, 1 - y, 1, to_right).start()

    for w in range(2):
        for t in range(taps):
            weight_to_y(w, t, 1 - g).start()

    def inner_to_y(i, zz):
        ref = inner_of(i, zz, y, c)
        return remote(ref, ref, py_send.at[zz, i], py_recv.at[zz, i], to_y)

    def inner_to_c(i, zz, yy):
        ref = inner_of(i, zz, yy, c)
        return remote(ref, ref, pc_send.at[zz, yy, i], pc_recv.at[zz, yy, i], to_c)

    def inner_out(i, d, where):
        return remote(own_inner(i), inner_of(i, z, y, c), own_send.at[d, i], pz_recv.at[z, i], where)

    for i in range(3):
        local_inner[i].wait()
        inner_to_y(i, z).start()
        inner_to_c(i, z, y).start()

    def order(k):
        low = jnp.minimum(z, last - z)
        near = jnp.where(low == 0, k, jnp.where(k < 2, 1 - k, k))
        return jnp.where(z * 2 < last, near, last - near)

    def edge_arrives_y(zz):
        ref = edge_of(zz, 1 - y, c)
        return remote(ref, ref, edge_ysend.at[zz], edge_y.at[zz], to_y)

    def send_own_rows(d, where):
        for i in range(3):
            inner_out(i, d, where).start()

    @pl.when(z == 0)
    def _():
        send_own_rows(1, to_right)

    @pl.when(z == last)
    def _():
        send_own_rows(0, to_left)

    def weight_step(k, carry):
        for sign in (-1, 1):
            zz = z + sign * k

            @pl.when((zz >= 0) & (zz <= last))
            def _():
                for w in range(2):
                    for b in range(2):
                        weight_z(w, zz, b, 0, to_y).wait_recv()

                        if sign < 0:
                            @pl.when(has_right)
                            def _():
                                weight_z(w, zz, b, 1, to_right).start()
                        else:
                            @pl.when(has_left)
                            def _():
                                weight_z(w, zz, b, 0, to_left).start()

                        weight_x(w, zz, b, g).start()

                edge_forward(zz, to_y).wait_recv()
                if sign < 0:
                    @pl.when(has_right)
                    def _():
                        edge_forward(zz, to_right).start()
                else:
                    @pl.when(has_left)
                    def _():
                        edge_forward(zz, to_left).start()

                edge_to_y(zz).start()
                edge_to_c(zz, y).start()

        @pl.when((z == k) & has_right)
        def _():
            send_own_rows(1, to_right)

        @pl.when((last - z == k) & has_left)
        def _():
            send_own_rows(0, to_left)

        return carry

    lax.fori_loop(1, last + 1, weight_step, 0)

    def inner_forward(i, zz, where):
        ref = inner_of(i, zz, y, c)
        return remote(ref, ref, pz_send.at[zz, i], pz_recv.at[zz, i], where)

    def receive(k):
        zz = order(k)
        for i in range(3):
            inner_forward(i, zz, to_y).wait_recv()

            @pl.when((zz < z) & has_right)
            def _():
                inner_forward(i, zz, to_right).start()

            @pl.when((zz > z) & has_left)
            def _():
                inner_forward(i, zz, to_left).start()

            inner_to_y(i, zz).start()
            inner_to_c(i, zz, y).start()

    lead = 1 + jnp.where(has_left & has_right, 1, 0)

    def receive_step(k, carry):
        receive(k)
        return carry

    lax.fori_loop(1, 1 + lead, receive_step, 0)

    def edge_end(zz, carry):
        edge_arrives_y(zz).wait_recv()
        edge_to_c(zz, 1 - y).start()
        return carry

    lax.fori_loop(0, last + 1, edge_end, 0)
    for zz in range(last + 1):
        for yy in range(2):
            ref = edge_of(zz, yy, 1 - c)
            remote(ref, ref, edge_csend.at[zz, yy], edge_c.at[zz, yy], to_c).wait_recv()

    def each_other_cell(body):
        def step(k, carry):
            body(order(k))
            return carry

        lax.fori_loop(1, last + 1, step, 0)

    for w in range(2):
        for t in range(taps):
            weight_from_y(
                weights, sources, wy_send, wy_recv, w, t, 1 - g, s, y, half, block, share, to_y, lanes
            ).wait_recv()

    def wait_x(zz):
        for w in range(2):
            for b in range(2):
                weight_x(w, zz, b, 1 - g).wait_recv()

    each_other_cell(wait_x)

    step_rows = 64

    def fold(i, carry):
        at = pl.ds(pl.multiple_of(i * step_rows, HALO), step_rows)
        w = [weights[1, at, t * share : (t + 1) * share].astype(F32) for t in range(5)]
        folded[0, at, :share] = (w[0] + w[1]).astype(BF16)
        folded[0, at, share : 2 * share] = (w[2] + w[3]).astype(BF16)
        folded[0, at, 2 * share :] = weights[1, at, 4 * share :]
        folded[1, at, :share] = weights[1, at, :share]
        folded[1, at, share : 2 * share] = (w[1] + w[2]).astype(BF16)
        folded[1, at, 2 * share :] = (w[3] + w[4]).astype(BF16)
        return carry

    lax.fori_loop(0, weights.shape[1] // step_rows, fold, 0)

    contract_rows = (((0,), (0,)), ((), ()))
    contract_last = (((1,), (1,)), ((), ()))
    wide_rows = cell + 2 * HALO
    mid_rows = cell + 2 * EDGE
    window = pl.ds(pl.multiple_of((2 * block * z) // LANES * LANES, LANES), 2 * LANES)
    offset = 2 * block * z - (2 * block * z) // LANES * LANES

    enc_sum[...] = jnp.zeros_like(enc_sum)
    dec_sum[...] = jnp.zeros_like(dec_sum)

    def sums_over_cores():
        for i in range(3):
            total = part[i] + take[i].astype(F32)
            part[i] = total
            rows = pl.ds(pl.multiple_of((1 - y) * chunk, HALO), chunk)
            give_y[i] = part[i, rows, :].astype(BF16)

    give_copy = remote(give, take, give_sem.at[0], take_sem.at[0], to_c)
    give_y_copy = remote(give_y, take_y, give_sem.at[1], take_sem.at[1], to_y)

    def cell_step(k, carry):
        zz = order(k)

        @pl.when((k > 0) & (k + lead <= last))
        def _():
            receive(k + lead)

        for i in range(3):
            ref = inner_of(i, zz, 1 - y, c)
            remote(ref, ref, py_send.at[zz, i], py_recv.at[zz, i], to_y).wait_recv()
            inner_to_c(i, zz, 1 - y).start()
        for yy in range(2):
            for i in range(3):
                ref = inner_of(i, zz, yy, 1 - c)
                remote(ref, ref, pc_send.at[zz, yy, i], pc_recv.at[zz, yy, i], to_c).wait_recv()

        base = pl.multiple_of(zz * cell, HALO)
        at = pl.ds(base, wide_rows)
        z_enc[...] = jnp.dot(rows_all[0, at, :], weights[0], preferred_element_type=F32)
        z_dec[...] = jnp.dot(
            rows_all[1, at, :], folded[0], preferred_element_type=F32
        ) + jnp.dot(rows_all[2, at, :], folded[1], preferred_element_type=F32)

        piece = mid_rows // 6

        def activate(r, carry):
            start = pl.multiple_of(r * piece, EDGE)
            near = pl.ds(start, piece + 2 * EDGE)

            def enc_tap(t):
                return z_enc[near, t * share : (t + 1) * share][6 + t : 6 + t + piece]

            def dec_tap(t):
                return z_dec[near, t * share : (t + 1) * share][9 - t : 9 - t + piece]

            pre = enc_tap(0) + enc_tap(1) + enc_tap(2) + enc_tap(3) + enc_tap(4)
            grad = dec_tap(0) + dec_tap(1) + dec_tap(2)
            value, slope = gelu_and_slope(pre)
            hid[pl.ds(start, piece), :] = value
            pre_grad[pl.ds(start, piece), :] = grad * slope
            return carry

        lax.fori_loop(0, 6, activate, 0)

        @pl.when(zz == 0)
        def _():
            hid[:EDGE, :] = jnp.zeros((EDGE, share), F32)
            pre_grad[:EDGE, :] = jnp.zeros((EDGE, share), F32)

        @pl.when(zz == last)
        def _():
            hid[mid_rows - EDGE :, :] = jnp.zeros((EDGE, share), F32)
            pre_grad[mid_rows - EDGE :, :] = jnp.zeros((EDGE, share), F32)

        def shifted(r, carry):
            start = pl.multiple_of(r * LANES, HALO)
            to = pl.ds(start, LANES)
            grad = pre_grad[pl.ds(start, LANES + 2 * EDGE), :]
            value = hid[pl.ds(start, LANES + 2 * EDGE), :]
            for t in range(5):
                by = EDGE + 2 - t
                g_taps[to, t * share : (t + 1) * share] = grad[by : by + LANES].astype(BF16)
            for t in range(3):
                by = EDGE - 1 + t
                h_taps[to, t * share : (t + 1) * share] = value[by : by + LANES].astype(BF16)
            return carry

        lax.fori_loop(0, cell // LANES, shifted, 0)

        body = pl.ds(base + HALO, cell)
        enc_sum[...] += lax.dot_general(
            rows_all[0, body, window], g_taps[...], contract_rows, preferred_element_type=F32
        )
        for i in range(2):
            dec_sum[i] += lax.dot_general(
                rows_all[1 + i, body, window], h_taps[...], contract_rows,
                preferred_element_type=F32,
            )

        @pl.when(k == 0)
        def _():
            for i in range(3):
                for h in range(2):
                    cols = pl.ds(pl.multiple_of((c if h == 0 else 1 - c) * wide, LANES), wide)
                    rhs = weights[0, cols, :] if i == 0 else folded[i - 1, cols, :]
                    lhs = g_taps[...] if i == 0 else h_taps[...]
                    value = lax.dot_general(lhs, rhs, contract_last, preferred_element_type=F32)
                    if h == 0:
                        part[i] = value
                    else:
                        give[i] = value.astype(BF16)
            give_copy.start()

        @pl.when(k == last - 1)
        def _():
            give_copy.wait_recv()
            sums_over_cores()
            give_y_copy.start()

        return carry

    lax.fori_loop(0, last + 1, cell_step, 0)

    def grad_copy(w):
        return remote(
            grad_give.at[w], grad_ref.at[w, :, :, lanes(y, share)], grad_sem.at[0, w], grad_sem.at[1, w], to_y
        )

    def grads(w, who):
        at = pl.ds(pl.multiple_of(offset + who * block, HALO), block)
        if w == 0:
            return [enc_sum[at, t * share : (t + 1) * share].astype(BF16) for t in range(5)]
        e = [dec_sum[0, at, k * share : (k + 1) * share] for k in range(3)]
        o = [dec_sum[1, at, k * share : (k + 1) * share] for k in range(3)]
        both = (e[0] + o[0], e[0] + o[1], e[1] + o[1], e[1] + o[2], e[2] + o[2])
        return [v.astype(BF16) for v in both]

    for w in range(2):
        for t, value in enumerate(grads(w, 1 - y)):
            grad_give[w, t] = value
        grad_copy(w).start()
    for w in range(2):
        for t, value in enumerate(grads(w, y)):
            grad_ref[w, t, :, lanes(y, share)] = value

    give_y_copy.wait_recv()
    for i in range(3):
        own = pl.ds(pl.multiple_of(y * chunk, HALO), chunk)
        out_ref[i] = part[i, own, :] + take_y[i].astype(F32)

    give_copy.wait_send()
    give_y_copy.wait_send()
    for w in range(2):
        for t in range(taps):
            weight_to_y(w, t, g).wait_send()
            weight_to_y(w, t, 1 - g).wait_send()

    @pl.when(has_left)
    def _():
        edge_out(0, to_left).wait_send()
        for i in range(3):
            inner_out(i, 0, to_left).wait_send()
        for w in range(2):
            for b in range(2):
                weight_z(w, z, b, 0, to_left).wait_send()

    @pl.when(has_right)
    def _():
        edge_out(1, to_right).wait_send()
        for i in range(3):
            inner_out(i, 1, to_right).wait_send()
        for w in range(2):
            for b in range(2):
                weight_z(w, z, b, 1, to_right).wait_send()

    def drain(k, carry):
        zz = order(k)
        edge_to_y(zz).wait_send()
        for yy in range(2):
            edge_to_c(zz, yy).wait_send()
        for i in range(3):
            inner_to_y(i, zz).wait_send()
            for yy in range(2):
                inner_to_c(i, zz, yy).wait_send()

        @pl.when(k > 0)
        def _():
            for w in range(2):
                for b in range(2):
                    weight_x(w, zz, b, g).wait_send()

        @pl.when((zz < z) & has_right)
        def _():
            edge_forward(zz, to_right).wait_send()
            for i in range(3):
                inner_forward(i, zz, to_right).wait_send()
            for w in range(2):
                for b in range(2):
                    weight_z(w, zz, b, 1, to_right).wait_send()

        @pl.when((zz > z) & has_left)
        def _():
            edge_forward(zz, to_left).wait_send()
            for i in range(3):
                inner_forward(i, zz, to_left).wait_send()
            for w in range(2):
                for b in range(2):
                    weight_z(w, zz, b, 0, to_left).wait_send()

        return carry

    lax.fori_loop(0, last + 1, drain, 0)
    for w in range(2):
        grad_copy(w).wait_send()
    for w in range(2):
        grad_arrives = remote(
            grad_give.at[w], grad_ref.at[w, :, :, lanes(1 - y, share)],
            grad_sem.at[0, w], grad_sem.at[1, w], to_y,
        )
        grad_arrives.wait_recv()


def weight_from_y(weights, sources, send, recv, w, t, side, s, y, half, block, share, to_y, lanes):
    other = s + 1 - 2 * y
    row = pl.multiple_of(other * block + side * half, HALO)
    return pltpu.make_async_remote_copy(
        src_ref=sources[w].at[t, pl.ds(pl.multiple_of(side * half, HALO), half), lanes(1 - y, share)],
        dst_ref=weights.at[w, pl.ds(row, half), pl.ds(t * share, share)],
        send_sem=send.at[w, t, side],
        recv_sem=recv.at[w, t, side],
        device_id=to_y,
        device_id_type=pl.DeviceIdType.MESH,
    )


def pair_call(own, enc_taps, dec_taps, cells):
    _, chunk, wide = own.shape
    taps, block, both = enc_taps.shape
    share = both // 2
    cell = 2 * chunk
    vmem = pl.BlockSpec(memory_space=pltpu.VMEM)
    anywhere = pl.BlockSpec(memory_space=pl.ANY)
    dma = pltpu.SemaphoreType.DMA
    tall = cells * cell + 2 * HALO
    width = 2 * wide
    return pl.pallas_call(
        pair_kernel,
        out_shape=[
            jax.ShapeDtypeStruct((2, taps, block, both), BF16),
            jax.ShapeDtypeStruct((3, chunk, wide), F32),
        ],
        in_specs=[vmem, anywhere, anywhere],
        out_specs=[vmem, vmem],
        scratch_shapes=[
            pltpu.VMEM((3, tall, width), BF16),
            pltpu.VMEM((2, width, taps * share), BF16),
            pltpu.VMEM((2, width, 3 * share), BF16),
            pltpu.VMEM((cell + 2 * HALO, taps * share), F32),
            pltpu.VMEM((cell + 2 * HALO, 3 * share), F32),
            pltpu.VMEM((cell + 2 * EDGE, share), F32),
            pltpu.VMEM((cell + 2 * EDGE, share), F32),
            pltpu.VMEM((cell, taps * share), BF16),
            pltpu.VMEM((cell, 3 * share), BF16),
            pltpu.VMEM((2 * LANES, taps * share), F32),
            pltpu.VMEM((2, 2 * LANES, 3 * share), F32),
            pltpu.VMEM((3, cell, wide), F32),
            pltpu.VMEM((3, cell, wide), BF16),
            pltpu.VMEM((3, cell, wide), BF16),
            pltpu.VMEM((3, chunk, wide), BF16),
            pltpu.VMEM((3, chunk, wide), BF16),
            pltpu.VMEM((2, taps, block, share), BF16),
            dma((2, taps + 3)),
            dma((2, taps, 2)), dma((2, taps, 2)),
            dma((2, 2, cells, 2)), dma((2, cells, 2)), dma((2, cells, 2)), dma((2, cells, 2)),
            dma((2,)), dma((cells,)), dma((cells,)), dma((cells, 2)), dma((cells,)), dma((cells,)),
            dma((cells, 2)),
            dma((2, 3)), dma((cells, 3)), dma((cells, 3)), dma((cells, 3)), dma((cells, 3)),
            dma((cells, 2, 3)), dma((cells, 2, 3)),
            dma((2,)), dma((2,)), dma((2, 2)),
        ],
        compiler_params=pltpu.CompilerParams(
            collective_id=0, has_side_effects=True, vmem_limit_bytes=58 * 2**20
        ),
        cost_estimate=pl.CostEstimate(
            flops=2 * 11 * cells * cell * width * share + 4 * 11 * cells * cell * block * share,
            bytes_accessed=4 * taps * block * both * 2,
            transcendentals=cells * cell * share,
        ),
    )(own, enc_taps, dec_taps)


def shards(inputs, enc_weight, dec_weight, cotangent):
    parts = lax.axis_size("seq")
    cores = lax.axis_size("chan")
    rows, width = inputs.shape
    chunk = rows // 2
    block, taps, share = enc_weight.shape
    wide = cotangent.shape[1]
    fits = parts == 8 and cores == 2 and lax.axis_size("groups") == 2 and taps == 5
    fits = fits and block == 96 and share % (2 * LANES) == 0 and wide % LANES == 0 and chunk == 256
    if not fits:
        return wide_shards(inputs, enc_weight, dec_weight, cotangent)
    core = lax.axis_index("chan")

    skip = lax.dynamic_slice_in_dim(inputs, core * wide, wide, 1)
    pooled = (skip.astype(F32).reshape(chunk, 2, wide).sum(axis=1) * 0.5).astype(BF16)
    cot = cotangent.reshape(chunk, 2, wide)
    own = jnp.stack([pooled, cot[:, 0], cot[:, 1]])
    grads, back = pair_call(own, enc_weight.transpose(1, 0, 2), dec_weight.transpose(1, 0, 2), parts // 2)
    decoded = jnp.stack([back[1], back[2]], axis=1).reshape(rows, wide)
    mixed_out = (skip.astype(F32) + decoded).astype(BF16)
    input_grad = (cotangent.astype(F32) + 0.5 * jnp.repeat(back[0], 2, axis=0)).astype(BF16)
    return mixed_out, input_grad, grads[0].transpose(1, 0, 2), grads[1].transpose(1, 0, 2)


def solution(mesh):
    return jax.shard_map(
        shards,
        mesh=mesh,
        in_specs=(
            P(("groups", "seq"), None),
            P("seq", None, "chan"),
            P("seq", None, "chan"),
            P(("groups", "seq"), "chan"),
        ),
        out_specs=(
            P(("groups", "seq"), "chan"),
            P(("groups", "seq"), "chan"),
            P(("groups", "seq"), None, "chan"),
            P(("groups", "seq"), None, "chan"),
        ),
        check_vma=False,
    )
```

```python
import functools
import math

import jax
import jax.numpy as jnp
from jax import lax
from jax.experimental import pallas as pl
from jax.experimental.pallas import tpu as pltpu
from jax.sharding import PartitionSpec as P

BF16 = jnp.bfloat16
F32 = jnp.float32


def shift(array, by):
    length = array.shape[0]
    if by == 0:
        return array
    pad = jnp.zeros((abs(by),) + array.shape[1:], array.dtype)
    if by > 0:
        return jnp.concatenate([array[by:], pad], axis=0)
    return jnp.concatenate([pad, array[: length + by]], axis=0)


def to_columns(array, parts):
    rows, cols = array.shape
    blocks = array.reshape(rows, parts, cols // parts).transpose(1, 0, 2)
    return lax.all_to_all(blocks, "seq", 0, 0, tiled=True)


def to_rows(blocks):
    parts, rows, cols = blocks.shape
    got = lax.all_to_all(blocks, "seq", 0, 0, tiled=True)
    return got.transpose(1, 0, 2).reshape(rows, parts * cols)


PIECES = 2


def ring_place(index, n):
    if n != 8:
        return index
    y = lax.rem(index, 2)
    z = index // 2
    return z + y * (n - 1 - 2 * z)


def ring_index(place, n):
    place = lax.rem(place + 2 * n, n)
    if n != 8:
        return place
    back = place // (n // 2)
    return 2 * place + back * (2 * n - 1 - 4 * place)


def gelu_and_slope(v):
    scale = math.sqrt(2.0 / math.pi)
    square = v * v
    th = jnp.tanh(scale * (v + 0.044715 * square * v))
    up = 0.5 * (1.0 + th)
    slope = up + 0.5 * v * (1.0 - th * th) * (scale * (1.0 + 3.0 * 0.044715 * square))
    return v * up, slope


def ring_kernel(
    n, x_ref, y_ref, enc_ref, dec_ref, out_ref, slots, term, mine,
    rs_send, rs_recv, ag_send, ag_recv, local_sem,
):
    me = lax.axis_index("seq")
    place = ring_place(me, n)
    nexts = (ring_index(place + 1, n), ring_index(place - 1, n))
    half = x_ref.shape[1]
    share = enc_ref.shape[1]
    side = half // 2
    piece = side // PIECES

    barrier = pltpu.get_barrier_semaphore()
    for other in nexts:
        pl.semaphore_signal(
            barrier, inc=1, device_id={"seq": other}, device_id_type=pl.DeviceIdType.MESH
        )
    pl.semaphore_wait(barrier, 2)

    def signed(d, steps):
        return place - steps if d == 0 else place + steps

    def own_term(d, steps):
        chunk = ring_index(signed(d, steps), n)
        at = pl.ds(d * side, side)
        a = jnp.dot(x_ref[chunk, at, :], enc_ref[...], preferred_element_type=jnp.float32)
        b = jnp.dot(y_ref[chunk, at, :], dec_ref[...], preferred_element_type=jnp.float32)
        return a, b

    def rs_copy(d, s, q):
        at = pl.ds(q * piece, piece)
        return pltpu.make_async_remote_copy(
            src_ref=slots.at[d, s, at],
            dst_ref=slots.at[d, s + 1, at],
            send_sem=rs_send.at[d, s, q],
            recv_sem=rs_recv.at[d, s, q],
            device_id={"seq": nexts[d]},
            device_id_type=pl.DeviceIdType.MESH,
        )

    def ag_copy(d, s, q, first):
        at = pl.ds(d * side + q * piece, piece)
        owner = ring_index(signed(d, s), n)
        return pltpu.make_async_remote_copy(
            src_ref=mine.at[at] if first else out_ref.at[owner, at],
            dst_ref=out_ref.at[owner, at],
            send_sem=ag_send.at[d, s, q],
            recv_sem=ag_recv.at[d, s, q],
            device_id={"seq": nexts[d]},
            device_id_type=pl.DeviceIdType.MESH,
        )

    for d in range(2):
        a, b = own_term(d, 1)
        slots[d, 0, :, :share] = a.astype(BF16)
        slots[d, 0, :, share:] = b.astype(BF16)
        for q in range(PIECES):
            rs_copy(d, 0, q).start()

    def fill(s):
        for d in range(2):
            a, b = own_term(d, s + 2)
            term[d, :, :share] = a
            term[d, :, share:] = b

    def rs_step(s, carry):
        fill(s)
        for q in range(PIECES):
            at = pl.ds(q * piece, piece)
            for d in range(2):
                rs_copy(d, s, q).wait_recv()
                total = slots[d, s + 1, at, :].astype(F32) + term[d, at, :]
                slots[d, s + 1, at, :] = total.astype(BF16)
                rs_copy(d, s + 1, q).start()
        return carry

    lax.fori_loop(0, n - 2, rs_step, 0)
    fill(n - 2)
    for q in range(PIECES):
        at = pl.ds(q * piece, piece)
        for d in range(2):
            rs_copy(d, n - 2, q).wait_recv()
            rows = pl.ds(d * side + q * piece, piece)
            pre = slots[d, n - 1, at, :share].astype(F32) + term[d, at, :share]
            grad = slots[d, n - 1, at, share:].astype(F32) + term[d, at, share:]
            value, slope = gelu_and_slope(pre)
            mine[rows, :share] = value.astype(BF16)
            mine[rows, share:] = (grad * slope).astype(BF16)
            ag_copy(d, 0, q, True).start()
    local = pltpu.make_async_copy(mine, out_ref.at[me], local_sem)
    local.start()

    def ag_step(s, carry):
        for q in range(PIECES):
            for d in range(2):
                incoming(d, s, q).wait_recv()
                ag_copy(d, s + 1, q, False).start()
        return carry

    def incoming(d, s, q):
        at = pl.ds(d * side + q * piece, piece)
        owner = ring_index(signed(d, s + 1), n)
        return pltpu.make_async_remote_copy(
            src_ref=mine.at[at],
            dst_ref=out_ref.at[owner, at],
            send_sem=ag_send.at[d, s, q],
            recv_sem=ag_recv.at[d, s, q],
            device_id={"seq": nexts[d]},
            device_id_type=pl.DeviceIdType.MESH,
        )

    lax.fori_loop(0, n - 2, ag_step, 0)
    for q in range(PIECES):
        for d in range(2):
            incoming(d, n - 2, q).wait_recv()

    def drain(s, carry):
        for q in range(PIECES):
            for d in range(2):
                rs_copy(d, s, q).wait_send()
                ag_copy(d, s, q, True).wait_send()
        return carry

    lax.fori_loop(0, n - 1, drain, 0)
    local.wait()


def ring(pool_taps, cot_taps, enc_mat, dec_mat, n):
    half = pool_taps.shape[1]
    share = enc_mat.shape[1]
    depth = enc_mat.shape[0]
    vmem = pl.BlockSpec(memory_space=pltpu.VMEM)
    steps = (2, n - 1, PIECES)
    return pl.pallas_call(
        functools.partial(ring_kernel, n),
        out_shape=jax.ShapeDtypeStruct((n, half, 2 * share), BF16),
        in_specs=[vmem] * 4,
        out_specs=pl.BlockSpec(memory_space=pl.ANY),
        scratch_shapes=[
            pltpu.VMEM((2, n, half // 2, 2 * share), BF16),
            pltpu.VMEM((2, half // 2, 2 * share), F32),
            pltpu.VMEM((half, 2 * share), BF16),
            pltpu.SemaphoreType.DMA(steps),
            pltpu.SemaphoreType.DMA(steps),
            pltpu.SemaphoreType.DMA(steps),
            pltpu.SemaphoreType.DMA(steps),
            pltpu.SemaphoreType.DMA,
        ],
        compiler_params=pltpu.CompilerParams(
            collective_id=0, has_side_effects=True, vmem_limit_bytes=48 * 2**20
        ),
        cost_estimate=pl.CostEstimate(
            flops=4 * n * half * depth * share,
            bytes_accessed=4 * n * half * share * 2,
            transcendentals=half * share,
        ),
    )(pool_taps, cot_taps, enc_mat, dec_mat)


def wide_shards(inputs, enc_weight, dec_weight, cotangent):
    parts = lax.axis_size("seq")
    rows, width = inputs.shape
    half = rows // 2
    total = half * parts
    block, taps, share = enc_weight.shape
    half_width = cotangent.shape[1]

    pooled = (inputs.astype(F32).reshape(half, 2, width).sum(axis=1) * 0.5).astype(BF16)
    cot_full = lax.all_gather(cotangent, "chan", axis=1, tiled=True)
    core = lax.axis_index("chan")
    cores = lax.axis_size("chan")
    few = half // cores
    leaving = jnp.concatenate(
        [
            lax.dynamic_slice_in_dim(pooled, core * few, few, 0),
            lax.dynamic_slice_in_dim(cot_full, core * 2 * few, 2 * few, 0),
        ],
        axis=0,
    )
    columns = to_columns(leaving, parts).reshape(parts, 1, 3 * few, block)
    columns = lax.all_gather(columns, "chan", axis=1, tiled=True)
    pool_col = columns[:, :, :few].reshape(total, block)
    cot_col = columns[:, :, few:].reshape(total, 2, block).astype(F32)
    even = cot_col[:, 0]
    odd = cot_col[:, 1]
    pair = (even + odd).astype(BF16)
    cross = (odd + shift(even, 1)).astype(BF16)
    before = jnp.concatenate([even[:1].astype(BF16), cross[:-1]], axis=0)
    pool_taps = jnp.concatenate([shift(pool_col, t - 2) for t in range(taps)], axis=1)
    cot_taps = jnp.concatenate([shift(pair, 1), cross, pair, before, shift(pair, -1)], axis=1)
    enc_mat = enc_weight.transpose(1, 0, 2).reshape(taps * block, share)
    dec_mat = dec_weight.transpose(1, 0, 2).reshape(taps * block, share)

    joint = ring(
        pool_taps.reshape(parts, half, taps * block),
        cot_taps.reshape(parts, half, taps * block),
        enc_mat,
        dec_mat,
        parts,
    ).reshape(total, 2 * share)
    hidden_all = joint[:, :share]
    grad_all = joint[:, share:]

    contract_rows = (((0,), (0,)), ((), ()))
    contract_last = (((1,), (1,)), ((), ()))
    dec_grad = lax.dot_general(cot_taps, hidden_all, contract_rows, preferred_element_type=F32)
    enc_grad = lax.dot_general(pool_taps, grad_all, contract_rows, preferred_element_type=F32)
    dec_grad = dec_grad.astype(BF16).reshape(taps, block, share).transpose(1, 0, 2)
    enc_grad = enc_grad.astype(BF16).reshape(taps, block, share).transpose(1, 0, 2)

    dec_out = lax.dot_general(hidden_all, dec_mat, contract_last, preferred_element_type=F32)
    p0, p1, p2, p3, p4 = [dec_out[:, t * block : (t + 1) * block] for t in range(taps)]
    after4 = shift(p4, 1)
    before0 = shift(p0, -1)
    dec_even = before0 + shift(p1, -1) + p2 + p3 + after4
    dec_odd = before0 + p1 + p2 + shift(p3, 1) + after4
    decoded = jnp.stack([dec_even, dec_odd], axis=1).astype(BF16).reshape(parts, rows, block)
    enc_out = lax.dot_general(grad_all, enc_mat, contract_last, preferred_element_type=F32)
    pool_grad = sum(shift(enc_out[:, t * block : (t + 1) * block], 2 - t) for t in range(taps))
    pool_grad = pool_grad.astype(BF16).reshape(parts, half, block)
    mine = jnp.concatenate([decoded, pool_grad], axis=1)
    mine = lax.psum_scatter(mine, "chan", scatter_dimension=1, tiled=True)
    mine = lax.all_gather(to_rows(mine), "chan", axis=0, tiled=True)
    col_start = core * half_width
    mine = lax.dynamic_slice_in_dim(mine, col_start, half_width, 1).astype(F32)

    skip = lax.dynamic_slice_in_dim(inputs, col_start, half_width, 1)
    mixed_out = (skip.astype(F32) + mine[:rows]).astype(BF16)
    input_grad = (cotangent.astype(F32) + 0.5 * jnp.repeat(mine[rows:], 2, axis=0)).astype(BF16)
    return mixed_out, input_grad, enc_grad, dec_grad


LANES = 128
HALO = 16
EDGE = 8


def pair_kernel(
    x_ref, enc_ref, dec_ref, cot_ref, mixed_ref, in_grad_ref, grad_ref,
    x_own, spread, pc_ref, rows_all, weights, folded, z_enc, z_dec, hid, pre_grad, g_taps, h_taps,
    enc_sum, dec_sum, part, give, take, give_y, take_y, grad_give,
    local_sem, wy_send, wy_recv, wz_send, wz_recv, wx_send, wx_recv,
    edge_send, edge_z, edge_y, edge_c, edge_fwd, edge_ysend, edge_csend,
    own_send, pz_send, pz_recv, py_send, py_recv, pc_send, pc_recv,
    give_sem, take_sem, grad_sem,
):
    g = lax.axis_index("groups")
    s = lax.axis_index("seq")
    c = lax.axis_index("chan")
    z, y = s // 2, lax.rem(s, 2)
    last = lax.axis_size("seq") // 2 - 1
    chunk, wide = pc_ref.shape[1], pc_ref.shape[2]
    cell = 2 * chunk
    taps, block = enc_ref.shape[0], enc_ref.shape[1]
    share = enc_ref.shape[2] // 2
    half = block // 2
    inner = chunk - HALO
    ids = pl.DeviceIdType.MESH
    to_y, to_x, to_c = {"seq": s + 1 - 2 * y}, {"groups": 1 - g}, {"chan": 1 - c}
    to_left, to_right = {"seq": s - 2}, {"seq": s + 2}
    has_left, has_right = z > 0, z < last

    def lanes(index, width):
        return pl.ds(pl.multiple_of(index * width, LANES), width)

    own_x = pltpu.make_async_copy(x_ref.at[:, lanes(c, wide)], x_own, local_sem.at[0, taps + 1])
    own_x.start()
    barrier = pltpu.get_barrier_semaphore()
    for where in (to_y, to_x, to_c):
        pl.semaphore_signal(barrier, inc=1, device_id=where, device_id_type=ids)

    @pl.when(has_left)
    def _():
        pl.semaphore_signal(barrier, inc=1, device_id=to_left, device_id_type=ids)

    @pl.when(has_right)
    def _():
        pl.semaphore_signal(barrier, inc=1, device_id=to_right, device_id_type=ids)

    inside = jnp.where(has_left, 1, 0) + jnp.where(has_right, 1, 0)
    pl.semaphore_wait(barrier, 3 + inside)

    def remote(src, dst, send, recv, where):
        return pltpu.make_async_remote_copy(
            src_ref=src, dst_ref=dst, send_sem=send, recv_sem=recv,
            device_id=where, device_id_type=ids,
        )

    sources = (enc_ref, dec_ref)

    def own_weight(w, t):
        return pltpu.make_async_copy(
            sources[w].at[t, :, lanes(y, share)],
            weights.at[w, pl.ds(pl.multiple_of(s * block, HALO), block), pl.ds(t * share, share)],
            local_sem.at[w, t],
        )

    def weight_to_y(w, t, side):
        at = pl.ds(pl.multiple_of(side * half, HALO), half)
        row = pl.multiple_of(s * block + side * half, HALO)
        return remote(
            sources[w].at[t, at, lanes(1 - y, share)],
            weights.at[w, pl.ds(row, half), pl.ds(t * share, share)],
            wy_send.at[w, t, side], wy_recv.at[w, t, side], to_y,
        )

    def slab(w, b, side):
        return weights.at[w, pl.ds(pl.multiple_of(b * block + side * half, HALO), half), :]

    def weight_z(w, zz, b, d, where):
        ref = slab(w, 2 * zz + b, g)
        return remote(ref, ref, wz_send.at[d, w, zz, b], wz_recv.at[w, zz, b], where)

    def weight_x(w, zz, b, side):
        ref = slab(w, 2 * zz + b, side)
        return remote(ref, ref, wx_send.at[w, zz, b], wx_recv.at[w, zz, b], to_x)

    def edge_of(zz, yy, cc):
        at = pl.multiple_of(HALO + (2 * zz + yy) * chunk + yy * inner, HALO)
        return rows_all.at[:, pl.ds(at, HALO), lanes(cc, wide)]

    def inner_of(i, zz, yy, cc):
        at = pl.multiple_of(HALO + (2 * zz + yy) * chunk + (1 - yy) * HALO, HALO)
        return rows_all.at[i, pl.ds(at, inner), lanes(cc, wide)]

    own_edge = pc_ref.at[:, pl.ds(pl.multiple_of(y * inner, HALO), HALO), :]

    def own_inner(i):
        return pc_ref.at[i, pl.ds(pl.multiple_of((1 - y) * HALO, HALO), inner), :]

    local_edge = pltpu.make_async_copy(own_edge, edge_of(z, y, c), local_sem.at[0, taps])
    local_inner = [
        pltpu.make_async_copy(own_inner(i), inner_of(i, z, y, c), local_sem.at[1, taps + i])
        for i in range(3)
    ]

    for w in range(2):
        for t in range(taps):
            own_weight(w, t).start()
            weight_to_y(w, t, g).start()

    def edge_out(d, where):
        return remote(own_edge, edge_of(z, y, c), edge_send.at[d], edge_z.at[z], where)

    def edge_forward(zz, where):
        ref = edge_of(zz, y, c)
        return remote(ref, ref, edge_fwd.at[zz], edge_z.at[zz], where)

    def edge_to_y(zz):
        src = edge_of(zz, y, c)
        return remote(src, src, edge_ysend.at[zz], edge_y.at[zz], to_y)

    def edge_to_c(zz, yy):
        ref = edge_of(zz, yy, c)
        return remote(ref, ref, edge_csend.at[zz, yy], edge_c.at[zz, yy], to_c)

    tiles = wide // LANES
    own_x.wait()
    for k in range(tiles):
        cols = slice(k * LANES, (k + 1) * LANES)
        spread[k] = x_own[:, cols].astype(F32)
        spread[tiles + k] = cot_ref[:, cols].astype(F32)
    for k in range(tiles):
        cols = slice(k * LANES, (k + 1) * LANES)
        even, odd = pl.ds(0, chunk, stride=2), pl.ds(1, chunk, stride=2)
        pc_ref[0, :, cols] = ((spread[k, even, :] + spread[k, odd, :]) * 0.5).astype(BF16)
        pc_ref[1, :, cols] = spread[tiles + k, even, :].astype(BF16)
        pc_ref[2, :, cols] = spread[tiles + k, odd, :].astype(BF16)

    local_edge.start()

    @pl.when(has_left)
    def _():
        edge_out(0, to_left).start()

    @pl.when(has_right)
    def _():
        edge_out(1, to_right).start()

    for copy in local_inner:
        copy.start()
    rows_all[:, :HALO, :] = jnp.zeros((3, HALO, 2 * wide), BF16)
    bottom = rows_all.shape[1] - HALO
    rows_all[:, bottom:, :] = jnp.zeros((3, HALO, 2 * wide), BF16)
    local_edge.wait()
    edge_to_y(z).start()
    edge_to_c(z, y).start()

    for w in range(2):
        for t in range(taps):
            own_weight(w, t).wait()

        @pl.when(has_left)
        def _():
            weight_z(w, z, y, 0, to_left).start()

        @pl.when(has_right)
        def _():
            weight_z(w, z, y, 1, to_right).start()

    for w in range(2):
        for t in range(taps):
            weight_from_y(
                weights, sources, wy_send, wy_recv, w, t, g, s, y, half, block, share, to_y, lanes
            ).wait_recv()

        @pl.when(has_left)
        def _():
            weight_z(w, z, 1 - y, 0, to_left).start()

        @pl.when(has_right)
        def _():
            weight_z(w, z, 1 - y, 1, to_right).start()

    for w in range(2):
        for t in range(taps):
            weight_to_y(w, t, 1 - g).start()

    def inner_to_y(i, zz):
        ref = inner_of(i, zz, y, c)
        return remote(ref, ref, py_send.at[zz, i], py_recv.at[zz, i], to_y)

    def inner_to_c(i, zz, yy):
        ref = inner_of(i, zz, yy, c)
        return remote(ref, ref, pc_send.at[zz, yy, i], pc_recv.at[zz, yy, i], to_c)

    def inner_out(i, d, where):
        return remote(own_inner(i), inner_of(i, z, y, c), own_send.at[d, i], pz_recv.at[z, i], where)

    for i in range(3):
        local_inner[i].wait()
        inner_to_y(i, z).start()
        inner_to_c(i, z, y).start()

    def order(k):
        low = jnp.minimum(z, last - z)
        near = jnp.where(low == 0, k, jnp.where(k < 2, 1 - k, k))
        return jnp.where(z * 2 < last, near, last - near)

    def edge_arrives_y(zz):
        ref = edge_of(zz, 1 - y, c)
        return remote(ref, ref, edge_ysend.at[zz], edge_y.at[zz], to_y)

    def send_own_rows(d, where):
        for i in range(3):
            inner_out(i, d, where).start()

    @pl.when(z == 0)
    def _():
        send_own_rows(1, to_right)

    @pl.when(z == last)
    def _():
        send_own_rows(0, to_left)

    def weight_step(k, carry):
        for sign in (-1, 1):
            zz = z + sign * k

            @pl.when((zz >= 0) & (zz <= last))
            def _():
                for w in range(2):
                    for b in range(2):
                        weight_z(w, zz, b, 0, to_y).wait_recv()

                        if sign < 0:
                            @pl.when(has_right)
                            def _():
                                weight_z(w, zz, b, 1, to_right).start()
                        else:
                            @pl.when(has_left)
                            def _():
                                weight_z(w, zz, b, 0, to_left).start()

                        weight_x(w, zz, b, g).start()

                edge_forward(zz, to_y).wait_recv()
                if sign < 0:
                    @pl.when(has_right)
                    def _():
                        edge_forward(zz, to_right).start()
                else:
                    @pl.when(has_left)
                    def _():
                        edge_forward(zz, to_left).start()

                edge_to_y(zz).start()
                edge_to_c(zz, y).start()

        @pl.when((z == k) & has_right)
        def _():
            send_own_rows(1, to_right)

        @pl.when((last - z == k) & has_left)
        def _():
            send_own_rows(0, to_left)

        return carry

    lax.fori_loop(1, last + 1, weight_step, 0)

    def inner_forward(i, zz, where):
        ref = inner_of(i, zz, y, c)
        return remote(ref, ref, pz_send.at[zz, i], pz_recv.at[zz, i], where)

    def receive(i, zz):
        inner_forward(i, zz, to_y).wait_recv()

        @pl.when((zz < z) & has_right)
        def _():
            inner_forward(i, zz, to_right).start()

        @pl.when((zz > z) & has_left)
        def _():
            inner_forward(i, zz, to_left).start()

        inner_to_y(i, zz).start()
        inner_to_c(i, zz, y).start()

    ahead = 1 + jnp.where(has_left & has_right, 1, 0)

    def receive_step(k, carry):
        for i in range(3):
            receive(i, order(k))
        return carry

    lax.fori_loop(1, 1 + ahead, receive_step, 0)

    def edge_end(zz, carry):
        edge_arrives_y(zz).wait_recv()
        edge_to_c(zz, 1 - y).start()
        return carry

    lax.fori_loop(0, last + 1, edge_end, 0)
    for zz in range(last + 1):
        for yy in range(2):
            ref = edge_of(zz, yy, 1 - c)
            remote(ref, ref, edge_csend.at[zz, yy], edge_c.at[zz, yy], to_c).wait_recv()

    def each_other_cell(body):
        def step(k, carry):
            body(order(k))
            return carry

        lax.fori_loop(1, last + 1, step, 0)

    for w in range(2):
        for t in range(taps):
            weight_from_y(
                weights, sources, wy_send, wy_recv, w, t, 1 - g, s, y, half, block, share, to_y, lanes
            ).wait_recv()

    def wait_x(zz):
        for w in range(2):
            for b in range(2):
                weight_x(w, zz, b, 1 - g).wait_recv()

    each_other_cell(wait_x)

    step_rows = 64

    def fold(i, carry):
        at = pl.ds(pl.multiple_of(i * step_rows, HALO), step_rows)
        w = [weights[1, at, t * share : (t + 1) * share].astype(F32) for t in range(5)]
        folded[0, at, :share] = (w[0] + w[1]).astype(BF16)
        folded[0, at, share : 2 * share] = (w[2] + w[3]).astype(BF16)
        folded[0, at, 2 * share :] = weights[1, at, 4 * share :]
        folded[1, at, :share] = weights[1, at, :share]
        folded[1, at, share : 2 * share] = (w[1] + w[2]).astype(BF16)
        folded[1, at, 2 * share :] = (w[3] + w[4]).astype(BF16)
        return carry

    lax.fori_loop(0, weights.shape[1] // step_rows, fold, 0)

    contract_rows = (((0,), (0,)), ((), ()))
    contract_last = (((1,), (1,)), ((), ()))
    wide_rows = cell + 2 * HALO
    mid_rows = cell + 2 * EDGE
    window = pl.ds(pl.multiple_of((2 * block * z) // LANES * LANES, LANES), 2 * LANES)
    offset = 2 * block * z - (2 * block * z) // LANES * LANES

    enc_sum[...] = jnp.zeros_like(enc_sum)
    dec_sum[...] = jnp.zeros_like(dec_sum)

    def sums_over_cores():
        for i in range(3):
            total = part[i] + take[i].astype(F32)
            part[i] = total
            rows = pl.ds(pl.multiple_of((1 - y) * chunk, HALO), chunk)
            give_y[i] = part[i, rows, :].astype(BF16)

    give_copy = remote(give, take, give_sem.at[0], take_sem.at[0], to_c)
    give_y_copy = remote(give_y, take_y, give_sem.at[1], take_sem.at[1], to_y)

    def cell_step(k, carry):
        zz = order(k)

        def receive_ahead(i):
            @pl.when(k + ahead + 1 <= last)
            def _():
                receive(i, order(k + ahead + 1))

        for i in range(3):
            ref = inner_of(i, zz, 1 - y, c)
            remote(ref, ref, py_send.at[zz, i], py_recv.at[zz, i], to_y).wait_recv()
            inner_to_c(i, zz, 1 - y).start()
        for yy in range(2):
            for i in range(3):
                ref = inner_of(i, zz, yy, 1 - c)
                remote(ref, ref, pc_send.at[zz, yy, i], pc_recv.at[zz, yy, i], to_c).wait_recv()

        base = pl.multiple_of(zz * cell, HALO)
        at = pl.ds(base, wide_rows)
        product = jnp.dot(rows_all[0, at, :], weights[0], preferred_element_type=F32)
        for t in range(5 * tiles):
            z_enc[t] = product[:, t * LANES : (t + 1) * LANES]
        receive_ahead(0)
        product = jnp.dot(
            rows_all[1, at, :], folded[0], preferred_element_type=F32
        ) + jnp.dot(rows_all[2, at, :], folded[1], preferred_element_type=F32)
        for t in range(3 * tiles):
            z_dec[t] = product[:, t * LANES : (t + 1) * LANES]
        receive_ahead(1)

        piece = mid_rows // 6

        def activate(r, carry):
            start = pl.multiple_of(r * piece, EDGE)
            for k in range(tiles):
                pre = z_enc[k, pl.ds(start + 6, piece), :]
                for t in range(1, 5):
                    pre += z_enc[t * tiles + k, pl.ds(start + 6 + t, piece), :]
                grad = z_dec[k, pl.ds(start + 9, piece), :]
                for t in range(1, 3):
                    grad += z_dec[t * tiles + k, pl.ds(start + 9 - t, piece), :]
                value, slope = gelu_and_slope(pre)
                hid[k, pl.ds(start, piece), :] = value
                pre_grad[k, pl.ds(start, piece), :] = grad * slope
            return carry

        lax.fori_loop(0, 6, activate, 0)

        @pl.when(zz == 0)
        def _():
            hid[:, :EDGE, :] = jnp.zeros((tiles, EDGE, LANES), F32)
            pre_grad[:, :EDGE, :] = jnp.zeros((tiles, EDGE, LANES), F32)

        @pl.when(zz == last)
        def _():
            hid[:, mid_rows - EDGE :, :] = jnp.zeros((tiles, EDGE, LANES), F32)
            pre_grad[:, mid_rows - EDGE :, :] = jnp.zeros((tiles, EDGE, LANES), F32)

        def shifted(r, carry):
            start = pl.multiple_of(r * LANES, HALO)
            to = pl.ds(start, LANES)
            for k in range(tiles):
                for t in range(5):
                    at = t * share + k * LANES
                    moved = pre_grad[k, pl.ds(start + EDGE + 2 - t, LANES), :]
                    g_taps[to, at : at + LANES] = moved.astype(BF16)
                for t in range(3):
                    at = t * share + k * LANES
                    moved = hid[k, pl.ds(start + EDGE - 1 + t, LANES), :]
                    h_taps[to, at : at + LANES] = moved.astype(BF16)
            return carry

        lax.fori_loop(0, cell // LANES, shifted, 0)

        receive_ahead(2)
        body = pl.ds(base + HALO, cell)
        enc_sum[...] += lax.dot_general(
            rows_all[0, body, window], g_taps[...], contract_rows, preferred_element_type=F32
        )
        for i in range(2):
            dec_sum[i] += lax.dot_general(
                rows_all[1 + i, body, window], h_taps[...], contract_rows,
                preferred_element_type=F32,
            )

        @pl.when(k == 0)
        def _():
            for i in range(3):
                for h in range(2):
                    cols = pl.ds(pl.multiple_of((c if h == 0 else 1 - c) * wide, LANES), wide)
                    rhs = weights[0, cols, :] if i == 0 else folded[i - 1, cols, :]
                    lhs = g_taps[...] if i == 0 else h_taps[...]
                    value = lax.dot_general(lhs, rhs, contract_last, preferred_element_type=F32)
                    if h == 0:
                        part[i] = value
                    else:
                        give[i] = value.astype(BF16)
            give_copy.start()

        @pl.when(k == last - 1)
        def _():
            give_copy.wait_recv()
            sums_over_cores()
            give_y_copy.start()

        return carry

    lax.fori_loop(0, last + 1, cell_step, 0)

    def grad_copy(w):
        return remote(
            grad_give.at[w], grad_ref.at[w, :, :, lanes(y, share)], grad_sem.at[0, w], grad_sem.at[1, w], to_y
        )

    def grads(w, who):
        at = pl.ds(pl.multiple_of(offset + who * block, HALO), block)
        if w == 0:
            return [enc_sum[at, t * share : (t + 1) * share].astype(BF16) for t in range(5)]
        e = [dec_sum[0, at, k * share : (k + 1) * share] for k in range(3)]
        o = [dec_sum[1, at, k * share : (k + 1) * share] for k in range(3)]
        both = (e[0] + o[0], e[0] + o[1], e[1] + o[1], e[1] + o[2], e[2] + o[2])
        return [v.astype(BF16) for v in both]

    for w in range(2):
        for t, value in enumerate(grads(w, 1 - y)):
            grad_give[w, t] = value
        grad_copy(w).start()
    for w in range(2):
        for t, value in enumerate(grads(w, y)):
            grad_ref[w, t, :, lanes(y, share)] = value

    give_y_copy.wait_recv()
    for k in range(tiles):
        cols = slice(k * LANES, (k + 1) * LANES)
        even, odd = pl.ds(0, chunk, stride=2), pl.ds(1, chunk, stride=2)
        own = pl.ds(pl.multiple_of(y * chunk, HALO), chunk)
        pool_grad, first, second = [part[i, own, cols] + take_y[i, :, cols].astype(F32) for i in range(3)]
        spread[k, even, :] = first
        spread[k, odd, :] = second
        spread[tiles + k, even, :] = pool_grad
        spread[tiles + k, odd, :] = pool_grad
        mixed_ref[:, cols] = (x_own[:, cols].astype(F32) + spread[k]).astype(BF16)
        in_grad_ref[:, cols] = (cot_ref[:, cols].astype(F32) + 0.5 * spread[tiles + k]).astype(BF16)

    give_copy.wait_send()
    give_y_copy.wait_send()
    for w in range(2):
        for t in range(taps):
            weight_to_y(w, t, g).wait_send()
            weight_to_y(w, t, 1 - g).wait_send()

    @pl.when(has_left)
    def _():
        edge_out(0, to_left).wait_send()
        for i in range(3):
            inner_out(i, 0, to_left).wait_send()
        for w in range(2):
            for b in range(2):
                weight_z(w, z, b, 0, to_left).wait_send()

    @pl.when(has_right)
    def _():
        edge_out(1, to_right).wait_send()
        for i in range(3):
            inner_out(i, 1, to_right).wait_send()
        for w in range(2):
            for b in range(2):
                weight_z(w, z, b, 1, to_right).wait_send()

    def drain(k, carry):
        zz = order(k)
        edge_to_y(zz).wait_send()
        for yy in range(2):
            edge_to_c(zz, yy).wait_send()
        for i in range(3):
            inner_to_y(i, zz).wait_send()
            for yy in range(2):
                inner_to_c(i, zz, yy).wait_send()

        @pl.when(k > 0)
        def _():
            for w in range(2):
                for b in range(2):
                    weight_x(w, zz, b, g).wait_send()

        @pl.when((zz < z) & has_right)
        def _():
            edge_forward(zz, to_right).wait_send()
            for i in range(3):
                inner_forward(i, zz, to_right).wait_send()
            for w in range(2):
                for b in range(2):
                    weight_z(w, zz, b, 1, to_right).wait_send()

        @pl.when((zz > z) & has_left)
        def _():
            edge_forward(zz, to_left).wait_send()
            for i in range(3):
                inner_forward(i, zz, to_left).wait_send()
            for w in range(2):
                for b in range(2):
                    weight_z(w, zz, b, 0, to_left).wait_send()

        return carry

    lax.fori_loop(0, last + 1, drain, 0)
    for w in range(2):
        grad_copy(w).wait_send()
    for w in range(2):
        grad_arrives = remote(
            grad_give.at[w], grad_ref.at[w, :, :, lanes(1 - y, share)],
            grad_sem.at[0, w], grad_sem.at[1, w], to_y,
        )
        grad_arrives.wait_recv()


def weight_from_y(weights, sources, send, recv, w, t, side, s, y, half, block, share, to_y, lanes):
    other = s + 1 - 2 * y
    row = pl.multiple_of(other * block + side * half, HALO)
    return pltpu.make_async_remote_copy(
        src_ref=sources[w].at[t, pl.ds(pl.multiple_of(side * half, HALO), half), lanes(1 - y, share)],
        dst_ref=weights.at[w, pl.ds(row, half), pl.ds(t * share, share)],
        send_sem=send.at[w, t, side],
        recv_sem=recv.at[w, t, side],
        device_id=to_y,
        device_id_type=pl.DeviceIdType.MESH,
    )


def pair_call(inputs, enc_taps, dec_taps, cotangent, cells):
    rows, wide = cotangent.shape
    chunk = rows // 2
    taps, block, both = enc_taps.shape
    share = both // 2
    cell = 2 * chunk
    vmem = pl.BlockSpec(memory_space=pltpu.VMEM)
    anywhere = pl.BlockSpec(memory_space=pl.ANY)
    dma = pltpu.SemaphoreType.DMA
    tall = cells * cell + 2 * HALO
    width = 2 * wide
    return pl.pallas_call(
        pair_kernel,
        out_shape=[
            jax.ShapeDtypeStruct((rows, wide), BF16),
            jax.ShapeDtypeStruct((rows, wide), BF16),
            jax.ShapeDtypeStruct((2, taps, block, both), BF16),
        ],
        in_specs=[anywhere, anywhere, anywhere, vmem],
        out_specs=[vmem, vmem, vmem],
        scratch_shapes=[
            pltpu.VMEM((rows, wide), BF16),
            pltpu.VMEM((2 * (wide // LANES), rows, LANES), F32),
            pltpu.VMEM((3, chunk, wide), BF16),
            pltpu.VMEM((3, tall, width), BF16),
            pltpu.VMEM((2, width, taps * share), BF16),
            pltpu.VMEM((2, width, 3 * share), BF16),
            pltpu.VMEM((taps * share // LANES, cell + 2 * HALO, LANES), F32),
            pltpu.VMEM((3 * share // LANES, cell + 2 * HALO, LANES), F32),
            pltpu.VMEM((share // LANES, cell + 2 * EDGE, LANES), F32),
            pltpu.VMEM((share // LANES, cell + 2 * EDGE, LANES), F32),
            pltpu.VMEM((cell, taps * share), BF16),
            pltpu.VMEM((cell, 3 * share), BF16),
            pltpu.VMEM((2 * LANES, taps * share), F32),
            pltpu.VMEM((2, 2 * LANES, 3 * share), F32),
            pltpu.VMEM((3, cell, wide), F32),
            pltpu.VMEM((3, cell, wide), BF16),
            pltpu.VMEM((3, cell, wide), BF16),
            pltpu.VMEM((3, chunk, wide), BF16),
            pltpu.VMEM((3, chunk, wide), BF16),
            pltpu.VMEM((2, taps, block, share), BF16),
            dma((2, taps + 3)),
            dma((2, taps, 2)), dma((2, taps, 2)),
            dma((2, 2, cells, 2)), dma((2, cells, 2)), dma((2, cells, 2)), dma((2, cells, 2)),
            dma((2,)), dma((cells,)), dma((cells,)), dma((cells, 2)), dma((cells,)), dma((cells,)),
            dma((cells, 2)),
            dma((2, 3)), dma((cells, 3)), dma((cells, 3)), dma((cells, 3)), dma((cells, 3)),
            dma((cells, 2, 3)), dma((cells, 2, 3)),
            dma((2,)), dma((2,)), dma((2, 2)),
        ],
        compiler_params=pltpu.CompilerParams(
            collective_id=0, has_side_effects=True, vmem_limit_bytes=58 * 2**20
        ),
        cost_estimate=pl.CostEstimate(
            flops=2 * 11 * cells * cell * width * share + 4 * 11 * cells * cell * block * share,
            bytes_accessed=4 * taps * block * both * 2,
            transcendentals=cells * cell * share,
        ),
    )(inputs, enc_taps, dec_taps, cotangent)


def shards(inputs, enc_weight, dec_weight, cotangent):
    parts = lax.axis_size("seq")
    cores = lax.axis_size("chan")
    rows, width = inputs.shape
    chunk = rows // 2
    block, taps, share = enc_weight.shape
    wide = cotangent.shape[1]
    fits = parts == 8 and cores == 2 and lax.axis_size("groups") == 2 and taps == 5
    fits = fits and block == 96 and share == 2 * wide and wide % LANES == 0 and chunk == 256
    if not fits:
        return wide_shards(inputs, enc_weight, dec_weight, cotangent)
    mixed_out, input_grad, grads = pair_call(
        inputs, enc_weight.transpose(1, 0, 2), dec_weight.transpose(1, 0, 2), cotangent, parts // 2
    )
    return mixed_out, input_grad, grads[0].transpose(1, 0, 2), grads[1].transpose(1, 0, 2)


def solution(mesh):
    return jax.shard_map(
        shards,
        mesh=mesh,
        in_specs=(
            P(("groups", "seq"), None),
            P("seq", None, "chan"),
            P("seq", None, "chan"),
            P(("groups", "seq"), "chan"),
        ),
        out_specs=(
            P(("groups", "seq"), "chan"),
            P(("groups", "seq"), "chan"),
            P(("groups", "seq"), None, "chan"),
            P(("groups", "seq"), None, "chan"),
        ),
        check_vma=False,
    )
```

```python
import functools
import math

import jax
import jax.numpy as jnp
from jax import lax
from jax.experimental import pallas as pl
from jax.experimental.pallas import tpu as pltpu
from jax.sharding import PartitionSpec as P

BF16 = jnp.bfloat16
F32 = jnp.float32


def shift(array, by):
    length = array.shape[0]
    if by == 0:
        return array
    pad = jnp.zeros((abs(by),) + array.shape[1:], array.dtype)
    if by > 0:
        return jnp.concatenate([array[by:], pad], axis=0)
    return jnp.concatenate([pad, array[: length + by]], axis=0)


def to_columns(array, parts):
    rows, cols = array.shape
    blocks = array.reshape(rows, parts, cols // parts).transpose(1, 0, 2)
    return lax.all_to_all(blocks, "seq", 0, 0, tiled=True)


def to_rows(blocks):
    parts, rows, cols = blocks.shape
    got = lax.all_to_all(blocks, "seq", 0, 0, tiled=True)
    return got.transpose(1, 0, 2).reshape(rows, parts * cols)


PIECES = 2


def ring_place(index, n):
    if n != 8:
        return index
    y = lax.rem(index, 2)
    z = index // 2
    return z + y * (n - 1 - 2 * z)


def ring_index(place, n):
    place = lax.rem(place + 2 * n, n)
    if n != 8:
        return place
    back = place // (n // 2)
    return 2 * place + back * (2 * n - 1 - 4 * place)


def gelu_and_slope(v):
    scale = math.sqrt(2.0 / math.pi)
    square = v * v
    th = jnp.tanh(scale * (v + 0.044715 * square * v))
    up = 0.5 * (1.0 + th)
    slope = up + 0.5 * v * (1.0 - th * th) * (scale * (1.0 + 3.0 * 0.044715 * square))
    return v * up, slope


def ring_kernel(
    n, x_ref, y_ref, enc_ref, dec_ref, out_ref, slots, term, mine,
    rs_send, rs_recv, ag_send, ag_recv, local_sem,
):
    me = lax.axis_index("seq")
    place = ring_place(me, n)
    nexts = (ring_index(place + 1, n), ring_index(place - 1, n))
    half = x_ref.shape[1]
    share = enc_ref.shape[1]
    side = half // 2
    piece = side // PIECES

    barrier = pltpu.get_barrier_semaphore()
    for other in nexts:
        pl.semaphore_signal(
            barrier, inc=1, device_id={"seq": other}, device_id_type=pl.DeviceIdType.MESH
        )
    pl.semaphore_wait(barrier, 2)

    def signed(d, steps):
        return place - steps if d == 0 else place + steps

    def own_term(d, steps):
        chunk = ring_index(signed(d, steps), n)
        at = pl.ds(d * side, side)
        a = jnp.dot(x_ref[chunk, at, :], enc_ref[...], preferred_element_type=jnp.float32)
        b = jnp.dot(y_ref[chunk, at, :], dec_ref[...], preferred_element_type=jnp.float32)
        return a, b

    def rs_copy(d, s, q):
        at = pl.ds(q * piece, piece)
        return pltpu.make_async_remote_copy(
            src_ref=slots.at[d, s, at],
            dst_ref=slots.at[d, s + 1, at],
            send_sem=rs_send.at[d, s, q],
            recv_sem=rs_recv.at[d, s, q],
            device_id={"seq": nexts[d]},
            device_id_type=pl.DeviceIdType.MESH,
        )

    def ag_copy(d, s, q, first):
        at = pl.ds(d * side + q * piece, piece)
        owner = ring_index(signed(d, s), n)
        return pltpu.make_async_remote_copy(
            src_ref=mine.at[at] if first else out_ref.at[owner, at],
            dst_ref=out_ref.at[owner, at],
            send_sem=ag_send.at[d, s, q],
            recv_sem=ag_recv.at[d, s, q],
            device_id={"seq": nexts[d]},
            device_id_type=pl.DeviceIdType.MESH,
        )

    for d in range(2):
        a, b = own_term(d, 1)
        slots[d, 0, :, :share] = a.astype(BF16)
        slots[d, 0, :, share:] = b.astype(BF16)
        for q in range(PIECES):
            rs_copy(d, 0, q).start()

    def fill(s):
        for d in range(2):
            a, b = own_term(d, s + 2)
            term[d, :, :share] = a
            term[d, :, share:] = b

    def rs_step(s, carry):
        fill(s)
        for q in range(PIECES):
            at = pl.ds(q * piece, piece)
            for d in range(2):
                rs_copy(d, s, q).wait_recv()
                total = slots[d, s + 1, at, :].astype(F32) + term[d, at, :]
                slots[d, s + 1, at, :] = total.astype(BF16)
                rs_copy(d, s + 1, q).start()
        return carry

    lax.fori_loop(0, n - 2, rs_step, 0)
    fill(n - 2)
    for q in range(PIECES):
        at = pl.ds(q * piece, piece)
        for d in range(2):
            rs_copy(d, n - 2, q).wait_recv()
            rows = pl.ds(d * side + q * piece, piece)
            pre = slots[d, n - 1, at, :share].astype(F32) + term[d, at, :share]
            grad = slots[d, n - 1, at, share:].astype(F32) + term[d, at, share:]
            value, slope = gelu_and_slope(pre)
            mine[rows, :share] = value.astype(BF16)
            mine[rows, share:] = (grad * slope).astype(BF16)
            ag_copy(d, 0, q, True).start()
    local = pltpu.make_async_copy(mine, out_ref.at[me], local_sem)
    local.start()

    def ag_step(s, carry):
        for q in range(PIECES):
            for d in range(2):
                incoming(d, s, q).wait_recv()
                ag_copy(d, s + 1, q, False).start()
        return carry

    def incoming(d, s, q):
        at = pl.ds(d * side + q * piece, piece)
        owner = ring_index(signed(d, s + 1), n)
        return pltpu.make_async_remote_copy(
            src_ref=mine.at[at],
            dst_ref=out_ref.at[owner, at],
            send_sem=ag_send.at[d, s, q],
            recv_sem=ag_recv.at[d, s, q],
            device_id={"seq": nexts[d]},
            device_id_type=pl.DeviceIdType.MESH,
        )

    lax.fori_loop(0, n - 2, ag_step, 0)
    for q in range(PIECES):
        for d in range(2):
            incoming(d, n - 2, q).wait_recv()

    def drain(s, carry):
        for q in range(PIECES):
            for d in range(2):
                rs_copy(d, s, q).wait_send()
                ag_copy(d, s, q, True).wait_send()
        return carry

    lax.fori_loop(0, n - 1, drain, 0)
    local.wait()


def ring(pool_taps, cot_taps, enc_mat, dec_mat, n):
    half = pool_taps.shape[1]
    share = enc_mat.shape[1]
    depth = enc_mat.shape[0]
    vmem = pl.BlockSpec(memory_space=pltpu.VMEM)
    steps = (2, n - 1, PIECES)
    return pl.pallas_call(
        functools.partial(ring_kernel, n),
        out_shape=jax.ShapeDtypeStruct((n, half, 2 * share), BF16),
        in_specs=[vmem] * 4,
        out_specs=pl.BlockSpec(memory_space=pl.ANY),
        scratch_shapes=[
            pltpu.VMEM((2, n, half // 2, 2 * share), BF16),
            pltpu.VMEM((2, half // 2, 2 * share), F32),
            pltpu.VMEM((half, 2 * share), BF16),
            pltpu.SemaphoreType.DMA(steps),
            pltpu.SemaphoreType.DMA(steps),
            pltpu.SemaphoreType.DMA(steps),
            pltpu.SemaphoreType.DMA(steps),
            pltpu.SemaphoreType.DMA,
        ],
        compiler_params=pltpu.CompilerParams(
            collective_id=0, has_side_effects=True, vmem_limit_bytes=48 * 2**20
        ),
        cost_estimate=pl.CostEstimate(
            flops=4 * n * half * depth * share,
            bytes_accessed=4 * n * half * share * 2,
            transcendentals=half * share,
        ),
    )(pool_taps, cot_taps, enc_mat, dec_mat)


def wide_shards(inputs, enc_weight, dec_weight, cotangent):
    parts = lax.axis_size("seq")
    rows, width = inputs.shape
    half = rows // 2
    total = half * parts
    block, taps, share = enc_weight.shape
    half_width = cotangent.shape[1]

    pooled = (inputs.astype(F32).reshape(half, 2, width).sum(axis=1) * 0.5).astype(BF16)
    cot_full = lax.all_gather(cotangent, "chan", axis=1, tiled=True)
    core = lax.axis_index("chan")
    cores = lax.axis_size("chan")
    few = half // cores
    leaving = jnp.concatenate(
        [
            lax.dynamic_slice_in_dim(pooled, core * few, few, 0),
            lax.dynamic_slice_in_dim(cot_full, core * 2 * few, 2 * few, 0),
        ],
        axis=0,
    )
    columns = to_columns(leaving, parts).reshape(parts, 1, 3 * few, block)
    columns = lax.all_gather(columns, "chan", axis=1, tiled=True)
    pool_col = columns[:, :, :few].reshape(total, block)
    cot_col = columns[:, :, few:].reshape(total, 2, block).astype(F32)
    even = cot_col[:, 0]
    odd = cot_col[:, 1]
    pair = (even + odd).astype(BF16)
    cross = (odd + shift(even, 1)).astype(BF16)
    before = jnp.concatenate([even[:1].astype(BF16), cross[:-1]], axis=0)
    pool_taps = jnp.concatenate([shift(pool_col, t - 2) for t in range(taps)], axis=1)
    cot_taps = jnp.concatenate([shift(pair, 1), cross, pair, before, shift(pair, -1)], axis=1)
    enc_mat = enc_weight.transpose(1, 0, 2).reshape(taps * block, share)
    dec_mat = dec_weight.transpose(1, 0, 2).reshape(taps * block, share)

    joint = ring(
        pool_taps.reshape(parts, half, taps * block),
        cot_taps.reshape(parts, half, taps * block),
        enc_mat,
        dec_mat,
        parts,
    ).reshape(total, 2 * share)
    hidden_all = joint[:, :share]
    grad_all = joint[:, share:]

    contract_rows = (((0,), (0,)), ((), ()))
    contract_last = (((1,), (1,)), ((), ()))
    dec_grad = lax.dot_general(cot_taps, hidden_all, contract_rows, preferred_element_type=F32)
    enc_grad = lax.dot_general(pool_taps, grad_all, contract_rows, preferred_element_type=F32)
    dec_grad = dec_grad.astype(BF16).reshape(taps, block, share).transpose(1, 0, 2)
    enc_grad = enc_grad.astype(BF16).reshape(taps, block, share).transpose(1, 0, 2)

    dec_out = lax.dot_general(hidden_all, dec_mat, contract_last, preferred_element_type=F32)
    p0, p1, p2, p3, p4 = [dec_out[:, t * block : (t + 1) * block] for t in range(taps)]
    after4 = shift(p4, 1)
    before0 = shift(p0, -1)
    dec_even = before0 + shift(p1, -1) + p2 + p3 + after4
    dec_odd = before0 + p1 + p2 + shift(p3, 1) + after4
    decoded = jnp.stack([dec_even, dec_odd], axis=1).astype(BF16).reshape(parts, rows, block)
    enc_out = lax.dot_general(grad_all, enc_mat, contract_last, preferred_element_type=F32)
    pool_grad = sum(shift(enc_out[:, t * block : (t + 1) * block], 2 - t) for t in range(taps))
    pool_grad = pool_grad.astype(BF16).reshape(parts, half, block)
    mine = jnp.concatenate([decoded, pool_grad], axis=1)
    mine = lax.psum_scatter(mine, "chan", scatter_dimension=1, tiled=True)
    mine = lax.all_gather(to_rows(mine), "chan", axis=0, tiled=True)
    col_start = core * half_width
    mine = lax.dynamic_slice_in_dim(mine, col_start, half_width, 1).astype(F32)

    skip = lax.dynamic_slice_in_dim(inputs, col_start, half_width, 1)
    mixed_out = (skip.astype(F32) + mine[:rows]).astype(BF16)
    input_grad = (cotangent.astype(F32) + 0.5 * jnp.repeat(mine[rows:], 2, axis=0)).astype(BF16)
    return mixed_out, input_grad, enc_grad, dec_grad


LANES = 128
HALO = 16
EDGE = 8


def pair_kernel(
    x_ref, enc_ref, dec_ref, cot_ref, mixed_ref, in_grad_ref, enc_grad_ref, dec_grad_ref,
    x_own, spread, pc_ref, rows_all, weights, folded, z_enc, z_dec, hid, slope, pre_grad, g_taps, h_taps,
    enc_sum, dec_sum, part, give, take, give_y, take_y, grad_give,
    local_sem, wy_send, wy_recv, wz_send, wz_recv, wx_send, wx_recv,
    edge_send, edge_z, edge_y, edge_c, edge_fwd, edge_ysend, edge_csend,
    own_send, pz_send, pz_recv, py_send, py_recv, pc_send, pc_recv,
    give_sem, take_sem, grad_sem,
):
    g = lax.axis_index("groups")
    s = lax.axis_index("seq")
    c = lax.axis_index("chan")
    z, y = s // 2, lax.rem(s, 2)
    last = lax.axis_size("seq") // 2 - 1
    chunk, wide = pc_ref.shape[1], pc_ref.shape[2]
    cell = 2 * chunk
    taps, block = enc_ref.shape[0], enc_ref.shape[1]
    share = enc_ref.shape[2] // 2
    half = block // 2
    inner = chunk - HALO
    ids = pl.DeviceIdType.MESH
    to_y, to_x, to_c = {"seq": s + 1 - 2 * y}, {"groups": 1 - g}, {"chan": 1 - c}
    to_left, to_right = {"seq": s - 2}, {"seq": s + 2}
    has_left, has_right = z > 0, z < last

    def lanes(index, width):
        return pl.ds(pl.multiple_of(index * width, LANES), width)

    own_x = pltpu.make_async_copy(x_ref.at[:, lanes(c, wide)], x_own, local_sem.at[0, taps + 1])
    own_x.start()
    sources = (enc_ref, dec_ref)
    grad_refs = (enc_grad_ref, dec_grad_ref)

    def own_weight(w, t):
        return pltpu.make_async_copy(
            sources[w].at[t, :, lanes(y, share)],
            weights.at[w, pl.ds(pl.multiple_of(s * block, HALO), block), pl.ds(t * share, share)],
            local_sem.at[w, t],
        )

    for w in range(2):
        for t in range(taps):
            own_weight(w, t).start()

    barrier = pltpu.get_barrier_semaphore()
    for where in (to_y, to_x, to_c):
        pl.semaphore_signal(barrier, inc=1, device_id=where, device_id_type=ids)

    @pl.when(has_left)
    def _():
        pl.semaphore_signal(barrier, inc=1, device_id=to_left, device_id_type=ids)

    @pl.when(has_right)
    def _():
        pl.semaphore_signal(barrier, inc=1, device_id=to_right, device_id_type=ids)

    inside = jnp.where(has_left, 1, 0) + jnp.where(has_right, 1, 0)
    pl.semaphore_wait(barrier, 3 + inside)

    def remote(src, dst, send, recv, where):
        return pltpu.make_async_remote_copy(
            src_ref=src, dst_ref=dst, send_sem=send, recv_sem=recv,
            device_id=where, device_id_type=ids,
        )

    def weight_to_y(w, t, side):
        at = pl.ds(pl.multiple_of(side * half, HALO), half)
        row = pl.multiple_of(s * block + side * half, HALO)
        return remote(
            sources[w].at[t, at, lanes(1 - y, share)],
            weights.at[w, pl.ds(row, half), pl.ds(t * share, share)],
            wy_send.at[w, t, side], wy_recv.at[w, t, side], to_y,
        )

    def slab(w, b, side):
        return weights.at[w, pl.ds(pl.multiple_of(b * block + side * half, HALO), half), :]

    def weight_z(w, zz, b, d, where):
        ref = slab(w, 2 * zz + b, g)
        return remote(ref, ref, wz_send.at[d, w, zz, b], wz_recv.at[w, zz, b], where)

    def weight_x(w, zz, b, side):
        ref = slab(w, 2 * zz + b, side)
        return remote(ref, ref, wx_send.at[w, zz, b], wx_recv.at[w, zz, b], to_x)

    def edge_of(zz, yy, cc):
        at = pl.multiple_of(HALO + (2 * zz + yy) * chunk + yy * inner, HALO)
        return rows_all.at[:, pl.ds(at, HALO), lanes(cc, wide)]

    def inner_of(i, zz, yy, cc):
        at = pl.multiple_of(HALO + (2 * zz + yy) * chunk + (1 - yy) * HALO, HALO)
        return rows_all.at[i, pl.ds(at, inner), lanes(cc, wide)]

    own_edge = pc_ref.at[:, pl.ds(pl.multiple_of(y * inner, HALO), HALO), :]

    def own_inner(i):
        return pc_ref.at[i, pl.ds(pl.multiple_of((1 - y) * HALO, HALO), inner), :]

    local_edge = pltpu.make_async_copy(own_edge, edge_of(z, y, c), local_sem.at[0, taps])
    local_inner = [
        pltpu.make_async_copy(own_inner(i), inner_of(i, z, y, c), local_sem.at[1, taps + i])
        for i in range(3)
    ]

    for w in range(2):
        for t in range(taps):
            weight_to_y(w, t, g).start()

    for w in range(2):
        for t in range(taps):
            own_weight(w, t).wait()

        @pl.when(has_left)
        def _():
            weight_z(w, z, y, 0, to_left).start()

        @pl.when(has_right)
        def _():
            weight_z(w, z, y, 1, to_right).start()

    def edge_out(d, where):
        return remote(own_edge, edge_of(z, y, c), edge_send.at[d], edge_z.at[z], where)

    def edge_forward(zz, where):
        ref = edge_of(zz, y, c)
        return remote(ref, ref, edge_fwd.at[zz], edge_z.at[zz], where)

    def edge_to_y(zz):
        src = edge_of(zz, y, c)
        return remote(src, src, edge_ysend.at[zz], edge_y.at[zz], to_y)

    def edge_to_c(zz, yy):
        ref = edge_of(zz, yy, c)
        return remote(ref, ref, edge_csend.at[zz, yy], edge_c.at[zz, yy], to_c)

    tiles = wide // LANES
    own_x.wait()
    for k in range(tiles):
        cols = slice(k * LANES, (k + 1) * LANES)
        spread[k] = x_own[:, cols].astype(F32)
        spread[tiles + k] = cot_ref[:, cols].astype(F32)
    for k in range(tiles):
        cols = slice(k * LANES, (k + 1) * LANES)
        even, odd = pl.ds(0, chunk, stride=2), pl.ds(1, chunk, stride=2)
        pc_ref[0, :, cols] = ((spread[k, even, :] + spread[k, odd, :]) * 0.5).astype(BF16)
        pc_ref[1, :, cols] = spread[tiles + k, even, :].astype(BF16)
        pc_ref[2, :, cols] = spread[tiles + k, odd, :].astype(BF16)

    local_edge.start()

    @pl.when(has_left)
    def _():
        edge_out(0, to_left).start()

    @pl.when(has_right)
    def _():
        edge_out(1, to_right).start()

    for copy in local_inner:
        copy.start()
    rows_all[:, :HALO, :] = jnp.zeros((3, HALO, 2 * wide), BF16)
    bottom = rows_all.shape[1] - HALO
    rows_all[:, bottom:, :] = jnp.zeros((3, HALO, 2 * wide), BF16)
    local_edge.wait()
    edge_to_y(z).start()
    edge_to_c(z, y).start()

    for w in range(2):
        for t in range(taps):
            weight_from_y(
                weights, sources, wy_send, wy_recv, w, t, g, s, y, half, block, share, to_y, lanes
            ).wait_recv()

        @pl.when(has_left)
        def _():
            weight_z(w, z, 1 - y, 0, to_left).start()

        @pl.when(has_right)
        def _():
            weight_z(w, z, 1 - y, 1, to_right).start()

    for w in range(2):
        for t in range(taps):
            weight_to_y(w, t, 1 - g).start()

    def inner_to_y(i, zz):
        ref = inner_of(i, zz, y, c)
        return remote(ref, ref, py_send.at[zz, i], py_recv.at[zz, i], to_y)

    def inner_to_c(i, zz, yy):
        ref = inner_of(i, zz, yy, c)
        return remote(ref, ref, pc_send.at[zz, yy, i], pc_recv.at[zz, yy, i], to_c)

    def inner_out(i, d, where):
        return remote(own_inner(i), inner_of(i, z, y, c), own_send.at[d, i], pz_recv.at[z, i], where)

    for i in range(3):
        local_inner[i].wait()
        inner_to_y(i, z).start()
        inner_to_c(i, z, y).start()

    def order(k):
        low = jnp.minimum(z, last - z)
        near = jnp.where(low == 0, k, jnp.where(k < 2, 1 - k, k))
        return jnp.where(z * 2 < last, near, last - near)

    def edge_arrives_y(zz):
        ref = edge_of(zz, 1 - y, c)
        return remote(ref, ref, edge_ysend.at[zz], edge_y.at[zz], to_y)

    def send_own_rows(d, where):
        for i in range(3):
            inner_out(i, d, where).start()

    @pl.when(z == 0)
    def _():
        send_own_rows(1, to_right)

    @pl.when(z == last)
    def _():
        send_own_rows(0, to_left)

    def weight_step(k, carry):
        for sign in (-1, 1):
            zz = z + sign * k

            @pl.when((zz >= 0) & (zz <= last))
            def _():
                for w in range(2):
                    for b in range(2):
                        weight_z(w, zz, b, 0, to_y).wait_recv()

                        if sign < 0:
                            @pl.when(has_right)
                            def _():
                                weight_z(w, zz, b, 1, to_right).start()
                        else:
                            @pl.when(has_left)
                            def _():
                                weight_z(w, zz, b, 0, to_left).start()

                        weight_x(w, zz, b, g).start()

                edge_forward(zz, to_y).wait_recv()
                if sign < 0:
                    @pl.when(has_right)
                    def _():
                        edge_forward(zz, to_right).start()
                else:
                    @pl.when(has_left)
                    def _():
                        edge_forward(zz, to_left).start()

                edge_to_y(zz).start()
                edge_to_c(zz, y).start()

        @pl.when((z == k) & has_right)
        def _():
            send_own_rows(1, to_right)

        @pl.when((last - z == k) & has_left)
        def _():
            send_own_rows(0, to_left)

        return carry

    lax.fori_loop(1, last + 1, weight_step, 0)

    def inner_forward(i, zz, where):
        ref = inner_of(i, zz, y, c)
        return remote(ref, ref, pz_send.at[zz, i], pz_recv.at[zz, i], where)

    def receive(i, zz):
        inner_forward(i, zz, to_y).wait_recv()

        @pl.when((zz < z) & has_right)
        def _():
            inner_forward(i, zz, to_right).start()

        @pl.when((zz > z) & has_left)
        def _():
            inner_forward(i, zz, to_left).start()

        inner_to_y(i, zz).start()
        inner_to_c(i, zz, y).start()

    ahead = 1 + jnp.where(has_left & has_right, 1, 0)

    def receive_step(k, carry):
        for i in range(3):
            receive(i, order(k))
        return carry

    lax.fori_loop(1, 1 + ahead, receive_step, 0)

    def edge_end(zz, carry):
        edge_arrives_y(zz).wait_recv()
        edge_to_c(zz, 1 - y).start()
        return carry

    lax.fori_loop(0, last + 1, edge_end, 0)
    for zz in range(last + 1):
        for yy in range(2):
            ref = edge_of(zz, yy, 1 - c)
            remote(ref, ref, edge_csend.at[zz, yy], edge_c.at[zz, yy], to_c).wait_recv()

    def each_other_cell(body):
        def step(k, carry):
            body(order(k))
            return carry

        lax.fori_loop(1, last + 1, step, 0)

    for w in range(2):
        for t in range(taps):
            weight_from_y(
                weights, sources, wy_send, wy_recv, w, t, 1 - g, s, y, half, block, share, to_y, lanes
            ).wait_recv()

    def wait_x(zz):
        for w in range(2):
            for b in range(2):
                weight_x(w, zz, b, 1 - g).wait_recv()

    each_other_cell(wait_x)

    step_rows = 64

    def fold(i, carry):
        at = pl.ds(pl.multiple_of(i * step_rows, HALO), step_rows)
        w = [weights[1, at, t * share : (t + 1) * share].astype(F32) for t in range(5)]
        folded[0, at, :share] = (w[0] + w[1]).astype(BF16)
        folded[0, at, share : 2 * share] = (w[2] + w[3]).astype(BF16)
        folded[0, at, 2 * share :] = weights[1, at, 4 * share :]
        folded[1, at, :share] = weights[1, at, :share]
        folded[1, at, share : 2 * share] = (w[1] + w[2]).astype(BF16)
        folded[1, at, 2 * share :] = (w[3] + w[4]).astype(BF16)
        return carry

    lax.fori_loop(0, weights.shape[1] // step_rows, fold, 0)

    contract_rows = (((0,), (0,)), ((), ()))
    contract_last = (((1,), (1,)), ((), ()))
    wide_rows = cell + 2 * HALO
    mid_rows = cell + 2 * EDGE
    window = pl.ds(pl.multiple_of((2 * block * z) // LANES * LANES, LANES), 2 * LANES)
    offset = 2 * block * z - (2 * block * z) // LANES * LANES

    enc_sum[...] = jnp.zeros_like(enc_sum)
    dec_sum[...] = jnp.zeros_like(dec_sum)

    def sums_over_cores():
        for i in range(3):
            total = part[i] + take[i].astype(F32)
            part[i] = total
            rows = pl.ds(pl.multiple_of((1 - y) * chunk, HALO), chunk)
            give_y[i] = part[i, rows, :].astype(BF16)

    give_copy = remote(give, take, give_sem.at[0], take_sem.at[0], to_c)
    give_y_copy = remote(give_y, take_y, give_sem.at[1], take_sem.at[1], to_y)

    def grad_copy(w):
        return remote(
            grad_give.at[w], grad_refs[w].at[:, :, lanes(y, share)], grad_sem.at[0, w], grad_sem.at[1, w], to_y
        )

    def grads(w, who):
        at = pl.ds(pl.multiple_of(offset + who * block, HALO), block)
        if w == 0:
            return [enc_sum[at, t * share : (t + 1) * share].astype(BF16) for t in range(5)]
        e = [dec_sum[0, at, k * share : (k + 1) * share] for k in range(3)]
        o = [dec_sum[1, at, k * share : (k + 1) * share] for k in range(3)]
        both = (e[0] + o[0], e[0] + o[1], e[1] + o[1], e[1] + o[2], e[2] + o[2])
        return [v.astype(BF16) for v in both]

    def give_grads(w):
        for t, value in enumerate(grads(w, 1 - y)):
            grad_give[w, t] = value
        grad_copy(w).start()

    def cell_step(k, carry):
        zz = order(k)

        def receive_ahead(i):
            @pl.when(k + ahead + 1 <= last)
            def _():
                receive(i, order(k + ahead + 1))

        for i in range(3):
            ref = inner_of(i, zz, 1 - y, c)
            remote(ref, ref, py_send.at[zz, i], py_recv.at[zz, i], to_y).wait_recv()
            inner_to_c(i, zz, 1 - y).start()
        for yy in range(2):
            for i in range(3):
                ref = inner_of(i, zz, yy, 1 - c)
                remote(ref, ref, pc_send.at[zz, yy, i], pc_recv.at[zz, yy, i], to_c).wait_recv()

        base = pl.multiple_of(zz * cell, HALO)
        at = pl.ds(base, wide_rows)
        product = jnp.dot(rows_all[0, at, :], weights[0], preferred_element_type=F32)
        for t in range(5 * tiles):
            z_enc[t] = product[:, t * LANES : (t + 1) * LANES]
        receive_ahead(0)

        piece = mid_rows // 6
        product = jnp.dot(
            rows_all[1, at, :], folded[0], preferred_element_type=F32
        ) + jnp.dot(rows_all[2, at, :], folded[1], preferred_element_type=F32)
        for r in range(6):
            start = r * piece
            for q in range(tiles):
                pre = z_enc[q, pl.ds(start + 6, piece), :]
                for t in range(1, 5):
                    pre += z_enc[t * tiles + q, pl.ds(start + 6 + t, piece), :]
                value, up = gelu_and_slope(pre)
                row = lax.broadcasted_iota(jnp.int32, (piece, LANES), 0)
                if r == 0:
                    keep = (row >= EDGE) | (zz > 0)
                    value, up = jnp.where(keep, value, 0.0), jnp.where(keep, up, 0.0)
                if r == 5:
                    keep = (row < piece - EDGE) | (zz < last)
                    value, up = jnp.where(keep, value, 0.0), jnp.where(keep, up, 0.0)
                hid[q, pl.ds(start, piece), :] = value
                slope[q, pl.ds(start, piece), :] = up
        for r in range(cell // LANES):
            for q in range(tiles):
                for t in range(3):
                    moved = hid[q, pl.ds(r * LANES + EDGE - 1 + t, LANES), :]
                    h_taps[r * LANES : (r + 1) * LANES, t * share + q * LANES : t * share + (q + 1) * LANES] = (
                        moved.astype(BF16)
                    )
        for t in range(3 * tiles):
            z_dec[t] = product[:, t * LANES : (t + 1) * LANES]
        receive_ahead(1)

        body = pl.ds(base + HALO, cell)
        for i in range(2):
            dec_sum[i] += lax.dot_general(
                rows_all[1 + i, body, window], h_taps[...], contract_rows,
                preferred_element_type=F32,
            )
        for r in range(6):
            start = r * piece
            for q in range(tiles):
                grad = z_dec[q, pl.ds(start + 9, piece), :]
                for t in range(1, 3):
                    grad += z_dec[t * tiles + q, pl.ds(start + 9 - t, piece), :]
                pre_grad[q, pl.ds(start, piece), :] = grad * slope[q, pl.ds(start, piece), :]
        for r in range(cell // LANES):
            for q in range(tiles):
                for t in range(5):
                    moved = pre_grad[q, pl.ds(r * LANES + EDGE + 2 - t, LANES), :]
                    g_taps[r * LANES : (r + 1) * LANES, t * share + q * LANES : t * share + (q + 1) * LANES] = (
                        moved.astype(BF16)
                    )
        receive_ahead(2)

        @pl.when(k == last)
        def _():
            give_grads(1)

        enc_sum[...] += lax.dot_general(
            rows_all[0, body, window], g_taps[...], contract_rows, preferred_element_type=F32
        )

        @pl.when(k == 0)
        def _():
            for i in range(3):
                for h in range(2):
                    cols = pl.ds(pl.multiple_of((c if h == 0 else 1 - c) * wide, LANES), wide)
                    rhs = weights[0, cols, :] if i == 0 else folded[i - 1, cols, :]
                    lhs = g_taps[...] if i == 0 else h_taps[...]
                    value = lax.dot_general(lhs, rhs, contract_last, preferred_element_type=F32)
                    if h == 0:
                        part[i] = value
                    else:
                        give[i] = value.astype(BF16)
            give_copy.start()

        @pl.when(k == last - 1)
        def _():
            give_copy.wait_recv()
            sums_over_cores()
            give_y_copy.start()

        return carry

    lax.fori_loop(0, last + 1, cell_step, 0)

    give_grads(0)
    for w in range(2):
        for t, value in enumerate(grads(w, y)):
            grad_refs[w][t, :, lanes(y, share)] = value

    give_y_copy.wait_recv()
    for k in range(tiles):
        cols = slice(k * LANES, (k + 1) * LANES)
        even, odd = pl.ds(0, chunk, stride=2), pl.ds(1, chunk, stride=2)
        own = pl.ds(pl.multiple_of(y * chunk, HALO), chunk)
        pool_grad, first, second = [part[i, own, cols] + take_y[i, :, cols].astype(F32) for i in range(3)]
        spread[k, even, :] = first
        spread[k, odd, :] = second
        spread[tiles + k, even, :] = pool_grad
        spread[tiles + k, odd, :] = pool_grad
        mixed_ref[:, cols] = (x_own[:, cols].astype(F32) + spread[k]).astype(BF16)
        in_grad_ref[:, cols] = (cot_ref[:, cols].astype(F32) + 0.5 * spread[tiles + k]).astype(BF16)

    give_copy.wait_send()
    give_y_copy.wait_send()
    for w in range(2):
        for t in range(taps):
            weight_to_y(w, t, g).wait_send()
            weight_to_y(w, t, 1 - g).wait_send()

    @pl.when(has_left)
    def _():
        edge_out(0, to_left).wait_send()
        for i in range(3):
            inner_out(i, 0, to_left).wait_send()
        for w in range(2):
            for b in range(2):
                weight_z(w, z, b, 0, to_left).wait_send()

    @pl.when(has_right)
    def _():
        edge_out(1, to_right).wait_send()
        for i in range(3):
            inner_out(i, 1, to_right).wait_send()
        for w in range(2):
            for b in range(2):
                weight_z(w, z, b, 1, to_right).wait_send()

    def drain(k, carry):
        zz = order(k)
        edge_to_y(zz).wait_send()
        for yy in range(2):
            edge_to_c(zz, yy).wait_send()
        for i in range(3):
            inner_to_y(i, zz).wait_send()
            for yy in range(2):
                inner_to_c(i, zz, yy).wait_send()

        @pl.when(k > 0)
        def _():
            for w in range(2):
                for b in range(2):
                    weight_x(w, zz, b, g).wait_send()

        @pl.when((zz < z) & has_right)
        def _():
            edge_forward(zz, to_right).wait_send()
            for i in range(3):
                inner_forward(i, zz, to_right).wait_send()
            for w in range(2):
                for b in range(2):
                    weight_z(w, zz, b, 1, to_right).wait_send()

        @pl.when((zz > z) & has_left)
        def _():
            edge_forward(zz, to_left).wait_send()
            for i in range(3):
                inner_forward(i, zz, to_left).wait_send()
            for w in range(2):
                for b in range(2):
                    weight_z(w, zz, b, 0, to_left).wait_send()

        return carry

    lax.fori_loop(0, last + 1, drain, 0)
    for w in range(2):
        grad_copy(w).wait_send()
    for w in range(2):
        grad_arrives = remote(
            grad_give.at[w], grad_refs[w].at[:, :, lanes(1 - y, share)],
            grad_sem.at[0, w], grad_sem.at[1, w], to_y,
        )
        grad_arrives.wait_recv()


def weight_from_y(weights, sources, send, recv, w, t, side, s, y, half, block, share, to_y, lanes):
    other = s + 1 - 2 * y
    row = pl.multiple_of(other * block + side * half, HALO)
    return pltpu.make_async_remote_copy(
        src_ref=sources[w].at[t, pl.ds(pl.multiple_of(side * half, HALO), half), lanes(1 - y, share)],
        dst_ref=weights.at[w, pl.ds(row, half), pl.ds(t * share, share)],
        send_sem=send.at[w, t, side],
        recv_sem=recv.at[w, t, side],
        device_id=to_y,
        device_id_type=pl.DeviceIdType.MESH,
    )


def pair_call(inputs, enc_taps, dec_taps, cotangent, cells):
    rows, wide = cotangent.shape
    chunk = rows // 2
    taps, block, both = enc_taps.shape
    share = both // 2
    cell = 2 * chunk
    vmem = pl.BlockSpec(memory_space=pltpu.VMEM)
    anywhere = pl.BlockSpec(memory_space=pl.ANY)
    dma = pltpu.SemaphoreType.DMA
    tall = cells * cell + 2 * HALO
    width = 2 * wide
    return pl.pallas_call(
        pair_kernel,
        out_shape=[
            jax.ShapeDtypeStruct((rows, wide), BF16),
            jax.ShapeDtypeStruct((rows, wide), BF16),
            jax.ShapeDtypeStruct((taps, block, both), BF16),
            jax.ShapeDtypeStruct((taps, block, both), BF16),
        ],
        in_specs=[anywhere, anywhere, anywhere, vmem],
        out_specs=[vmem] * 4,
        scratch_shapes=[
            pltpu.VMEM((rows, wide), BF16),
            pltpu.VMEM((2 * (wide // LANES), rows, LANES), F32),
            pltpu.VMEM((3, chunk, wide), BF16),
            pltpu.VMEM((3, tall, width), BF16),
            pltpu.VMEM((2, width, taps * share), BF16),
            pltpu.VMEM((2, width, 3 * share), BF16),
            pltpu.VMEM((taps * share // LANES, cell + 2 * HALO, LANES), F32),
            pltpu.VMEM((3 * share // LANES, cell + 2 * HALO, LANES), F32),
            pltpu.VMEM((share // LANES, cell + 2 * EDGE, LANES), F32),
            pltpu.VMEM((share // LANES, cell + 2 * EDGE, LANES), F32),
            pltpu.VMEM((share // LANES, cell + 2 * EDGE, LANES), F32),
            pltpu.VMEM((cell, taps * share), BF16),
            pltpu.VMEM((cell, 3 * share), BF16),
            pltpu.VMEM((2 * LANES, taps * share), F32),
            pltpu.VMEM((2, 2 * LANES, 3 * share), F32),
            pltpu.VMEM((3, cell, wide), F32),
            pltpu.VMEM((3, cell, wide), BF16),
            pltpu.VMEM((3, cell, wide), BF16),
            pltpu.VMEM((3, chunk, wide), BF16),
            pltpu.VMEM((3, chunk, wide), BF16),
            pltpu.VMEM((2, taps, block, share), BF16),
            dma((2, taps + 3)),
            dma((2, taps, 2)), dma((2, taps, 2)),
            dma((2, 2, cells, 2)), dma((2, cells, 2)), dma((2, cells, 2)), dma((2, cells, 2)),
            dma((2,)), dma((cells,)), dma((cells,)), dma((cells, 2)), dma((cells,)), dma((cells,)),
            dma((cells, 2)),
            dma((2, 3)), dma((cells, 3)), dma((cells, 3)), dma((cells, 3)), dma((cells, 3)),
            dma((cells, 2, 3)), dma((cells, 2, 3)),
            dma((2,)), dma((2,)), dma((2, 2)),
        ],
        compiler_params=pltpu.CompilerParams(
            collective_id=0, has_side_effects=True, vmem_limit_bytes=58 * 2**20
        ),
        cost_estimate=pl.CostEstimate(
            flops=2 * 11 * cells * cell * width * share + 4 * 11 * cells * cell * block * share,
            bytes_accessed=4 * taps * block * both * 2,
            transcendentals=cells * cell * share,
        ),
    )(inputs, enc_taps, dec_taps, cotangent)


def shards(inputs, enc_weight, dec_weight, cotangent):
    parts = lax.axis_size("seq")
    cores = lax.axis_size("chan")
    rows, width = inputs.shape
    chunk = rows // 2
    block, taps, share = enc_weight.shape
    wide = cotangent.shape[1]
    fits = parts == 8 and cores == 2 and lax.axis_size("groups") == 2 and taps == 5
    fits = fits and block == 96 and share == 2 * wide and wide % LANES == 0 and chunk == 256
    if not fits:
        return wide_shards(inputs, enc_weight, dec_weight, cotangent)
    mixed_out, input_grad, enc_grad, dec_grad = pair_call(
        inputs, enc_weight.transpose(1, 0, 2), dec_weight.transpose(1, 0, 2), cotangent, parts // 2
    )
    return mixed_out, input_grad, enc_grad.transpose(1, 0, 2), dec_grad.transpose(1, 0, 2)


def solution(mesh):
    return jax.shard_map(
        shards,
        mesh=mesh,
        in_specs=(
            P(("groups", "seq"), None),
            P("seq", None, "chan"),
            P("seq", None, "chan"),
            P(("groups", "seq"), "chan"),
        ),
        out_specs=(
            P(("groups", "seq"), "chan"),
            P(("groups", "seq"), "chan"),
            P(("groups", "seq"), None, "chan"),
            P(("groups", "seq"), None, "chan"),
        ),
        check_vma=False,
    )
```

```python
import functools
import math

import jax
import jax.numpy as jnp
from jax import lax
from jax.experimental import pallas as pl
from jax.experimental.pallas import tpu as pltpu
from jax.sharding import PartitionSpec as P

BF16 = jnp.bfloat16
F32 = jnp.float32


def shift(array, by):
    length = array.shape[0]
    if by == 0:
        return array
    pad = jnp.zeros((abs(by),) + array.shape[1:], array.dtype)
    if by > 0:
        return jnp.concatenate([array[by:], pad], axis=0)
    return jnp.concatenate([pad, array[: length + by]], axis=0)


def to_columns(array, parts):
    rows, cols = array.shape
    blocks = array.reshape(rows, parts, cols // parts).transpose(1, 0, 2)
    return lax.all_to_all(blocks, "seq", 0, 0, tiled=True)


def to_rows(blocks):
    parts, rows, cols = blocks.shape
    got = lax.all_to_all(blocks, "seq", 0, 0, tiled=True)
    return got.transpose(1, 0, 2).reshape(rows, parts * cols)


PIECES = 2


def ring_place(index, n):
    if n != 8:
        return index
    y = lax.rem(index, 2)
    z = index // 2
    return z + y * (n - 1 - 2 * z)


def ring_index(place, n):
    place = lax.rem(place + 2 * n, n)
    if n != 8:
        return place
    back = place // (n // 2)
    return 2 * place + back * (2 * n - 1 - 4 * place)


def gelu_and_slope(v):
    scale = math.sqrt(2.0 / math.pi)
    square = v * v
    th = jnp.tanh(scale * (v + 0.044715 * square * v))
    up = 0.5 * (1.0 + th)
    slope = up + 0.5 * v * (1.0 - th * th) * (scale * (1.0 + 3.0 * 0.044715 * square))
    return v * up, slope


def ring_kernel(
    n, x_ref, y_ref, enc_ref, dec_ref, out_ref, slots, term, mine,
    rs_send, rs_recv, ag_send, ag_recv, local_sem,
):
    me = lax.axis_index("seq")
    place = ring_place(me, n)
    nexts = (ring_index(place + 1, n), ring_index(place - 1, n))
    half = x_ref.shape[1]
    share = enc_ref.shape[1]
    side = half // 2
    piece = side // PIECES

    barrier = pltpu.get_barrier_semaphore()
    for other in nexts:
        pl.semaphore_signal(
            barrier, inc=1, device_id={"seq": other}, device_id_type=pl.DeviceIdType.MESH
        )
    pl.semaphore_wait(barrier, 2)

    def signed(d, steps):
        return place - steps if d == 0 else place + steps

    def own_term(d, steps):
        chunk = ring_index(signed(d, steps), n)
        at = pl.ds(d * side, side)
        a = jnp.dot(x_ref[chunk, at, :], enc_ref[...], preferred_element_type=jnp.float32)
        b = jnp.dot(y_ref[chunk, at, :], dec_ref[...], preferred_element_type=jnp.float32)
        return a, b

    def rs_copy(d, s, q):
        at = pl.ds(q * piece, piece)
        return pltpu.make_async_remote_copy(
            src_ref=slots.at[d, s, at],
            dst_ref=slots.at[d, s + 1, at],
            send_sem=rs_send.at[d, s, q],
            recv_sem=rs_recv.at[d, s, q],
            device_id={"seq": nexts[d]},
            device_id_type=pl.DeviceIdType.MESH,
        )

    def ag_copy(d, s, q, first):
        at = pl.ds(d * side + q * piece, piece)
        owner = ring_index(signed(d, s), n)
        return pltpu.make_async_remote_copy(
            src_ref=mine.at[at] if first else out_ref.at[owner, at],
            dst_ref=out_ref.at[owner, at],
            send_sem=ag_send.at[d, s, q],
            recv_sem=ag_recv.at[d, s, q],
            device_id={"seq": nexts[d]},
            device_id_type=pl.DeviceIdType.MESH,
        )

    for d in range(2):
        a, b = own_term(d, 1)
        slots[d, 0, :, :share] = a.astype(BF16)
        slots[d, 0, :, share:] = b.astype(BF16)
        for q in range(PIECES):
            rs_copy(d, 0, q).start()

    def fill(s):
        for d in range(2):
            a, b = own_term(d, s + 2)
            term[d, :, :share] = a
            term[d, :, share:] = b

    def rs_step(s, carry):
        fill(s)
        for q in range(PIECES):
            at = pl.ds(q * piece, piece)
            for d in range(2):
                rs_copy(d, s, q).wait_recv()
                total = slots[d, s + 1, at, :].astype(F32) + term[d, at, :]
                slots[d, s + 1, at, :] = total.astype(BF16)
                rs_copy(d, s + 1, q).start()
        return carry

    lax.fori_loop(0, n - 2, rs_step, 0)
    fill(n - 2)
    for q in range(PIECES):
        at = pl.ds(q * piece, piece)
        for d in range(2):
            rs_copy(d, n - 2, q).wait_recv()
            rows = pl.ds(d * side + q * piece, piece)
            pre = slots[d, n - 1, at, :share].astype(F32) + term[d, at, :share]
            grad = slots[d, n - 1, at, share:].astype(F32) + term[d, at, share:]
            value, slope = gelu_and_slope(pre)
            mine[rows, :share] = value.astype(BF16)
            mine[rows, share:] = (grad * slope).astype(BF16)
            ag_copy(d, 0, q, True).start()
    local = pltpu.make_async_copy(mine, out_ref.at[me], local_sem)
    local.start()

    def ag_step(s, carry):
        for q in range(PIECES):
            for d in range(2):
                incoming(d, s, q).wait_recv()
                ag_copy(d, s + 1, q, False).start()
        return carry

    def incoming(d, s, q):
        at = pl.ds(d * side + q * piece, piece)
        owner = ring_index(signed(d, s + 1), n)
        return pltpu.make_async_remote_copy(
            src_ref=mine.at[at],
            dst_ref=out_ref.at[owner, at],
            send_sem=ag_send.at[d, s, q],
            recv_sem=ag_recv.at[d, s, q],
            device_id={"seq": nexts[d]},
            device_id_type=pl.DeviceIdType.MESH,
        )

    lax.fori_loop(0, n - 2, ag_step, 0)
    for q in range(PIECES):
        for d in range(2):
            incoming(d, n - 2, q).wait_recv()

    def drain(s, carry):
        for q in range(PIECES):
            for d in range(2):
                rs_copy(d, s, q).wait_send()
                ag_copy(d, s, q, True).wait_send()
        return carry

    lax.fori_loop(0, n - 1, drain, 0)
    local.wait()


def ring(pool_taps, cot_taps, enc_mat, dec_mat, n):
    half = pool_taps.shape[1]
    share = enc_mat.shape[1]
    depth = enc_mat.shape[0]
    vmem = pl.BlockSpec(memory_space=pltpu.VMEM)
    steps = (2, n - 1, PIECES)
    return pl.pallas_call(
        functools.partial(ring_kernel, n),
        out_shape=jax.ShapeDtypeStruct((n, half, 2 * share), BF16),
        in_specs=[vmem] * 4,
        out_specs=pl.BlockSpec(memory_space=pl.ANY),
        scratch_shapes=[
            pltpu.VMEM((2, n, half // 2, 2 * share), BF16),
            pltpu.VMEM((2, half // 2, 2 * share), F32),
            pltpu.VMEM((half, 2 * share), BF16),
            pltpu.SemaphoreType.DMA(steps),
            pltpu.SemaphoreType.DMA(steps),
            pltpu.SemaphoreType.DMA(steps),
            pltpu.SemaphoreType.DMA(steps),
            pltpu.SemaphoreType.DMA,
        ],
        compiler_params=pltpu.CompilerParams(
            collective_id=0, has_side_effects=True, vmem_limit_bytes=48 * 2**20
        ),
        cost_estimate=pl.CostEstimate(
            flops=4 * n * half * depth * share,
            bytes_accessed=4 * n * half * share * 2,
            transcendentals=half * share,
        ),
    )(pool_taps, cot_taps, enc_mat, dec_mat)


def wide_shards(inputs, enc_weight, dec_weight, cotangent):
    parts = lax.axis_size("seq")
    rows, width = inputs.shape
    half = rows // 2
    total = half * parts
    block, taps, share = enc_weight.shape
    half_width = cotangent.shape[1]

    pooled = (inputs.astype(F32).reshape(half, 2, width).sum(axis=1) * 0.5).astype(BF16)
    cot_full = lax.all_gather(cotangent, "chan", axis=1, tiled=True)
    core = lax.axis_index("chan")
    cores = lax.axis_size("chan")
    few = half // cores
    leaving = jnp.concatenate(
        [
            lax.dynamic_slice_in_dim(pooled, core * few, few, 0),
            lax.dynamic_slice_in_dim(cot_full, core * 2 * few, 2 * few, 0),
        ],
        axis=0,
    )
    columns = to_columns(leaving, parts).reshape(parts, 1, 3 * few, block)
    columns = lax.all_gather(columns, "chan", axis=1, tiled=True)
    pool_col = columns[:, :, :few].reshape(total, block)
    cot_col = columns[:, :, few:].reshape(total, 2, block).astype(F32)
    even = cot_col[:, 0]
    odd = cot_col[:, 1]
    pair = (even + odd).astype(BF16)
    cross = (odd + shift(even, 1)).astype(BF16)
    before = jnp.concatenate([even[:1].astype(BF16), cross[:-1]], axis=0)
    pool_taps = jnp.concatenate([shift(pool_col, t - 2) for t in range(taps)], axis=1)
    cot_taps = jnp.concatenate([shift(pair, 1), cross, pair, before, shift(pair, -1)], axis=1)
    enc_mat = enc_weight.transpose(1, 0, 2).reshape(taps * block, share)
    dec_mat = dec_weight.transpose(1, 0, 2).reshape(taps * block, share)

    joint = ring(
        pool_taps.reshape(parts, half, taps * block),
        cot_taps.reshape(parts, half, taps * block),
        enc_mat,
        dec_mat,
        parts,
    ).reshape(total, 2 * share)
    hidden_all = joint[:, :share]
    grad_all = joint[:, share:]

    contract_rows = (((0,), (0,)), ((), ()))
    contract_last = (((1,), (1,)), ((), ()))
    dec_grad = lax.dot_general(cot_taps, hidden_all, contract_rows, preferred_element_type=F32)
    enc_grad = lax.dot_general(pool_taps, grad_all, contract_rows, preferred_element_type=F32)
    dec_grad = dec_grad.astype(BF16).reshape(taps, block, share).transpose(1, 0, 2)
    enc_grad = enc_grad.astype(BF16).reshape(taps, block, share).transpose(1, 0, 2)

    dec_out = lax.dot_general(hidden_all, dec_mat, contract_last, preferred_element_type=F32)
    p0, p1, p2, p3, p4 = [dec_out[:, t * block : (t + 1) * block] for t in range(taps)]
    after4 = shift(p4, 1)
    before0 = shift(p0, -1)
    dec_even = before0 + shift(p1, -1) + p2 + p3 + after4
    dec_odd = before0 + p1 + p2 + shift(p3, 1) + after4
    decoded = jnp.stack([dec_even, dec_odd], axis=1).astype(BF16).reshape(parts, rows, block)
    enc_out = lax.dot_general(grad_all, enc_mat, contract_last, preferred_element_type=F32)
    pool_grad = sum(shift(enc_out[:, t * block : (t + 1) * block], 2 - t) for t in range(taps))
    pool_grad = pool_grad.astype(BF16).reshape(parts, half, block)
    mine = jnp.concatenate([decoded, pool_grad], axis=1)
    mine = lax.psum_scatter(mine, "chan", scatter_dimension=1, tiled=True)
    mine = lax.all_gather(to_rows(mine), "chan", axis=0, tiled=True)
    col_start = core * half_width
    mine = lax.dynamic_slice_in_dim(mine, col_start, half_width, 1).astype(F32)

    skip = lax.dynamic_slice_in_dim(inputs, col_start, half_width, 1)
    mixed_out = (skip.astype(F32) + mine[:rows]).astype(BF16)
    input_grad = (cotangent.astype(F32) + 0.5 * jnp.repeat(mine[rows:], 2, axis=0)).astype(BF16)
    return mixed_out, input_grad, enc_grad, dec_grad


LANES = 128
HALO = 16
EDGE = 8


def pair_kernel(
    x_ref, enc_ref, dec_ref, cot_ref, mixed_ref, in_grad_ref, enc_grad_ref, dec_grad_ref,
    x_own, spread, pc_ref, rows_all, weights, folded, z_enc, z_dec, hid, slope, pre_grad, g_taps, h_taps,
    enc_sum, dec_sum, part, give, take, give_y, take_y, grad_give,
    local_sem, wy_send, wy_recv, wz_send, wz_recv, wx_send, wx_recv,
    edge_send, edge_z, edge_y, edge_c, edge_fwd, edge_ysend, edge_csend,
    own_send, pz_send, pz_recv, py_send, py_recv, pc_send, pc_recv,
    give_sem, take_sem, grad_sem,
):
    g = lax.axis_index("groups")
    s = lax.axis_index("seq")
    c = lax.axis_index("chan")
    z, y = s // 2, lax.rem(s, 2)
    last = lax.axis_size("seq") // 2 - 1
    chunk, wide = pc_ref.shape[1], pc_ref.shape[2]
    cell = 2 * chunk
    taps, block = enc_ref.shape[0], enc_ref.shape[1]
    share = enc_ref.shape[2] // 2
    half = block // 2
    inner = chunk - HALO
    ids = pl.DeviceIdType.MESH
    to_y, to_x, to_c = {"seq": s + 1 - 2 * y}, {"groups": 1 - g}, {"chan": 1 - c}
    to_left, to_right = {"seq": s - 2}, {"seq": s + 2}
    has_left, has_right = z > 0, z < last

    def lanes(index, width):
        return pl.ds(pl.multiple_of(index * width, LANES), width)

    own_x = pltpu.make_async_copy(x_ref.at[:, lanes(c, wide)], x_own, local_sem.at[0, taps + 1])
    own_x.start()
    sources = (enc_ref, dec_ref)
    grad_refs = (enc_grad_ref, dec_grad_ref)

    def own_weight(w, t):
        return pltpu.make_async_copy(
            sources[w].at[t, :, lanes(y, share)],
            weights.at[w, pl.ds(pl.multiple_of(s * block, HALO), block), pl.ds(t * share, share)],
            local_sem.at[w, t],
        )

    for w in range(2):
        for t in range(taps):
            own_weight(w, t).start()

    barrier = pltpu.get_barrier_semaphore()
    for where in (to_y, to_x, to_c):
        pl.semaphore_signal(barrier, inc=1, device_id=where, device_id_type=ids)

    @pl.when(has_left)
    def _():
        pl.semaphore_signal(barrier, inc=1, device_id=to_left, device_id_type=ids)

    @pl.when(has_right)
    def _():
        pl.semaphore_signal(barrier, inc=1, device_id=to_right, device_id_type=ids)

    inside = jnp.where(has_left, 1, 0) + jnp.where(has_right, 1, 0)
    pl.semaphore_wait(barrier, 3 + inside)

    def remote(src, dst, send, recv, where):
        return pltpu.make_async_remote_copy(
            src_ref=src, dst_ref=dst, send_sem=send, recv_sem=recv,
            device_id=where, device_id_type=ids,
        )

    def weight_to_y(w, t, side):
        at = pl.ds(pl.multiple_of(side * half, HALO), half)
        row = pl.multiple_of(s * block + side * half, HALO)
        return remote(
            sources[w].at[t, at, lanes(1 - y, share)],
            weights.at[w, pl.ds(row, half), pl.ds(t * share, share)],
            wy_send.at[w, t, side], wy_recv.at[w, t, side], to_y,
        )

    def slab(w, b, side):
        return weights.at[w, pl.ds(pl.multiple_of(b * block + side * half, HALO), half), :]

    def weight_z(w, zz, b, d, where):
        ref = slab(w, 2 * zz + b, g)
        return remote(ref, ref, wz_send.at[d, w, zz, b], wz_recv.at[w, zz, b], where)

    def weight_x(w, zz, b, side):
        ref = slab(w, 2 * zz + b, side)
        return remote(ref, ref, wx_send.at[w, zz, b], wx_recv.at[w, zz, b], to_x)

    def edge_of(zz, yy, cc):
        at = pl.multiple_of(HALO + (2 * zz + yy) * chunk + yy * inner, HALO)
        return rows_all.at[:, pl.ds(at, HALO), lanes(cc, wide)]

    def inner_of(i, zz, yy, cc):
        at = pl.multiple_of(HALO + (2 * zz + yy) * chunk + (1 - yy) * HALO, HALO)
        return rows_all.at[i, pl.ds(at, inner), lanes(cc, wide)]

    own_edge = pc_ref.at[:, pl.ds(pl.multiple_of(y * inner, HALO), HALO), :]

    def own_inner(i):
        return pc_ref.at[i, pl.ds(pl.multiple_of((1 - y) * HALO, HALO), inner), :]

    local_edge = pltpu.make_async_copy(own_edge, edge_of(z, y, c), local_sem.at[0, taps])
    local_inner = [
        pltpu.make_async_copy(own_inner(i), inner_of(i, z, y, c), local_sem.at[1, taps + i])
        for i in range(3)
    ]

    for w in range(2):
        for t in range(taps):
            weight_to_y(w, t, g).start()

    for w in range(2):
        for t in range(taps):
            own_weight(w, t).wait()

        @pl.when(has_left)
        def _():
            weight_z(w, z, y, 0, to_left).start()

        @pl.when(has_right)
        def _():
            weight_z(w, z, y, 1, to_right).start()

    def edge_out(d, where):
        return remote(own_edge, edge_of(z, y, c), edge_send.at[d], edge_z.at[z], where)

    def edge_forward(zz, where):
        ref = edge_of(zz, y, c)
        return remote(ref, ref, edge_fwd.at[zz], edge_z.at[zz], where)

    def edge_to_y(zz):
        src = edge_of(zz, y, c)
        return remote(src, src, edge_ysend.at[zz], edge_y.at[zz], to_y)

    def edge_to_c(zz, yy):
        ref = edge_of(zz, yy, c)
        return remote(ref, ref, edge_csend.at[zz, yy], edge_c.at[zz, yy], to_c)

    tiles = wide // LANES
    own_x.wait()
    for k in range(tiles):
        cols = slice(k * LANES, (k + 1) * LANES)
        spread[k] = x_own[:, cols].astype(F32)
        spread[tiles + k] = cot_ref[:, cols].astype(F32)
    for k in range(tiles):
        cols = slice(k * LANES, (k + 1) * LANES)
        even, odd = pl.ds(0, chunk, stride=2), pl.ds(1, chunk, stride=2)
        pc_ref[0, :, cols] = ((spread[k, even, :] + spread[k, odd, :]) * 0.5).astype(BF16)
        pc_ref[1, :, cols] = spread[tiles + k, even, :].astype(BF16)
        pc_ref[2, :, cols] = spread[tiles + k, odd, :].astype(BF16)

    local_edge.start()

    @pl.when(has_left)
    def _():
        edge_out(0, to_left).start()

    @pl.when(has_right)
    def _():
        edge_out(1, to_right).start()

    for copy in local_inner:
        copy.start()
    rows_all[:, :HALO, :] = jnp.zeros((3, HALO, 2 * wide), BF16)
    bottom = rows_all.shape[1] - HALO
    rows_all[:, bottom:, :] = jnp.zeros((3, HALO, 2 * wide), BF16)
    local_edge.wait()
    edge_to_y(z).start()
    edge_to_c(z, y).start()

    for w in range(2):
        for t in range(taps):
            weight_from_y(
                weights, sources, wy_send, wy_recv, w, t, g, s, y, half, block, share, to_y, lanes
            ).wait_recv()

        @pl.when(has_left)
        def _():
            weight_z(w, z, 1 - y, 0, to_left).start()

        @pl.when(has_right)
        def _():
            weight_z(w, z, 1 - y, 1, to_right).start()

    for w in range(2):
        for t in range(taps):
            weight_to_y(w, t, 1 - g).start()

    def inner_to_y(i, zz):
        ref = inner_of(i, zz, y, c)
        return remote(ref, ref, py_send.at[zz, i], py_recv.at[zz, i], to_y)

    def inner_to_c(i, zz, yy):
        ref = inner_of(i, zz, yy, c)
        return remote(ref, ref, pc_send.at[zz, yy, i], pc_recv.at[zz, yy, i], to_c)

    def inner_out(i, d, where):
        return remote(own_inner(i), inner_of(i, z, y, c), own_send.at[d, i], pz_recv.at[z, i], where)

    for i in range(3):
        local_inner[i].wait()
        inner_to_y(i, z).start()
        inner_to_c(i, z, y).start()

    def order(k):
        low = jnp.minimum(z, last - z)
        near = jnp.where(low == 0, k, jnp.where(k < 2, 1 - k, k))
        return jnp.where(z * 2 < last, near, last - near)

    def edge_arrives_y(zz):
        ref = edge_of(zz, 1 - y, c)
        return remote(ref, ref, edge_ysend.at[zz], edge_y.at[zz], to_y)

    def send_own_rows(d, where):
        for i in range(3):
            inner_out(i, d, where).start()

    @pl.when(z == 0)
    def _():
        send_own_rows(1, to_right)

    @pl.when(z == last)
    def _():
        send_own_rows(0, to_left)

    def weight_step(k, carry):
        for sign in (-1, 1):
            zz = z + sign * k

            @pl.when((zz >= 0) & (zz <= last))
            def _():
                for w in range(2):
                    for b in range(2):
                        weight_z(w, zz, b, 0, to_y).wait_recv()

                        if sign < 0:
                            @pl.when(has_right)
                            def _():
                                weight_z(w, zz, b, 1, to_right).start()
                        else:
                            @pl.when(has_left)
                            def _():
                                weight_z(w, zz, b, 0, to_left).start()

                        weight_x(w, zz, b, g).start()

                edge_forward(zz, to_y).wait_recv()
                if sign < 0:
                    @pl.when(has_right)
                    def _():
                        edge_forward(zz, to_right).start()
                else:
                    @pl.when(has_left)
                    def _():
                        edge_forward(zz, to_left).start()

                edge_to_y(zz).start()
                edge_to_c(zz, y).start()

        @pl.when((z == k) & has_right)
        def _():
            send_own_rows(1, to_right)

        @pl.when((last - z == k) & has_left)
        def _():
            send_own_rows(0, to_left)

        return carry

    lax.fori_loop(1, last + 1, weight_step, 0)

    def inner_forward(i, zz, where):
        ref = inner_of(i, zz, y, c)
        return remote(ref, ref, pz_send.at[zz, i], pz_recv.at[zz, i], where)

    def receive(i, zz):
        inner_forward(i, zz, to_y).wait_recv()

        @pl.when((zz < z) & has_right)
        def _():
            inner_forward(i, zz, to_right).start()

        @pl.when((zz > z) & has_left)
        def _():
            inner_forward(i, zz, to_left).start()

        inner_to_y(i, zz).start()
        inner_to_c(i, zz, y).start()

    def edge_end(zz, carry):
        edge_arrives_y(zz).wait_recv()
        edge_to_c(zz, 1 - y).start()
        return carry

    lax.fori_loop(0, last + 1, edge_end, 0)

    def across(zz):
        for i in range(3):
            ref = inner_of(i, zz, 1 - y, c)
            remote(ref, ref, py_send.at[zz, i], py_recv.at[zz, i], to_y).wait_recv()
            inner_to_c(i, zz, 1 - y).start()

    across(z)
    middle = has_left & has_right

    def receive_step(k, carry):
        for i in range(3):
            receive(i, order(k))
        return carry

    lax.fori_loop(1, jnp.where(middle, last + 1, 2), receive_step, 0)

    for zz in range(last + 1):
        for yy in range(2):
            ref = edge_of(zz, yy, 1 - c)
            remote(ref, ref, edge_csend.at[zz, yy], edge_c.at[zz, yy], to_c).wait_recv()

    def each_other_cell(body):
        def step(k, carry):
            body(order(k))
            return carry

        lax.fori_loop(1, last + 1, step, 0)

    for w in range(2):
        for t in range(taps):
            weight_from_y(
                weights, sources, wy_send, wy_recv, w, t, 1 - g, s, y, half, block, share, to_y, lanes
            ).wait_recv()

    def wait_x(zz):
        for w in range(2):
            for b in range(2):
                weight_x(w, zz, b, 1 - g).wait_recv()

    each_other_cell(wait_x)

    step_rows = 64

    def fold(i, carry):
        at = pl.ds(pl.multiple_of(i * step_rows, HALO), step_rows)
        w = [weights[1, at, t * share : (t + 1) * share].astype(F32) for t in range(5)]
        folded[0, at, :share] = (w[0] + w[1]).astype(BF16)
        folded[0, at, share : 2 * share] = (w[2] + w[3]).astype(BF16)
        folded[0, at, 2 * share :] = weights[1, at, 4 * share :]
        folded[1, at, :share] = weights[1, at, :share]
        folded[1, at, share : 2 * share] = (w[1] + w[2]).astype(BF16)
        folded[1, at, 2 * share :] = (w[3] + w[4]).astype(BF16)
        return carry

    lax.fori_loop(0, weights.shape[1] // step_rows, fold, 0)

    contract_rows = (((0,), (0,)), ((), ()))
    contract_last = (((1,), (1,)), ((), ()))
    wide_rows = cell + 2 * HALO
    mid_rows = cell + 2 * EDGE
    window = pl.ds(pl.multiple_of((2 * block * z) // LANES * LANES, LANES), 2 * LANES)
    offset = 2 * block * z - (2 * block * z) // LANES * LANES

    enc_sum[...] = jnp.zeros_like(enc_sum)
    dec_sum[...] = jnp.zeros_like(dec_sum)

    def sums_over_cores():
        for i in range(3):
            total = part[i] + take[i].astype(F32)
            part[i] = total
            rows = pl.ds(pl.multiple_of((1 - y) * chunk, HALO), chunk)
            give_y[i] = part[i, rows, :].astype(BF16)

    give_copy = remote(give, take, give_sem.at[0], take_sem.at[0], to_c)
    give_y_copy = remote(give_y, take_y, give_sem.at[1], take_sem.at[1], to_y)

    def grad_copy(w):
        return remote(
            grad_give.at[w], grad_refs[w].at[:, :, lanes(y, share)], grad_sem.at[0, w], grad_sem.at[1, w], to_y
        )

    def grads(w, who):
        at = pl.ds(pl.multiple_of(offset + who * block, HALO), block)
        if w == 0:
            return [enc_sum[at, t * share : (t + 1) * share].astype(BF16) for t in range(5)]
        e = [dec_sum[0, at, k * share : (k + 1) * share] for k in range(3)]
        o = [dec_sum[1, at, k * share : (k + 1) * share] for k in range(3)]
        both = (e[0] + o[0], e[0] + o[1], e[1] + o[1], e[1] + o[2], e[2] + o[2])
        return [v.astype(BF16) for v in both]

    def give_grads(w):
        for t, value in enumerate(grads(w, 1 - y)):
            grad_give[w, t] = value
        grad_copy(w).start()

    def cell_step(k, carry):
        zz = order(k)

        def slot(when, q):
            @pl.when(when & ((z == 0) | (z == last)) & (q < 3 * (last - 1)))
            def _():
                receive(lax.rem(q, 3), order(2 + q // 3))

        for yy in range(2):
            for i in range(3):
                ref = inner_of(i, zz, yy, 1 - c)
                remote(ref, ref, pc_send.at[zz, yy, i], pc_recv.at[zz, yy, i], to_c).wait_recv()

        base = pl.multiple_of(zz * cell, HALO)
        at = pl.ds(base, wide_rows)
        product = jnp.dot(rows_all[0, at, :], weights[0], preferred_element_type=F32)
        for t in range(5 * tiles):
            z_enc[t] = product[:, t * LANES : (t + 1) * LANES]
        slot(k < 2, 3 * k)

        piece = mid_rows // 6
        product = jnp.dot(
            rows_all[1, at, :], folded[0], preferred_element_type=F32
        ) + jnp.dot(rows_all[2, at, :], folded[1], preferred_element_type=F32)
        for r in range(6):
            start = r * piece
            for q in range(tiles):
                pre = z_enc[q, pl.ds(start + 6, piece), :]
                for t in range(1, 5):
                    pre += z_enc[t * tiles + q, pl.ds(start + 6 + t, piece), :]
                value, up = gelu_and_slope(pre)
                row = lax.broadcasted_iota(jnp.int32, (piece, LANES), 0)
                if r == 0:
                    keep = (row >= EDGE) | (zz > 0)
                    value, up = jnp.where(keep, value, 0.0), jnp.where(keep, up, 0.0)
                if r == 5:
                    keep = (row < piece - EDGE) | (zz < last)
                    value, up = jnp.where(keep, value, 0.0), jnp.where(keep, up, 0.0)
                hid[q, pl.ds(start, piece), :] = value
                slope[q, pl.ds(start, piece), :] = up
        for r in range(cell // LANES):
            for q in range(tiles):
                for t in range(3):
                    moved = hid[q, pl.ds(r * LANES + EDGE - 1 + t, LANES), :]
                    h_taps[r * LANES : (r + 1) * LANES, t * share + q * LANES : t * share + (q + 1) * LANES] = (
                        moved.astype(BF16)
                    )
        for t in range(3 * tiles):
            z_dec[t] = product[:, t * LANES : (t + 1) * LANES]
        slot(k < 2, 3 * k + 1)

        body = pl.ds(base + HALO, cell)
        for i in range(2):
            dec_sum[i] += lax.dot_general(
                rows_all[1 + i, body, window], h_taps[...], contract_rows,
                preferred_element_type=F32,
            )
        for r in range(6):
            start = r * piece
            for q in range(tiles):
                grad = z_dec[q, pl.ds(start + 9, piece), :]
                for t in range(1, 3):
                    grad += z_dec[t * tiles + q, pl.ds(start + 9 - t, piece), :]
                pre_grad[q, pl.ds(start, piece), :] = grad * slope[q, pl.ds(start, piece), :]
        for r in range(cell // LANES):
            for q in range(tiles):
                for t in range(5):
                    moved = pre_grad[q, pl.ds(r * LANES + EDGE + 2 - t, LANES), :]
                    g_taps[r * LANES : (r + 1) * LANES, t * share + q * LANES : t * share + (q + 1) * LANES] = (
                        moved.astype(BF16)
                    )

        @pl.when(k < last)
        def _():
            across(order(k + 1))

        @pl.when(k == last)
        def _():
            give_grads(1)

        enc_sum[...] += lax.dot_general(
            rows_all[0, body, window], g_taps[...], contract_rows, preferred_element_type=F32
        )

        @pl.when(k == 0)
        def _():
            for i in range(3):
                for h in range(2):
                    cols = pl.ds(pl.multiple_of((c if h == 0 else 1 - c) * wide, LANES), wide)
                    rhs = weights[0, cols, :] if i == 0 else folded[i - 1, cols, :]
                    lhs = g_taps[...] if i == 0 else h_taps[...]
                    value = lax.dot_general(lhs, rhs, contract_last, preferred_element_type=F32)
                    if h == 0:
                        part[i] = value
                    else:
                        give[i] = value.astype(BF16)
                if i == 0:
                    slot(k == 0, 2)
            give_copy.start()

        slot(k == 1, 5)

        @pl.when(k == 1)
        def _():
            give_copy.wait_recv()
            sums_over_cores()
            give_y_copy.start()

        return carry

    lax.fori_loop(0, last + 1, cell_step, 0)

    give_grads(0)
    for w in range(2):
        for t, value in enumerate(grads(w, y)):
            grad_refs[w][t, :, lanes(y, share)] = value

    give_y_copy.wait_recv()
    for k in range(tiles):
        cols = slice(k * LANES, (k + 1) * LANES)
        even, odd = pl.ds(0, chunk, stride=2), pl.ds(1, chunk, stride=2)
        own = pl.ds(pl.multiple_of(y * chunk, HALO), chunk)
        pool_grad, first, second = [part[i, own, cols] + take_y[i, :, cols].astype(F32) for i in range(3)]
        spread[k, even, :] = first
        spread[k, odd, :] = second
        spread[tiles + k, even, :] = pool_grad
        spread[tiles + k, odd, :] = pool_grad
        mixed_ref[:, cols] = (x_own[:, cols].astype(F32) + spread[k]).astype(BF16)
        in_grad_ref[:, cols] = (cot_ref[:, cols].astype(F32) + 0.5 * spread[tiles + k]).astype(BF16)

    give_copy.wait_send()
    give_y_copy.wait_send()
    for w in range(2):
        for t in range(taps):
            weight_to_y(w, t, g).wait_send()
            weight_to_y(w, t, 1 - g).wait_send()

    @pl.when(has_left)
    def _():
        edge_out(0, to_left).wait_send()
        for i in range(3):
            inner_out(i, 0, to_left).wait_send()
        for w in range(2):
            for b in range(2):
                weight_z(w, z, b, 0, to_left).wait_send()

    @pl.when(has_right)
    def _():
        edge_out(1, to_right).wait_send()
        for i in range(3):
            inner_out(i, 1, to_right).wait_send()
        for w in range(2):
            for b in range(2):
                weight_z(w, z, b, 1, to_right).wait_send()

    def drain(k, carry):
        zz = order(k)
        edge_to_y(zz).wait_send()
        for yy in range(2):
            edge_to_c(zz, yy).wait_send()
        for i in range(3):
            inner_to_y(i, zz).wait_send()
            for yy in range(2):
                inner_to_c(i, zz, yy).wait_send()

        @pl.when(k > 0)
        def _():
            for w in range(2):
                for b in range(2):
                    weight_x(w, zz, b, g).wait_send()

        @pl.when((zz < z) & has_right)
        def _():
            edge_forward(zz, to_right).wait_send()
            for i in range(3):
                inner_forward(i, zz, to_right).wait_send()
            for w in range(2):
                for b in range(2):
                    weight_z(w, zz, b, 1, to_right).wait_send()

        @pl.when((zz > z) & has_left)
        def _():
            edge_forward(zz, to_left).wait_send()
            for i in range(3):
                inner_forward(i, zz, to_left).wait_send()
            for w in range(2):
                for b in range(2):
                    weight_z(w, zz, b, 0, to_left).wait_send()

        return carry

    lax.fori_loop(0, last + 1, drain, 0)
    for w in range(2):
        grad_copy(w).wait_send()
    for w in range(2):
        grad_arrives = remote(
            grad_give.at[w], grad_refs[w].at[:, :, lanes(1 - y, share)],
            grad_sem.at[0, w], grad_sem.at[1, w], to_y,
        )
        grad_arrives.wait_recv()


def weight_from_y(weights, sources, send, recv, w, t, side, s, y, half, block, share, to_y, lanes):
    other = s + 1 - 2 * y
    row = pl.multiple_of(other * block + side * half, HALO)
    return pltpu.make_async_remote_copy(
        src_ref=sources[w].at[t, pl.ds(pl.multiple_of(side * half, HALO), half), lanes(1 - y, share)],
        dst_ref=weights.at[w, pl.ds(row, half), pl.ds(t * share, share)],
        send_sem=send.at[w, t, side],
        recv_sem=recv.at[w, t, side],
        device_id=to_y,
        device_id_type=pl.DeviceIdType.MESH,
    )


def pair_call(inputs, enc_taps, dec_taps, cotangent, cells):
    rows, wide = cotangent.shape
    chunk = rows // 2
    taps, block, both = enc_taps.shape
    share = both // 2
    cell = 2 * chunk
    vmem = pl.BlockSpec(memory_space=pltpu.VMEM)
    anywhere = pl.BlockSpec(memory_space=pl.ANY)
    dma = pltpu.SemaphoreType.DMA
    tall = cells * cell + 2 * HALO
    width = 2 * wide
    return pl.pallas_call(
        pair_kernel,
        out_shape=[
            jax.ShapeDtypeStruct((rows, wide), BF16),
            jax.ShapeDtypeStruct((rows, wide), BF16),
            jax.ShapeDtypeStruct((taps, block, both), BF16),
            jax.ShapeDtypeStruct((taps, block, both), BF16),
        ],
        in_specs=[anywhere, anywhere, anywhere, vmem],
        out_specs=[vmem] * 4,
        scratch_shapes=[
            pltpu.VMEM((rows, wide), BF16),
            pltpu.VMEM((2 * (wide // LANES), rows, LANES), F32),
            pltpu.VMEM((3, chunk, wide), BF16),
            pltpu.VMEM((3, tall, width), BF16),
            pltpu.VMEM((2, width, taps * share), BF16),
            pltpu.VMEM((2, width, 3 * share), BF16),
            pltpu.VMEM((taps * share // LANES, cell + 2 * HALO, LANES), F32),
            pltpu.VMEM((3 * share // LANES, cell + 2 * HALO, LANES), F32),
            pltpu.VMEM((share // LANES, cell + 2 * EDGE, LANES), F32),
            pltpu.VMEM((share // LANES, cell + 2 * EDGE, LANES), F32),
            pltpu.VMEM((share // LANES, cell + 2 * EDGE, LANES), F32),
            pltpu.VMEM((cell, taps * share), BF16),
            pltpu.VMEM((cell, 3 * share), BF16),
            pltpu.VMEM((2 * LANES, taps * share), F32),
            pltpu.VMEM((2, 2 * LANES, 3 * share), F32),
            pltpu.VMEM((3, cell, wide), F32),
            pltpu.VMEM((3, cell, wide), BF16),
            pltpu.VMEM((3, cell, wide), BF16),
            pltpu.VMEM((3, chunk, wide), BF16),
            pltpu.VMEM((3, chunk, wide), BF16),
            pltpu.VMEM((2, taps, block, share), BF16),
            dma((2, taps + 3)),
            dma((2, taps, 2)), dma((2, taps, 2)),
            dma((2, 2, cells, 2)), dma((2, cells, 2)), dma((2, cells, 2)), dma((2, cells, 2)),
            dma((2,)), dma((cells,)), dma((cells,)), dma((cells, 2)), dma((cells,)), dma((cells,)),
            dma((cells, 2)),
            dma((2, 3)), dma((cells, 3)), dma((cells, 3)), dma((cells, 3)), dma((cells, 3)),
            dma((cells, 2, 3)), dma((cells, 2, 3)),
            dma((2,)), dma((2,)), dma((2, 2)),
        ],
        compiler_params=pltpu.CompilerParams(
            collective_id=0, has_side_effects=True, vmem_limit_bytes=58 * 2**20
        ),
        cost_estimate=pl.CostEstimate(
            flops=2 * 11 * cells * cell * width * share + 4 * 11 * cells * cell * block * share,
            bytes_accessed=4 * taps * block * both * 2,
            transcendentals=cells * cell * share,
        ),
    )(inputs, enc_taps, dec_taps, cotangent)


def shards(inputs, enc_weight, dec_weight, cotangent):
    parts = lax.axis_size("seq")
    cores = lax.axis_size("chan")
    rows, width = inputs.shape
    chunk = rows // 2
    block, taps, share = enc_weight.shape
    wide = cotangent.shape[1]
    fits = parts == 8 and cores == 2 and lax.axis_size("groups") == 2 and taps == 5
    fits = fits and block == 96 and share == 2 * wide and wide % LANES == 0 and chunk == 256
    if not fits:
        return wide_shards(inputs, enc_weight, dec_weight, cotangent)
    mixed_out, input_grad, enc_grad, dec_grad = pair_call(
        inputs, enc_weight.transpose(1, 0, 2), dec_weight.transpose(1, 0, 2), cotangent, parts // 2
    )
    return mixed_out, input_grad, enc_grad.transpose(1, 0, 2), dec_grad.transpose(1, 0, 2)


def solution(mesh):
    return jax.shard_map(
        shards,
        mesh=mesh,
        in_specs=(
            P(("groups", "seq"), None),
            P("seq", None, "chan"),
            P("seq", None, "chan"),
            P(("groups", "seq"), "chan"),
        ),
        out_specs=(
            P(("groups", "seq"), "chan"),
            P(("groups", "seq"), "chan"),
            P(("groups", "seq"), None, "chan"),
            P(("groups", "seq"), None, "chan"),
        ),
        check_vma=False,
    )
```

```python
import functools
import math

import jax
import jax.numpy as jnp
from jax import lax
from jax.experimental import pallas as pl
from jax.experimental.pallas import tpu as pltpu
from jax.sharding import PartitionSpec as P

BF16 = jnp.bfloat16
F32 = jnp.float32


def shift(array, by):
    length = array.shape[0]
    if by == 0:
        return array
    pad = jnp.zeros((abs(by),) + array.shape[1:], array.dtype)
    if by > 0:
        return jnp.concatenate([array[by:], pad], axis=0)
    return jnp.concatenate([pad, array[: length + by]], axis=0)


def to_columns(array, parts):
    rows, cols = array.shape
    blocks = array.reshape(rows, parts, cols // parts).transpose(1, 0, 2)
    return lax.all_to_all(blocks, "seq", 0, 0, tiled=True)


def to_rows(blocks):
    parts, rows, cols = blocks.shape
    got = lax.all_to_all(blocks, "seq", 0, 0, tiled=True)
    return got.transpose(1, 0, 2).reshape(rows, parts * cols)


PIECES = 2


def ring_place(index, n):
    if n != 8:
        return index
    y = lax.rem(index, 2)
    z = index // 2
    return z + y * (n - 1 - 2 * z)


def ring_index(place, n):
    place = lax.rem(place + 2 * n, n)
    if n != 8:
        return place
    back = place // (n // 2)
    return 2 * place + back * (2 * n - 1 - 4 * place)


def gelu_and_slope(v):
    scale = math.sqrt(2.0 / math.pi)
    square = v * v
    th = jnp.tanh(scale * (v + 0.044715 * square * v))
    up = 0.5 * (1.0 + th)
    slope = up + 0.5 * v * (1.0 - th * th) * (scale * (1.0 + 3.0 * 0.044715 * square))
    return v * up, slope


def ring_kernel(
    n, x_ref, y_ref, enc_ref, dec_ref, out_ref, slots, term, mine,
    rs_send, rs_recv, ag_send, ag_recv, local_sem,
):
    me = lax.axis_index("seq")
    place = ring_place(me, n)
    nexts = (ring_index(place + 1, n), ring_index(place - 1, n))
    half = x_ref.shape[1]
    share = enc_ref.shape[1]
    side = half // 2
    piece = side // PIECES

    barrier = pltpu.get_barrier_semaphore()
    for other in nexts:
        pl.semaphore_signal(
            barrier, inc=1, device_id={"seq": other}, device_id_type=pl.DeviceIdType.MESH
        )
    pl.semaphore_wait(barrier, 2)

    def signed(d, steps):
        return place - steps if d == 0 else place + steps

    def own_term(d, steps):
        chunk = ring_index(signed(d, steps), n)
        at = pl.ds(d * side, side)
        a = jnp.dot(x_ref[chunk, at, :], enc_ref[...], preferred_element_type=jnp.float32)
        b = jnp.dot(y_ref[chunk, at, :], dec_ref[...], preferred_element_type=jnp.float32)
        return a, b

    def rs_copy(d, s, q):
        at = pl.ds(q * piece, piece)
        return pltpu.make_async_remote_copy(
            src_ref=slots.at[d, s, at],
            dst_ref=slots.at[d, s + 1, at],
            send_sem=rs_send.at[d, s, q],
            recv_sem=rs_recv.at[d, s, q],
            device_id={"seq": nexts[d]},
            device_id_type=pl.DeviceIdType.MESH,
        )

    def ag_copy(d, s, q, first):
        at = pl.ds(d * side + q * piece, piece)
        owner = ring_index(signed(d, s), n)
        return pltpu.make_async_remote_copy(
            src_ref=mine.at[at] if first else out_ref.at[owner, at],
            dst_ref=out_ref.at[owner, at],
            send_sem=ag_send.at[d, s, q],
            recv_sem=ag_recv.at[d, s, q],
            device_id={"seq": nexts[d]},
            device_id_type=pl.DeviceIdType.MESH,
        )

    for d in range(2):
        a, b = own_term(d, 1)
        slots[d, 0, :, :share] = a.astype(BF16)
        slots[d, 0, :, share:] = b.astype(BF16)
        for q in range(PIECES):
            rs_copy(d, 0, q).start()

    def fill(s):
        for d in range(2):
            a, b = own_term(d, s + 2)
            term[d, :, :share] = a
            term[d, :, share:] = b

    def rs_step(s, carry):
        fill(s)
        for q in range(PIECES):
            at = pl.ds(q * piece, piece)
            for d in range(2):
                rs_copy(d, s, q).wait_recv()
                total = slots[d, s + 1, at, :].astype(F32) + term[d, at, :]
                slots[d, s + 1, at, :] = total.astype(BF16)
                rs_copy(d, s + 1, q).start()
        return carry

    lax.fori_loop(0, n - 2, rs_step, 0)
    fill(n - 2)
    for q in range(PIECES):
        at = pl.ds(q * piece, piece)
        for d in range(2):
            rs_copy(d, n - 2, q).wait_recv()
            rows = pl.ds(d * side + q * piece, piece)
            pre = slots[d, n - 1, at, :share].astype(F32) + term[d, at, :share]
            grad = slots[d, n - 1, at, share:].astype(F32) + term[d, at, share:]
            value, slope = gelu_and_slope(pre)
            mine[rows, :share] = value.astype(BF16)
            mine[rows, share:] = (grad * slope).astype(BF16)
            ag_copy(d, 0, q, True).start()
    local = pltpu.make_async_copy(mine, out_ref.at[me], local_sem)
    local.start()

    def ag_step(s, carry):
        for q in range(PIECES):
            for d in range(2):
                incoming(d, s, q).wait_recv()
                ag_copy(d, s + 1, q, False).start()
        return carry

    def incoming(d, s, q):
        at = pl.ds(d * side + q * piece, piece)
        owner = ring_index(signed(d, s + 1), n)
        return pltpu.make_async_remote_copy(
            src_ref=mine.at[at],
            dst_ref=out_ref.at[owner, at],
            send_sem=ag_send.at[d, s, q],
            recv_sem=ag_recv.at[d, s, q],
            device_id={"seq": nexts[d]},
            device_id_type=pl.DeviceIdType.MESH,
        )

    lax.fori_loop(0, n - 2, ag_step, 0)
    for q in range(PIECES):
        for d in range(2):
            incoming(d, n - 2, q).wait_recv()

    def drain(s, carry):
        for q in range(PIECES):
            for d in range(2):
                rs_copy(d, s, q).wait_send()
                ag_copy(d, s, q, True).wait_send()
        return carry

    lax.fori_loop(0, n - 1, drain, 0)
    local.wait()


def ring(pool_taps, cot_taps, enc_mat, dec_mat, n):
    half = pool_taps.shape[1]
    share = enc_mat.shape[1]
    depth = enc_mat.shape[0]
    vmem = pl.BlockSpec(memory_space=pltpu.VMEM)
    steps = (2, n - 1, PIECES)
    return pl.pallas_call(
        functools.partial(ring_kernel, n),
        out_shape=jax.ShapeDtypeStruct((n, half, 2 * share), BF16),
        in_specs=[vmem] * 4,
        out_specs=pl.BlockSpec(memory_space=pl.ANY),
        scratch_shapes=[
            pltpu.VMEM((2, n, half // 2, 2 * share), BF16),
            pltpu.VMEM((2, half // 2, 2 * share), F32),
            pltpu.VMEM((half, 2 * share), BF16),
            pltpu.SemaphoreType.DMA(steps),
            pltpu.SemaphoreType.DMA(steps),
            pltpu.SemaphoreType.DMA(steps),
            pltpu.SemaphoreType.DMA(steps),
            pltpu.SemaphoreType.DMA,
        ],
        compiler_params=pltpu.CompilerParams(
            collective_id=0, has_side_effects=True, vmem_limit_bytes=48 * 2**20
        ),
        cost_estimate=pl.CostEstimate(
            flops=4 * n * half * depth * share,
            bytes_accessed=4 * n * half * share * 2,
            transcendentals=half * share,
        ),
    )(pool_taps, cot_taps, enc_mat, dec_mat)


def wide_shards(inputs, enc_weight, dec_weight, cotangent):
    parts = lax.axis_size("seq")
    rows, width = inputs.shape
    half = rows // 2
    total = half * parts
    block, taps, share = enc_weight.shape
    half_width = cotangent.shape[1]

    pooled = (inputs.astype(F32).reshape(half, 2, width).sum(axis=1) * 0.5).astype(BF16)
    cot_full = lax.all_gather(cotangent, "chan", axis=1, tiled=True)
    core = lax.axis_index("chan")
    cores = lax.axis_size("chan")
    few = half // cores
    leaving = jnp.concatenate(
        [
            lax.dynamic_slice_in_dim(pooled, core * few, few, 0),
            lax.dynamic_slice_in_dim(cot_full, core * 2 * few, 2 * few, 0),
        ],
        axis=0,
    )
    columns = to_columns(leaving, parts).reshape(parts, 1, 3 * few, block)
    columns = lax.all_gather(columns, "chan", axis=1, tiled=True)
    pool_col = columns[:, :, :few].reshape(total, block)
    cot_col = columns[:, :, few:].reshape(total, 2, block).astype(F32)
    even = cot_col[:, 0]
    odd = cot_col[:, 1]
    pair = (even + odd).astype(BF16)
    cross = (odd + shift(even, 1)).astype(BF16)
    before = jnp.concatenate([even[:1].astype(BF16), cross[:-1]], axis=0)
    pool_taps = jnp.concatenate([shift(pool_col, t - 2) for t in range(taps)], axis=1)
    cot_taps = jnp.concatenate([shift(pair, 1), cross, pair, before, shift(pair, -1)], axis=1)
    enc_mat = enc_weight.transpose(1, 0, 2).reshape(taps * block, share)
    dec_mat = dec_weight.transpose(1, 0, 2).reshape(taps * block, share)

    joint = ring(
        pool_taps.reshape(parts, half, taps * block),
        cot_taps.reshape(parts, half, taps * block),
        enc_mat,
        dec_mat,
        parts,
    ).reshape(total, 2 * share)
    hidden_all = joint[:, :share]
    grad_all = joint[:, share:]

    contract_rows = (((0,), (0,)), ((), ()))
    contract_last = (((1,), (1,)), ((), ()))
    dec_grad = lax.dot_general(cot_taps, hidden_all, contract_rows, preferred_element_type=F32)
    enc_grad = lax.dot_general(pool_taps, grad_all, contract_rows, preferred_element_type=F32)
    dec_grad = dec_grad.astype(BF16).reshape(taps, block, share).transpose(1, 0, 2)
    enc_grad = enc_grad.astype(BF16).reshape(taps, block, share).transpose(1, 0, 2)

    dec_out = lax.dot_general(hidden_all, dec_mat, contract_last, preferred_element_type=F32)
    p0, p1, p2, p3, p4 = [dec_out[:, t * block : (t + 1) * block] for t in range(taps)]
    after4 = shift(p4, 1)
    before0 = shift(p0, -1)
    dec_even = before0 + shift(p1, -1) + p2 + p3 + after4
    dec_odd = before0 + p1 + p2 + shift(p3, 1) + after4
    decoded = jnp.stack([dec_even, dec_odd], axis=1).astype(BF16).reshape(parts, rows, block)
    enc_out = lax.dot_general(grad_all, enc_mat, contract_last, preferred_element_type=F32)
    pool_grad = sum(shift(enc_out[:, t * block : (t + 1) * block], 2 - t) for t in range(taps))
    pool_grad = pool_grad.astype(BF16).reshape(parts, half, block)
    mine = jnp.concatenate([decoded, pool_grad], axis=1)
    mine = lax.psum_scatter(mine, "chan", scatter_dimension=1, tiled=True)
    mine = lax.all_gather(to_rows(mine), "chan", axis=0, tiled=True)
    col_start = core * half_width
    mine = lax.dynamic_slice_in_dim(mine, col_start, half_width, 1).astype(F32)

    skip = lax.dynamic_slice_in_dim(inputs, col_start, half_width, 1)
    mixed_out = (skip.astype(F32) + mine[:rows]).astype(BF16)
    input_grad = (cotangent.astype(F32) + 0.5 * jnp.repeat(mine[rows:], 2, axis=0)).astype(BF16)
    return mixed_out, input_grad, enc_grad, dec_grad


LANES = 128
HALO = 16
EDGE = 8


def pair_kernel(
    x_ref, enc_ref, dec_ref, cot_ref, mixed_ref, in_grad_ref, enc_grad_ref, dec_grad_ref,
    x_own, spread, pc_ref, rows_all, weights, folded, z_enc, z_dec, hid, slope, pre_grad, g_taps, h_taps,
    enc_sum, dec_sum, part, give, take, give_y, take_y, grad_give,
    local_sem, wy_send, wy_recv, wz_send, wz_recv, wx_send, wx_recv,
    edge_send, edge_z, edge_y, edge_c, edge_fwd, edge_ysend, edge_csend,
    own_send, pz_send, pz_recv, py_send, py_recv, pc_send, pc_recv,
    give_sem, take_sem, grad_sem, turn_sem,
):
    g = lax.axis_index("groups")
    s = lax.axis_index("seq")
    c = lax.axis_index("chan")
    z, y = s // 2, lax.rem(s, 2)
    last = lax.axis_size("seq") // 2 - 1
    chunk, wide = pc_ref.shape[1], pc_ref.shape[2]
    cell = 2 * chunk
    taps, block = enc_ref.shape[0], enc_ref.shape[1]
    share = enc_ref.shape[2] // 2
    half = block // 2
    inner = chunk - HALO
    ids = pl.DeviceIdType.MESH
    to_y, to_x, to_c = {"seq": s + 1 - 2 * y}, {"groups": 1 - g}, {"chan": 1 - c}
    to_left, to_right = {"seq": s - 2}, {"seq": s + 2}
    has_left, has_right = z > 0, z < last

    def lanes(index, width):
        return pl.ds(pl.multiple_of(index * width, LANES), width)

    own_x = pltpu.make_async_copy(x_ref.at[:, lanes(c, wide)], x_own, local_sem.at[0, taps + 1])
    own_x.start()
    sources = (enc_ref, dec_ref)
    grad_refs = (enc_grad_ref, dec_grad_ref)

    def own_weight(w, t):
        return pltpu.make_async_copy(
            sources[w].at[t, :, lanes(y, share)],
            weights.at[w, pl.ds(pl.multiple_of(s * block, HALO), block), pl.ds(t * share, share)],
            local_sem.at[w, t],
        )

    for w in range(2):
        for t in range(taps):
            own_weight(w, t).start()

    barrier = pltpu.get_barrier_semaphore()
    for where in (to_y, to_x, to_c):
        pl.semaphore_signal(barrier, inc=1, device_id=where, device_id_type=ids)

    @pl.when(has_left)
    def _():
        pl.semaphore_signal(barrier, inc=1, device_id=to_left, device_id_type=ids)

    @pl.when(has_right)
    def _():
        pl.semaphore_signal(barrier, inc=1, device_id=to_right, device_id_type=ids)

    inside = jnp.where(has_left, 1, 0) + jnp.where(has_right, 1, 0)
    pl.semaphore_wait(barrier, 3 + inside)

    def remote(src, dst, send, recv, where):
        return pltpu.make_async_remote_copy(
            src_ref=src, dst_ref=dst, send_sem=send, recv_sem=recv,
            device_id=where, device_id_type=ids,
        )

    def weight_to_y(w, t, side):
        at = pl.ds(pl.multiple_of(side * half, HALO), half)
        row = pl.multiple_of(s * block + side * half, HALO)
        return remote(
            sources[w].at[t, at, lanes(1 - y, share)],
            weights.at[w, pl.ds(row, half), pl.ds(t * share, share)],
            wy_send.at[w, t, side], wy_recv.at[w, t, side], to_y,
        )

    def slab(w, b, side):
        return weights.at[w, pl.ds(pl.multiple_of(b * block + side * half, HALO), half), :]

    def weight_z(w, zz, b, d, where):
        ref = slab(w, 2 * zz + b, g)
        return remote(ref, ref, wz_send.at[d, w, zz, b], wz_recv.at[w, zz, b], where)

    def weight_x(w, zz, b, side):
        ref = slab(w, 2 * zz + b, side)
        return remote(ref, ref, wx_send.at[w, zz, b], wx_recv.at[w, zz, b], to_x)

    def edge_of(zz, yy, cc):
        at = pl.multiple_of(HALO + (2 * zz + yy) * chunk + yy * inner, HALO)
        return rows_all.at[:, pl.ds(at, HALO), lanes(cc, wide)]

    def inner_of(i, zz, yy, cc):
        at = pl.multiple_of(HALO + (2 * zz + yy) * chunk + (1 - yy) * HALO, HALO)
        return rows_all.at[i, pl.ds(at, inner), lanes(cc, wide)]

    own_edge = pc_ref.at[:, pl.ds(pl.multiple_of(y * inner, HALO), HALO), :]

    def own_inner(i):
        return pc_ref.at[i, pl.ds(pl.multiple_of((1 - y) * HALO, HALO), inner), :]

    local_edge = pltpu.make_async_copy(own_edge, edge_of(z, y, c), local_sem.at[0, taps])
    local_inner = [
        pltpu.make_async_copy(own_inner(i), inner_of(i, z, y, c), local_sem.at[1, taps + i])
        for i in range(3)
    ]

    for w in range(2):
        for t in range(taps):
            weight_to_y(w, t, g).start()

    for w in range(2):
        for t in range(taps):
            own_weight(w, t).wait()

        @pl.when(has_left)
        def _():
            weight_z(w, z, y, 0, to_left).start()

        @pl.when(has_right)
        def _():
            weight_z(w, z, y, 1, to_right).start()

    def edge_out(d, where):
        return remote(own_edge, edge_of(z, y, c), edge_send.at[d], edge_z.at[z], where)

    def edge_forward(zz, where):
        ref = edge_of(zz, y, c)
        return remote(ref, ref, edge_fwd.at[zz], edge_z.at[zz], where)

    def edge_to_y(zz):
        src = edge_of(zz, y, c)
        return remote(src, src, edge_ysend.at[zz], edge_y.at[zz], to_y)

    def edge_to_c(zz, yy):
        ref = edge_of(zz, yy, c)
        return remote(ref, ref, edge_csend.at[zz, yy], edge_c.at[zz, yy], to_c)

    tiles = wide // LANES
    own_x.wait()
    for k in range(tiles):
        cols = slice(k * LANES, (k + 1) * LANES)
        spread[k] = x_own[:, cols].astype(F32)
        spread[tiles + k] = cot_ref[:, cols].astype(F32)
    for k in range(tiles):
        cols = slice(k * LANES, (k + 1) * LANES)
        even, odd = pl.ds(0, chunk, stride=2), pl.ds(1, chunk, stride=2)
        pc_ref[0, :, cols] = ((spread[k, even, :] + spread[k, odd, :]) * 0.5).astype(BF16)
        pc_ref[1, :, cols] = spread[tiles + k, even, :].astype(BF16)
        pc_ref[2, :, cols] = spread[tiles + k, odd, :].astype(BF16)

    local_edge.start()

    @pl.when(has_left)
    def _():
        edge_out(0, to_left).start()

    @pl.when(has_right)
    def _():
        edge_out(1, to_right).start()

    for copy in local_inner:
        copy.start()
    rows_all[:, :HALO, :] = jnp.zeros((3, HALO, 2 * wide), BF16)
    bottom = rows_all.shape[1] - HALO
    rows_all[:, bottom:, :] = jnp.zeros((3, HALO, 2 * wide), BF16)
    local_edge.wait()
    edge_to_y(z).start()
    edge_to_c(z, y).start()

    for w in range(2):
        for t in range(taps):
            weight_from_y(
                weights, sources, wy_send, wy_recv, w, t, g, s, y, half, block, share, to_y, lanes
            ).wait_recv()

        @pl.when(has_left)
        def _():
            weight_z(w, z, 1 - y, 0, to_left).start()

        @pl.when(has_right)
        def _():
            weight_z(w, z, 1 - y, 1, to_right).start()

    for w in range(2):
        for t in range(taps):
            weight_to_y(w, t, 1 - g).start()

    def inner_to_y(i, zz):
        ref = inner_of(i, zz, y, c)
        return remote(ref, ref, py_send.at[zz, i], py_recv.at[zz, i], to_y)

    def inner_to_c(i, zz, yy):
        ref = inner_of(i, zz, yy, c)
        return remote(ref, ref, pc_send.at[zz, yy, i], pc_recv.at[zz, yy, i], to_c)

    def inner_out(i, d, where):
        return remote(own_inner(i), inner_of(i, z, y, c), own_send.at[d, i], pz_recv.at[z, i], where)

    for i in range(3):
        local_inner[i].wait()
        inner_to_y(i, z).start()
        inner_to_c(i, z, y).start()

    def order(k):
        low = jnp.minimum(z, last - z)
        near = jnp.where(low == 0, k, jnp.where(k < 2, 1 - k, k))
        return jnp.where(z * 2 < last, near, last - near)

    def edge_arrives_y(zz):
        ref = edge_of(zz, 1 - y, c)
        return remote(ref, ref, edge_ysend.at[zz], edge_y.at[zz], to_y)

    def send_own_rows(d, where):
        for i in range(3):
            inner_out(i, d, where).start()

    @pl.when(z == 0)
    def _():
        send_own_rows(1, to_right)

    @pl.when(z == last)
    def _():
        send_own_rows(0, to_left)

    def weight_step(k, carry):
        for sign in (-1, 1):
            zz = z + sign * k

            @pl.when((zz >= 0) & (zz <= last))
            def _():
                for w in range(2):
                    for b in range(2):
                        weight_z(w, zz, b, 0, to_y).wait_recv()

                        if sign < 0:
                            @pl.when(has_right)
                            def _():
                                weight_z(w, zz, b, 1, to_right).start()
                        else:
                            @pl.when(has_left)
                            def _():
                                weight_z(w, zz, b, 0, to_left).start()

                        weight_x(w, zz, b, g).start()

                edge_forward(zz, to_y).wait_recv()
                if sign < 0:
                    @pl.when(has_right)
                    def _():
                        edge_forward(zz, to_right).start()
                else:
                    @pl.when(has_left)
                    def _():
                        edge_forward(zz, to_left).start()

                edge_to_y(zz).start()
                edge_to_c(zz, y).start()

        @pl.when((z == k) & has_right)
        def _():
            send_own_rows(1, to_right)

        @pl.when((last - z == k) & has_left)
        def _():
            send_own_rows(0, to_left)

        return carry

    lax.fori_loop(1, last + 1, weight_step, 0)

    def inner_forward(i, zz, where):
        ref = inner_of(i, zz, y, c)
        return remote(ref, ref, pz_send.at[zz, i], pz_recv.at[zz, i], where)

    def receive(i, zz):
        inner_forward(i, zz, to_y).wait_recv()

        @pl.when((zz < z) & has_right)
        def _():
            inner_forward(i, zz, to_right).start()

        @pl.when((zz > z) & has_left)
        def _():
            inner_forward(i, zz, to_left).start()

        @pl.when(jnp.logical_not(turns(i, zz)))
        def _():
            inner_to_y(i, zz).start()

        inner_to_c(i, zz, y).start()

    def edge_end(zz, carry):
        edge_arrives_y(zz).wait_recv()
        edge_to_c(zz, 1 - y).start()
        return carry

    lax.fori_loop(0, last + 1, edge_end, 0)

    corner = (z == 0) | (z == last)

    def turned(where):
        ref = inner_of(2, order(last), 1 - y, c)
        return remote(ref, ref, turn_sem.at[0], turn_sem.at[1], where)

    def turns(i, zz):
        return corner & (zz == order(last)) & (i == 2)

    def across(zz):
        for i in range(3):
            @pl.when(jnp.logical_not(turns(i, zz)))
            def _():
                ref = inner_of(i, zz, 1 - y, c)
                remote(ref, ref, py_send.at[zz, i], py_recv.at[zz, i], to_y).wait_recv()

            if i == 2:
                @pl.when(turns(i, zz))
                def _():
                    turned(to_y).wait_recv()

            inner_to_c(i, zz, 1 - y).start()

    across(z)
    middle = has_left & has_right

    def receive_step(k, carry):
        for i in range(3):
            receive(i, order(k))
        return carry

    lax.fori_loop(1, jnp.where(middle, last + 1, 2), receive_step, 0)

    for zz in range(last + 1):
        for yy in range(2):
            ref = edge_of(zz, yy, 1 - c)
            remote(ref, ref, edge_csend.at[zz, yy], edge_c.at[zz, yy], to_c).wait_recv()

    def each_other_cell(body):
        def step(k, carry):
            body(order(k))
            return carry

        lax.fori_loop(1, last + 1, step, 0)

    for w in range(2):
        for t in range(taps):
            weight_from_y(
                weights, sources, wy_send, wy_recv, w, t, 1 - g, s, y, half, block, share, to_y, lanes
            ).wait_recv()

    def wait_x(zz):
        for w in range(2):
            for b in range(2):
                weight_x(w, zz, b, 1 - g).wait_recv()

    each_other_cell(wait_x)

    step_rows = 64

    def fold(i, carry):
        at = pl.ds(pl.multiple_of(i * step_rows, HALO), step_rows)
        w = [weights[1, at, t * share : (t + 1) * share].astype(F32) for t in range(5)]
        folded[0, at, :share] = (w[0] + w[1]).astype(BF16)
        folded[0, at, share : 2 * share] = (w[2] + w[3]).astype(BF16)
        folded[0, at, 2 * share :] = weights[1, at, 4 * share :]
        folded[1, at, :share] = weights[1, at, :share]
        folded[1, at, share : 2 * share] = (w[1] + w[2]).astype(BF16)
        folded[1, at, 2 * share :] = (w[3] + w[4]).astype(BF16)
        return carry

    lax.fori_loop(0, weights.shape[1] // step_rows, fold, 0)

    contract_rows = (((0,), (0,)), ((), ()))
    contract_last = (((1,), (1,)), ((), ()))
    wide_rows = cell + 2 * HALO
    mid_rows = cell + 2 * EDGE
    window = pl.ds(pl.multiple_of((2 * block * z) // LANES * LANES, LANES), 2 * LANES)
    offset = 2 * block * z - (2 * block * z) // LANES * LANES

    enc_sum[...] = jnp.zeros_like(enc_sum)
    dec_sum[...] = jnp.zeros_like(dec_sum)

    def sums_over_cores():
        for i in range(3):
            total = part[i] + take[i].astype(F32)
            part[i] = total
            rows = pl.ds(pl.multiple_of((1 - y) * chunk, HALO), chunk)
            give_y[i] = part[i, rows, :].astype(BF16)

    give_copy = remote(give, take, give_sem.at[0], take_sem.at[0], to_c)
    give_y_copy = remote(give_y, take_y, give_sem.at[1], take_sem.at[1], to_y)

    def grad_copy(w):
        return remote(
            grad_give.at[w], grad_refs[w].at[:, :, lanes(y, share)], grad_sem.at[0, w], grad_sem.at[1, w], to_y
        )

    def grads(w, who):
        at = pl.ds(pl.multiple_of(offset + who * block, HALO), block)
        if w == 0:
            return [enc_sum[at, t * share : (t + 1) * share].astype(BF16) for t in range(5)]
        e = [dec_sum[0, at, k * share : (k + 1) * share] for k in range(3)]
        o = [dec_sum[1, at, k * share : (k + 1) * share] for k in range(3)]
        both = (e[0] + o[0], e[0] + o[1], e[1] + o[1], e[1] + o[2], e[2] + o[2])
        return [v.astype(BF16) for v in both]

    def give_grads(w):
        for t, value in enumerate(grads(w, 1 - y)):
            grad_give[w, t] = value
        grad_copy(w).start()

    def cell_step(k, carry):
        zz = order(k)

        def slot(when, q):
            @pl.when(when & ((z == 0) | (z == last)) & (q < 3 * (last - 1)))
            def _():
                receive(lax.rem(q, 3), order(2 + q // 3))

        for yy in range(2):
            for i in range(3):
                ref = inner_of(i, zz, yy, 1 - c)
                remote(ref, ref, pc_send.at[zz, yy, i], pc_recv.at[zz, yy, i], to_c).wait_recv()

        base = pl.multiple_of(zz * cell, HALO)
        at = pl.ds(base, wide_rows)
        product = jnp.dot(rows_all[0, at, :], weights[0], preferred_element_type=F32)
        for t in range(5 * tiles):
            z_enc[t] = product[:, t * LANES : (t + 1) * LANES]
        slot(k < 2, 3 * k)

        piece = mid_rows // 6
        product = jnp.dot(
            rows_all[1, at, :], folded[0], preferred_element_type=F32
        ) + jnp.dot(rows_all[2, at, :], folded[1], preferred_element_type=F32)
        for r in range(6):
            start = r * piece
            for q in range(tiles):
                pre = z_enc[q, pl.ds(start + 6, piece), :]
                for t in range(1, 5):
                    pre += z_enc[t * tiles + q, pl.ds(start + 6 + t, piece), :]
                value, up = gelu_and_slope(pre)
                row = lax.broadcasted_iota(jnp.int32, (piece, LANES), 0)
                if r == 0:
                    keep = (row >= EDGE) | (zz > 0)
                    value, up = jnp.where(keep, value, 0.0), jnp.where(keep, up, 0.0)
                if r == 5:
                    keep = (row < piece - EDGE) | (zz < last)
                    value, up = jnp.where(keep, value, 0.0), jnp.where(keep, up, 0.0)
                hid[q, pl.ds(start, piece), :] = value
                slope[q, pl.ds(start, piece), :] = up
        for r in range(cell // LANES):
            for q in range(tiles):
                for t in range(3):
                    moved = hid[q, pl.ds(r * LANES + EDGE - 1 + t, LANES), :]
                    h_taps[r * LANES : (r + 1) * LANES, t * share + q * LANES : t * share + (q + 1) * LANES] = (
                        moved.astype(BF16)
                    )
        for t in range(3 * tiles):
            z_dec[t] = product[:, t * LANES : (t + 1) * LANES]
        slot(k < 2, 3 * k + 1)

        body = pl.ds(base + HALO, cell)
        for i in range(2):
            dec_sum[i] += lax.dot_general(
                rows_all[1 + i, body, window], h_taps[...], contract_rows,
                preferred_element_type=F32,
            )
        for r in range(6):
            start = r * piece
            for q in range(tiles):
                grad = z_dec[q, pl.ds(start + 9, piece), :]
                for t in range(1, 3):
                    grad += z_dec[t * tiles + q, pl.ds(start + 9 - t, piece), :]
                pre_grad[q, pl.ds(start, piece), :] = grad * slope[q, pl.ds(start, piece), :]
        for r in range(cell // LANES):
            for q in range(tiles):
                for t in range(5):
                    moved = pre_grad[q, pl.ds(r * LANES + EDGE + 2 - t, LANES), :]
                    g_taps[r * LANES : (r + 1) * LANES, t * share + q * LANES : t * share + (q + 1) * LANES] = (
                        moved.astype(BF16)
                    )

        @pl.when((k < last - 1) | ((k < last) & corner))
        def _():
            across(order(k + 1))

        @pl.when((k == 1) & middle)
        def _():
            across(order(last))

            @pl.when(z * 2 < last)
            def _():
                turned(to_left).start()

            @pl.when(z * 2 > last)
            def _():
                turned(to_right).start()

        @pl.when(k == last)
        def _():
            give_grads(1)

        enc_sum[...] += lax.dot_general(
            rows_all[0, body, window], g_taps[...], contract_rows, preferred_element_type=F32
        )

        @pl.when(k == 0)
        def _():
            for i in range(3):
                for h in range(2):
                    cols = pl.ds(pl.multiple_of((c if h == 0 else 1 - c) * wide, LANES), wide)
                    rhs = weights[0, cols, :] if i == 0 else folded[i - 1, cols, :]
                    lhs = g_taps[...] if i == 0 else h_taps[...]
                    value = lax.dot_general(lhs, rhs, contract_last, preferred_element_type=F32)
                    if h == 0:
                        part[i] = value
                    else:
                        give[i] = value.astype(BF16)
                if i == 0:
                    slot(k == 0, 2)
            give_copy.start()

        slot(k == 1, 5)

        @pl.when(k == 1)
        def _():
            give_copy.wait_recv()
            sums_over_cores()
            give_y_copy.start()

        return carry

    lax.fori_loop(0, last + 1, cell_step, 0)

    give_grads(0)
    for w in range(2):
        for t, value in enumerate(grads(w, y)):
            grad_refs[w][t, :, lanes(y, share)] = value

    give_y_copy.wait_recv()
    for k in range(tiles):
        cols = slice(k * LANES, (k + 1) * LANES)
        even, odd = pl.ds(0, chunk, stride=2), pl.ds(1, chunk, stride=2)
        own = pl.ds(pl.multiple_of(y * chunk, HALO), chunk)
        pool_grad, first, second = [part[i, own, cols] + take_y[i, :, cols].astype(F32) for i in range(3)]
        spread[k, even, :] = first
        spread[k, odd, :] = second
        spread[tiles + k, even, :] = pool_grad
        spread[tiles + k, odd, :] = pool_grad
        mixed_ref[:, cols] = (x_own[:, cols].astype(F32) + spread[k]).astype(BF16)
        in_grad_ref[:, cols] = (cot_ref[:, cols].astype(F32) + 0.5 * spread[tiles + k]).astype(BF16)

    give_copy.wait_send()
    give_y_copy.wait_send()
    for w in range(2):
        for t in range(taps):
            weight_to_y(w, t, g).wait_send()
            weight_to_y(w, t, 1 - g).wait_send()

    @pl.when(has_left)
    def _():
        edge_out(0, to_left).wait_send()
        for i in range(3):
            inner_out(i, 0, to_left).wait_send()
        for w in range(2):
            for b in range(2):
                weight_z(w, z, b, 0, to_left).wait_send()

    @pl.when(has_right)
    def _():
        edge_out(1, to_right).wait_send()
        for i in range(3):
            inner_out(i, 1, to_right).wait_send()
        for w in range(2):
            for b in range(2):
                weight_z(w, z, b, 1, to_right).wait_send()

    def drain(k, carry):
        zz = order(k)
        edge_to_y(zz).wait_send()
        for yy in range(2):
            edge_to_c(zz, yy).wait_send()
        for i in range(3):
            @pl.when(jnp.logical_not(turns(i, zz)))
            def _():
                inner_to_y(i, zz).wait_send()

            for yy in range(2):
                inner_to_c(i, zz, yy).wait_send()

        @pl.when(k > 0)
        def _():
            for w in range(2):
                for b in range(2):
                    weight_x(w, zz, b, g).wait_send()

        @pl.when((zz < z) & has_right)
        def _():
            edge_forward(zz, to_right).wait_send()
            for i in range(3):
                inner_forward(i, zz, to_right).wait_send()
            for w in range(2):
                for b in range(2):
                    weight_z(w, zz, b, 1, to_right).wait_send()

        @pl.when((zz > z) & has_left)
        def _():
            edge_forward(zz, to_left).wait_send()
            for i in range(3):
                inner_forward(i, zz, to_left).wait_send()
            for w in range(2):
                for b in range(2):
                    weight_z(w, zz, b, 0, to_left).wait_send()

        return carry

    lax.fori_loop(0, last + 1, drain, 0)

    @pl.when(middle)
    def _():
        turned(to_y).wait_send()

    for w in range(2):
        grad_copy(w).wait_send()
    for w in range(2):
        grad_arrives = remote(
            grad_give.at[w], grad_refs[w].at[:, :, lanes(1 - y, share)],
            grad_sem.at[0, w], grad_sem.at[1, w], to_y,
        )
        grad_arrives.wait_recv()


def weight_from_y(weights, sources, send, recv, w, t, side, s, y, half, block, share, to_y, lanes):
    other = s + 1 - 2 * y
    row = pl.multiple_of(other * block + side * half, HALO)
    return pltpu.make_async_remote_copy(
        src_ref=sources[w].at[t, pl.ds(pl.multiple_of(side * half, HALO), half), lanes(1 - y, share)],
        dst_ref=weights.at[w, pl.ds(row, half), pl.ds(t * share, share)],
        send_sem=send.at[w, t, side],
        recv_sem=recv.at[w, t, side],
        device_id=to_y,
        device_id_type=pl.DeviceIdType.MESH,
    )


def pair_call(inputs, enc_taps, dec_taps, cotangent, cells):
    rows, wide = cotangent.shape
    chunk = rows // 2
    taps, block, both = enc_taps.shape
    share = both // 2
    cell = 2 * chunk
    vmem = pl.BlockSpec(memory_space=pltpu.VMEM)
    anywhere = pl.BlockSpec(memory_space=pl.ANY)
    dma = pltpu.SemaphoreType.DMA
    tall = cells * cell + 2 * HALO
    width = 2 * wide
    return pl.pallas_call(
        pair_kernel,
        out_shape=[
            jax.ShapeDtypeStruct((rows, wide), BF16),
            jax.ShapeDtypeStruct((rows, wide), BF16),
            jax.ShapeDtypeStruct((taps, block, both), BF16),
            jax.ShapeDtypeStruct((taps, block, both), BF16),
        ],
        in_specs=[anywhere, anywhere, anywhere, vmem],
        out_specs=[vmem] * 4,
        scratch_shapes=[
            pltpu.VMEM((rows, wide), BF16),
            pltpu.VMEM((2 * (wide // LANES), rows, LANES), F32),
            pltpu.VMEM((3, chunk, wide), BF16),
            pltpu.VMEM((3, tall, width), BF16),
            pltpu.VMEM((2, width, taps * share), BF16),
            pltpu.VMEM((2, width, 3 * share), BF16),
            pltpu.VMEM((taps * share // LANES, cell + 2 * HALO, LANES), F32),
            pltpu.VMEM((3 * share // LANES, cell + 2 * HALO, LANES), F32),
            pltpu.VMEM((share // LANES, cell + 2 * EDGE, LANES), F32),
            pltpu.VMEM((share // LANES, cell + 2 * EDGE, LANES), F32),
            pltpu.VMEM((share // LANES, cell + 2 * EDGE, LANES), F32),
            pltpu.VMEM((cell, taps * share), BF16),
            pltpu.VMEM((cell, 3 * share), BF16),
            pltpu.VMEM((2 * LANES, taps * share), F32),
            pltpu.VMEM((2, 2 * LANES, 3 * share), F32),
            pltpu.VMEM((3, cell, wide), F32),
            pltpu.VMEM((3, cell, wide), BF16),
            pltpu.VMEM((3, cell, wide), BF16),
            pltpu.VMEM((3, chunk, wide), BF16),
            pltpu.VMEM((3, chunk, wide), BF16),
            pltpu.VMEM((2, taps, block, share), BF16),
            dma((2, taps + 3)),
            dma((2, taps, 2)), dma((2, taps, 2)),
            dma((2, 2, cells, 2)), dma((2, cells, 2)), dma((2, cells, 2)), dma((2, cells, 2)),
            dma((2,)), dma((cells,)), dma((cells,)), dma((cells, 2)), dma((cells,)), dma((cells,)),
            dma((cells, 2)),
            dma((2, 3)), dma((cells, 3)), dma((cells, 3)), dma((cells, 3)), dma((cells, 3)),
            dma((cells, 2, 3)), dma((cells, 2, 3)),
            dma((2,)), dma((2,)), dma((2, 2)), dma((2,)),
        ],
        compiler_params=pltpu.CompilerParams(
            collective_id=0, has_side_effects=True, vmem_limit_bytes=58 * 2**20
        ),
        cost_estimate=pl.CostEstimate(
            flops=2 * 11 * cells * cell * width * share + 4 * 11 * cells * cell * block * share,
            bytes_accessed=4 * taps * block * both * 2,
            transcendentals=cells * cell * share,
        ),
    )(inputs, enc_taps, dec_taps, cotangent)


def settle_kernel(*refs):
    count = len(refs) // 3
    arrived, left = refs[3 * count :]
    for i in range(count):
        pltpu.make_async_copy(refs[i], refs[2 * count + i], arrived.at[i]).start()
    for i in range(count):
        pltpu.make_async_copy(refs[i], refs[2 * count + i], arrived.at[i]).wait()
        pltpu.make_async_copy(refs[2 * count + i], refs[count + i], left.at[i]).start()
    for i in range(count):
        pltpu.make_async_copy(refs[2 * count + i], refs[count + i], left.at[i]).wait()


def settle(arrays):
    anywhere = pl.BlockSpec(memory_space=pl.ANY)
    return pl.pallas_call(
        settle_kernel,
        out_shape=[jax.ShapeDtypeStruct(a.shape, a.dtype) for a in arrays],
        in_specs=[anywhere] * len(arrays),
        out_specs=[anywhere] * len(arrays),
        scratch_shapes=[pltpu.VMEM(a.shape, a.dtype) for a in arrays]
        + [pltpu.SemaphoreType.DMA((len(arrays),))] * 2,
    )(*arrays)


def shards(inputs, enc_weight, dec_weight, cotangent):
    parts = lax.axis_size("seq")
    cores = lax.axis_size("chan")
    rows, width = inputs.shape
    chunk = rows // 2
    block, taps, share = enc_weight.shape
    wide = cotangent.shape[1]
    fits = parts == 8 and cores == 2 and lax.axis_size("groups") == 2 and taps == 5
    fits = fits and block == 96 and share == 2 * wide and wide % LANES == 0 and chunk == 256
    if not fits:
        return wide_shards(inputs, enc_weight, dec_weight, cotangent)
    found = pair_call(
        inputs, enc_weight.transpose(1, 0, 2), dec_weight.transpose(1, 0, 2), cotangent, parts // 2
    )
    mixed_out, input_grad, enc_grad, dec_grad = settle(found)
    return mixed_out, input_grad, enc_grad.transpose(1, 0, 2), dec_grad.transpose(1, 0, 2)


def solution(mesh):
    return jax.shard_map(
        shards,
        mesh=mesh,
        in_specs=(
            P(("groups", "seq"), None),
            P("seq", None, "chan"),
            P("seq", None, "chan"),
            P(("groups", "seq"), "chan"),
        ),
        out_specs=(
            P(("groups", "seq"), "chan"),
            P(("groups", "seq"), "chan"),
            P(("groups", "seq"), None, "chan"),
            P(("groups", "seq"), None, "chan"),
        ),
        check_vma=False,
    )
```

```python
import functools
import math

import jax
import jax.numpy as jnp
from jax import lax
from jax.experimental import pallas as pl
from jax.experimental.pallas import tpu as pltpu
from jax.sharding import PartitionSpec as P

BF16 = jnp.bfloat16
F32 = jnp.float32


def shift(array, by):
    length = array.shape[0]
    if by == 0:
        return array
    pad = jnp.zeros((abs(by),) + array.shape[1:], array.dtype)
    if by > 0:
        return jnp.concatenate([array[by:], pad], axis=0)
    return jnp.concatenate([pad, array[: length + by]], axis=0)


def to_columns(array, parts):
    rows, cols = array.shape
    blocks = array.reshape(rows, parts, cols // parts).transpose(1, 0, 2)
    return lax.all_to_all(blocks, "seq", 0, 0, tiled=True)


def to_rows(blocks):
    parts, rows, cols = blocks.shape
    got = lax.all_to_all(blocks, "seq", 0, 0, tiled=True)
    return got.transpose(1, 0, 2).reshape(rows, parts * cols)


PIECES = 2


def ring_place(index, n):
    if n != 8:
        return index
    y = lax.rem(index, 2)
    z = index // 2
    return z + y * (n - 1 - 2 * z)


def ring_index(place, n):
    place = lax.rem(place + 2 * n, n)
    if n != 8:
        return place
    back = place // (n // 2)
    return 2 * place + back * (2 * n - 1 - 4 * place)


def gelu_and_slope(v):
    scale = math.sqrt(2.0 / math.pi)
    square = v * v
    th = jnp.tanh(scale * (v + 0.044715 * square * v))
    up = 0.5 * (1.0 + th)
    slope = up + 0.5 * v * (1.0 - th * th) * (scale * (1.0 + 3.0 * 0.044715 * square))
    return v * up, slope


def ring_kernel(
    n, x_ref, y_ref, enc_ref, dec_ref, out_ref, slots, term, mine,
    rs_send, rs_recv, ag_send, ag_recv, local_sem,
):
    me = lax.axis_index("seq")
    place = ring_place(me, n)
    nexts = (ring_index(place + 1, n), ring_index(place - 1, n))
    half = x_ref.shape[1]
    share = enc_ref.shape[1]
    side = half // 2
    piece = side // PIECES

    barrier = pltpu.get_barrier_semaphore()
    for other in nexts:
        pl.semaphore_signal(
            barrier, inc=1, device_id={"seq": other}, device_id_type=pl.DeviceIdType.MESH
        )
    pl.semaphore_wait(barrier, 2)

    def signed(d, steps):
        return place - steps if d == 0 else place + steps

    def own_term(d, steps):
        chunk = ring_index(signed(d, steps), n)
        at = pl.ds(d * side, side)
        a = jnp.dot(x_ref[chunk, at, :], enc_ref[...], preferred_element_type=jnp.float32)
        b = jnp.dot(y_ref[chunk, at, :], dec_ref[...], preferred_element_type=jnp.float32)
        return a, b

    def rs_copy(d, s, q):
        at = pl.ds(q * piece, piece)
        return pltpu.make_async_remote_copy(
            src_ref=slots.at[d, s, at],
            dst_ref=slots.at[d, s + 1, at],
            send_sem=rs_send.at[d, s, q],
            recv_sem=rs_recv.at[d, s, q],
            device_id={"seq": nexts[d]},
            device_id_type=pl.DeviceIdType.MESH,
        )

    def ag_copy(d, s, q, first):
        at = pl.ds(d * side + q * piece, piece)
        owner = ring_index(signed(d, s), n)
        return pltpu.make_async_remote_copy(
            src_ref=mine.at[at] if first else out_ref.at[owner, at],
            dst_ref=out_ref.at[owner, at],
            send_sem=ag_send.at[d, s, q],
            recv_sem=ag_recv.at[d, s, q],
            device_id={"seq": nexts[d]},
            device_id_type=pl.DeviceIdType.MESH,
        )

    for d in range(2):
        a, b = own_term(d, 1)
        slots[d, 0, :, :share] = a.astype(BF16)
        slots[d, 0, :, share:] = b.astype(BF16)
        for q in range(PIECES):
            rs_copy(d, 0, q).start()

    def fill(s):
        for d in range(2):
            a, b = own_term(d, s + 2)
            term[d, :, :share] = a
            term[d, :, share:] = b

    def rs_step(s, carry):
        fill(s)
        for q in range(PIECES):
            at = pl.ds(q * piece, piece)
            for d in range(2):
                rs_copy(d, s, q).wait_recv()
                total = slots[d, s + 1, at, :].astype(F32) + term[d, at, :]
                slots[d, s + 1, at, :] = total.astype(BF16)
                rs_copy(d, s + 1, q).start()
        return carry

    lax.fori_loop(0, n - 2, rs_step, 0)
    fill(n - 2)
    for q in range(PIECES):
        at = pl.ds(q * piece, piece)
        for d in range(2):
            rs_copy(d, n - 2, q).wait_recv()
            rows = pl.ds(d * side + q * piece, piece)
            pre = slots[d, n - 1, at, :share].astype(F32) + term[d, at, :share]
            grad = slots[d, n - 1, at, share:].astype(F32) + term[d, at, share:]
            value, slope = gelu_and_slope(pre)
            mine[rows, :share] = value.astype(BF16)
            mine[rows, share:] = (grad * slope).astype(BF16)
            ag_copy(d, 0, q, True).start()
    local = pltpu.make_async_copy(mine, out_ref.at[me], local_sem)
    local.start()

    def ag_step(s, carry):
        for q in range(PIECES):
            for d in range(2):
                incoming(d, s, q).wait_recv()
                ag_copy(d, s + 1, q, False).start()
        return carry

    def incoming(d, s, q):
        at = pl.ds(d * side + q * piece, piece)
        owner = ring_index(signed(d, s + 1), n)
        return pltpu.make_async_remote_copy(
            src_ref=mine.at[at],
            dst_ref=out_ref.at[owner, at],
            send_sem=ag_send.at[d, s, q],
            recv_sem=ag_recv.at[d, s, q],
            device_id={"seq": nexts[d]},
            device_id_type=pl.DeviceIdType.MESH,
        )

    lax.fori_loop(0, n - 2, ag_step, 0)
    for q in range(PIECES):
        for d in range(2):
            incoming(d, n - 2, q).wait_recv()

    def drain(s, carry):
        for q in range(PIECES):
            for d in range(2):
                rs_copy(d, s, q).wait_send()
                ag_copy(d, s, q, True).wait_send()
        return carry

    lax.fori_loop(0, n - 1, drain, 0)
    local.wait()


def ring(pool_taps, cot_taps, enc_mat, dec_mat, n):
    half = pool_taps.shape[1]
    share = enc_mat.shape[1]
    depth = enc_mat.shape[0]
    vmem = pl.BlockSpec(memory_space=pltpu.VMEM)
    steps = (2, n - 1, PIECES)
    return pl.pallas_call(
        functools.partial(ring_kernel, n),
        out_shape=jax.ShapeDtypeStruct((n, half, 2 * share), BF16),
        in_specs=[vmem] * 4,
        out_specs=pl.BlockSpec(memory_space=pl.ANY),
        scratch_shapes=[
            pltpu.VMEM((2, n, half // 2, 2 * share), BF16),
            pltpu.VMEM((2, half // 2, 2 * share), F32),
            pltpu.VMEM((half, 2 * share), BF16),
            pltpu.SemaphoreType.DMA(steps),
            pltpu.SemaphoreType.DMA(steps),
            pltpu.SemaphoreType.DMA(steps),
            pltpu.SemaphoreType.DMA(steps),
            pltpu.SemaphoreType.DMA,
        ],
        compiler_params=pltpu.CompilerParams(
            collective_id=0, has_side_effects=True, vmem_limit_bytes=48 * 2**20
        ),
        cost_estimate=pl.CostEstimate(
            flops=4 * n * half * depth * share,
            bytes_accessed=4 * n * half * share * 2,
            transcendentals=half * share,
        ),
    )(pool_taps, cot_taps, enc_mat, dec_mat)


def wide_shards(inputs, enc_weight, dec_weight, cotangent):
    parts = lax.axis_size("seq")
    rows, width = inputs.shape
    half = rows // 2
    total = half * parts
    block, taps, share = enc_weight.shape
    half_width = cotangent.shape[1]

    pooled = (inputs.astype(F32).reshape(half, 2, width).sum(axis=1) * 0.5).astype(BF16)
    cot_full = lax.all_gather(cotangent, "chan", axis=1, tiled=True)
    core = lax.axis_index("chan")
    cores = lax.axis_size("chan")
    few = half // cores
    leaving = jnp.concatenate(
        [
            lax.dynamic_slice_in_dim(pooled, core * few, few, 0),
            lax.dynamic_slice_in_dim(cot_full, core * 2 * few, 2 * few, 0),
        ],
        axis=0,
    )
    columns = to_columns(leaving, parts).reshape(parts, 1, 3 * few, block)
    columns = lax.all_gather(columns, "chan", axis=1, tiled=True)
    pool_col = columns[:, :, :few].reshape(total, block)
    cot_col = columns[:, :, few:].reshape(total, 2, block).astype(F32)
    even = cot_col[:, 0]
    odd = cot_col[:, 1]
    pair = (even + odd).astype(BF16)
    cross = (odd + shift(even, 1)).astype(BF16)
    before = jnp.concatenate([even[:1].astype(BF16), cross[:-1]], axis=0)
    pool_taps = jnp.concatenate([shift(pool_col, t - 2) for t in range(taps)], axis=1)
    cot_taps = jnp.concatenate([shift(pair, 1), cross, pair, before, shift(pair, -1)], axis=1)
    enc_mat = enc_weight.transpose(1, 0, 2).reshape(taps * block, share)
    dec_mat = dec_weight.transpose(1, 0, 2).reshape(taps * block, share)

    joint = ring(
        pool_taps.reshape(parts, half, taps * block),
        cot_taps.reshape(parts, half, taps * block),
        enc_mat,
        dec_mat,
        parts,
    ).reshape(total, 2 * share)
    hidden_all = joint[:, :share]
    grad_all = joint[:, share:]

    contract_rows = (((0,), (0,)), ((), ()))
    contract_last = (((1,), (1,)), ((), ()))
    dec_grad = lax.dot_general(cot_taps, hidden_all, contract_rows, preferred_element_type=F32)
    enc_grad = lax.dot_general(pool_taps, grad_all, contract_rows, preferred_element_type=F32)
    dec_grad = dec_grad.astype(BF16).reshape(taps, block, share).transpose(1, 0, 2)
    enc_grad = enc_grad.astype(BF16).reshape(taps, block, share).transpose(1, 0, 2)

    dec_out = lax.dot_general(hidden_all, dec_mat, contract_last, preferred_element_type=F32)
    p0, p1, p2, p3, p4 = [dec_out[:, t * block : (t + 1) * block] for t in range(taps)]
    after4 = shift(p4, 1)
    before0 = shift(p0, -1)
    dec_even = before0 + shift(p1, -1) + p2 + p3 + after4
    dec_odd = before0 + p1 + p2 + shift(p3, 1) + after4
    decoded = jnp.stack([dec_even, dec_odd], axis=1).astype(BF16).reshape(parts, rows, block)
    enc_out = lax.dot_general(grad_all, enc_mat, contract_last, preferred_element_type=F32)
    pool_grad = sum(shift(enc_out[:, t * block : (t + 1) * block], 2 - t) for t in range(taps))
    pool_grad = pool_grad.astype(BF16).reshape(parts, half, block)
    mine = jnp.concatenate([decoded, pool_grad], axis=1)
    mine = lax.psum_scatter(mine, "chan", scatter_dimension=1, tiled=True)
    mine = lax.all_gather(to_rows(mine), "chan", axis=0, tiled=True)
    col_start = core * half_width
    mine = lax.dynamic_slice_in_dim(mine, col_start, half_width, 1).astype(F32)

    skip = lax.dynamic_slice_in_dim(inputs, col_start, half_width, 1)
    mixed_out = (skip.astype(F32) + mine[:rows]).astype(BF16)
    input_grad = (cotangent.astype(F32) + 0.5 * jnp.repeat(mine[rows:], 2, axis=0)).astype(BF16)
    return mixed_out, input_grad, enc_grad, dec_grad


LANES = 128
HALO = 16
EDGE = 8


def pair_kernel(
    x_ref, enc_ref, dec_ref, cot_ref, mixed_ref, in_grad_ref, enc_grad_ref, dec_grad_ref,
    x_own, spread, pc_ref, rows_all, weights, folded, z_enc, z_dec, hid, slope, pre_grad, g_taps, h_taps,
    enc_sum, dec_sum, part, give, take, give_y, take_y, grad_give,
    local_sem, wy_send, wy_recv, wz_send, wz_recv, wx_send, wx_recv,
    edge_send, edge_z, edge_y, edge_c, edge_fwd, edge_ysend, edge_csend,
    own_send, pz_send, pz_recv, py_send, py_recv, pc_send, pc_recv,
    give_sem, take_sem, grad_sem, turn_sem,
):
    g = lax.axis_index("groups")
    s = lax.axis_index("seq")
    c = lax.axis_index("chan")
    z, y = s // 2, lax.rem(s, 2)
    last = lax.axis_size("seq") // 2 - 1
    chunk, wide = pc_ref.shape[1], pc_ref.shape[2]
    cell = 2 * chunk
    taps, block = enc_ref.shape[0], enc_ref.shape[1]
    share = enc_ref.shape[2] // 2
    half = block // 2
    inner = chunk - HALO
    ids = pl.DeviceIdType.MESH
    to_y, to_x, to_c = {"seq": s + 1 - 2 * y}, {"groups": 1 - g}, {"chan": 1 - c}
    to_left, to_right = {"seq": s - 2}, {"seq": s + 2}
    has_left, has_right = z > 0, z < last

    def lanes(index, width):
        return pl.ds(pl.multiple_of(index * width, LANES), width)

    own_x = pltpu.make_async_copy(x_ref.at[:, lanes(c, wide)], x_own, local_sem.at[0, taps + 1])
    own_x.start()
    sources = (enc_ref, dec_ref)
    grad_refs = (enc_grad_ref, dec_grad_ref)

    def own_weight(w, t):
        return pltpu.make_async_copy(
            sources[w].at[t, :, lanes(y, share)],
            weights.at[w, pl.ds(pl.multiple_of(s * block, HALO), block), pl.ds(t * share, share)],
            local_sem.at[w, t],
        )

    for w in range(2):
        for t in range(taps):
            own_weight(w, t).start()

    barrier = pltpu.get_barrier_semaphore()
    for where in (to_y, to_x, to_c):
        pl.semaphore_signal(barrier, inc=1, device_id=where, device_id_type=ids)

    @pl.when(has_left)
    def _():
        pl.semaphore_signal(barrier, inc=1, device_id=to_left, device_id_type=ids)

    @pl.when(has_right)
    def _():
        pl.semaphore_signal(barrier, inc=1, device_id=to_right, device_id_type=ids)

    inside = jnp.where(has_left, 1, 0) + jnp.where(has_right, 1, 0)
    pl.semaphore_wait(barrier, 3 + inside)

    def remote(src, dst, send, recv, where):
        return pltpu.make_async_remote_copy(
            src_ref=src, dst_ref=dst, send_sem=send, recv_sem=recv,
            device_id=where, device_id_type=ids,
        )

    def weight_to_y(w, t, side):
        at = pl.ds(pl.multiple_of(side * half, HALO), half)
        row = pl.multiple_of(s * block + side * half, HALO)
        return remote(
            sources[w].at[t, at, lanes(1 - y, share)],
            weights.at[w, pl.ds(row, half), pl.ds(t * share, share)],
            wy_send.at[w, t, side], wy_recv.at[w, t, side], to_y,
        )

    def slab(w, b, side):
        return weights.at[w, pl.ds(pl.multiple_of(b * block + side * half, HALO), half), :]

    def weight_z(w, zz, b, d, where):
        ref = slab(w, 2 * zz + b, g)
        return remote(ref, ref, wz_send.at[d, w, zz, b], wz_recv.at[w, zz, b], where)

    def weight_x(w, zz, b, side):
        ref = slab(w, 2 * zz + b, side)
        return remote(ref, ref, wx_send.at[w, zz, b], wx_recv.at[w, zz, b], to_x)

    def edge_of(zz, yy, cc):
        at = pl.multiple_of(HALO + (2 * zz + yy) * chunk + yy * inner, HALO)
        return rows_all.at[:, pl.ds(at, HALO), lanes(cc, wide)]

    def inner_of(i, zz, yy, cc):
        at = pl.multiple_of(HALO + (2 * zz + yy) * chunk + (1 - yy) * HALO, HALO)
        return rows_all.at[i, pl.ds(at, inner), lanes(cc, wide)]

    own_edge = pc_ref.at[:, pl.ds(pl.multiple_of(y * inner, HALO), HALO), :]

    def own_inner(i):
        return pc_ref.at[i, pl.ds(pl.multiple_of((1 - y) * HALO, HALO), inner), :]

    local_edge = pltpu.make_async_copy(own_edge, edge_of(z, y, c), local_sem.at[0, taps])
    local_inner = [
        pltpu.make_async_copy(own_inner(i), inner_of(i, z, y, c), local_sem.at[1, taps + i])
        for i in range(3)
    ]

    for w in range(2):
        for t in range(taps):
            weight_to_y(w, t, g).start()

    for w in range(2):
        for t in range(taps):
            own_weight(w, t).wait()

        @pl.when(has_left)
        def _():
            weight_z(w, z, y, 0, to_left).start()

        @pl.when(has_right)
        def _():
            weight_z(w, z, y, 1, to_right).start()

    def edge_out(d, where):
        return remote(own_edge, edge_of(z, y, c), edge_send.at[d], edge_z.at[z], where)

    def edge_forward(zz, where):
        ref = edge_of(zz, y, c)
        return remote(ref, ref, edge_fwd.at[zz], edge_z.at[zz], where)

    def edge_to_y(zz):
        src = edge_of(zz, y, c)
        return remote(src, src, edge_ysend.at[zz], edge_y.at[zz], to_y)

    def edge_to_c(zz, yy):
        ref = edge_of(zz, yy, c)
        return remote(ref, ref, edge_csend.at[zz, yy], edge_c.at[zz, yy], to_c)

    tiles = wide // LANES
    own_x.wait()
    for k in range(tiles):
        cols = slice(k * LANES, (k + 1) * LANES)
        spread[k] = x_own[:, cols].astype(F32)
        spread[tiles + k] = cot_ref[:, cols].astype(F32)
    for k in range(tiles):
        cols = slice(k * LANES, (k + 1) * LANES)
        even, odd = pl.ds(0, chunk, stride=2), pl.ds(1, chunk, stride=2)
        pc_ref[0, :, cols] = ((spread[k, even, :] + spread[k, odd, :]) * 0.5).astype(BF16)
        pc_ref[1, :, cols] = spread[tiles + k, even, :].astype(BF16)
        pc_ref[2, :, cols] = spread[tiles + k, odd, :].astype(BF16)

    local_edge.start()

    @pl.when(has_left)
    def _():
        edge_out(0, to_left).start()

    @pl.when(has_right)
    def _():
        edge_out(1, to_right).start()

    for copy in local_inner:
        copy.start()
    rows_all[:, :HALO, :] = jnp.zeros((3, HALO, 2 * wide), BF16)
    bottom = rows_all.shape[1] - HALO
    rows_all[:, bottom:, :] = jnp.zeros((3, HALO, 2 * wide), BF16)
    local_edge.wait()
    edge_to_y(z).start()
    edge_to_c(z, y).start()

    for w in range(2):
        for t in range(taps):
            weight_from_y(
                weights, sources, wy_send, wy_recv, w, t, g, s, y, half, block, share, to_y, lanes
            ).wait_recv()

        @pl.when(has_left)
        def _():
            weight_z(w, z, 1 - y, 0, to_left).start()

        @pl.when(has_right)
        def _():
            weight_z(w, z, 1 - y, 1, to_right).start()

    for w in range(2):
        for t in range(taps):
            weight_to_y(w, t, 1 - g).start()

    def inner_to_y(i, zz):
        ref = inner_of(i, zz, y, c)
        return remote(ref, ref, py_send.at[zz, i], py_recv.at[zz, i], to_y)

    def inner_to_c(i, zz, yy):
        ref = inner_of(i, zz, yy, c)
        return remote(ref, ref, pc_send.at[zz, yy, i], pc_recv.at[zz, yy, i], to_c)

    def inner_out(i, d, where):
        return remote(own_inner(i), inner_of(i, z, y, c), own_send.at[d, i], pz_recv.at[z, i], where)

    for i in range(3):
        local_inner[i].wait()
        inner_to_y(i, z).start()
        inner_to_c(i, z, y).start()

    def order(k):
        low = jnp.minimum(z, last - z)
        near = jnp.where(low == 0, k, jnp.where(k < 2, 1 - k, k))
        return jnp.where(z * 2 < last, near, last - near)

    def edge_arrives_y(zz):
        ref = edge_of(zz, 1 - y, c)
        return remote(ref, ref, edge_ysend.at[zz], edge_y.at[zz], to_y)

    def send_own_rows(d, where):
        for i in range(3):
            inner_out(i, d, where).start()

    @pl.when(z == 0)
    def _():
        send_own_rows(1, to_right)

    @pl.when(z == last)
    def _():
        send_own_rows(0, to_left)

    def weight_step(k, carry):
        for sign in (-1, 1):
            zz = z + sign * k

            @pl.when((zz >= 0) & (zz <= last))
            def _():
                for w in range(2):
                    for b in range(2):
                        weight_z(w, zz, b, 0, to_y).wait_recv()

                        if sign < 0:
                            @pl.when(has_right)
                            def _():
                                weight_z(w, zz, b, 1, to_right).start()
                        else:
                            @pl.when(has_left)
                            def _():
                                weight_z(w, zz, b, 0, to_left).start()

                        weight_x(w, zz, b, g).start()

                edge_forward(zz, to_y).wait_recv()
                if sign < 0:
                    @pl.when(has_right)
                    def _():
                        edge_forward(zz, to_right).start()
                else:
                    @pl.when(has_left)
                    def _():
                        edge_forward(zz, to_left).start()

                edge_to_y(zz).start()
                edge_to_c(zz, y).start()

        @pl.when((z == k) & has_right)
        def _():
            send_own_rows(1, to_right)

        @pl.when((last - z == k) & has_left)
        def _():
            send_own_rows(0, to_left)

        return carry

    lax.fori_loop(1, last + 1, weight_step, 0)

    def inner_forward(i, zz, where):
        ref = inner_of(i, zz, y, c)
        return remote(ref, ref, pz_send.at[zz, i], pz_recv.at[zz, i], where)

    def receive(i, zz):
        inner_forward(i, zz, to_y).wait_recv()

        @pl.when((zz < z) & has_right)
        def _():
            inner_forward(i, zz, to_right).start()

        @pl.when((zz > z) & has_left)
        def _():
            inner_forward(i, zz, to_left).start()

        @pl.when(jnp.logical_not(turns(i, zz)))
        def _():
            inner_to_y(i, zz).start()

        inner_to_c(i, zz, y).start()

    def edge_end(zz, carry):
        edge_arrives_y(zz).wait_recv()
        edge_to_c(zz, 1 - y).start()
        return carry

    lax.fori_loop(0, last + 1, edge_end, 0)

    corner = (z == 0) | (z == last)

    def turned(where):
        ref = inner_of(2, order(last), 1 - y, c)
        return remote(ref, ref, turn_sem.at[0], turn_sem.at[1], where)

    def turns(i, zz):
        return corner & (zz == order(last)) & (i == 2)

    def across(i, zz):
        @pl.when(jnp.logical_not(turns(i, zz)))
        def _():
            ref = inner_of(i, zz, 1 - y, c)
            remote(ref, ref, py_send.at[zz, i], py_recv.at[zz, i], to_y).wait_recv()

        if i == 2:
            @pl.when(turns(i, zz))
            def _():
                turned(to_y).wait_recv()

        inner_to_c(i, zz, 1 - y).start()

    across(0, z)
    middle = has_left & has_right

    def receive_step(k, carry):
        for i in range(3):
            receive(i, order(k))
        return carry

    lax.fori_loop(1, jnp.where(middle, last + 1, 2), receive_step, 0)

    for zz in range(last + 1):
        for yy in range(2):
            ref = edge_of(zz, yy, 1 - c)
            remote(ref, ref, edge_csend.at[zz, yy], edge_c.at[zz, yy], to_c).wait_recv()

    def each_other_cell(body):
        def step(k, carry):
            body(order(k))
            return carry

        lax.fori_loop(1, last + 1, step, 0)

    for w in range(2):
        for t in range(taps):
            weight_from_y(
                weights, sources, wy_send, wy_recv, w, t, 1 - g, s, y, half, block, share, to_y, lanes
            ).wait_recv()

    def wait_x(zz):
        for w in range(2):
            for b in range(2):
                weight_x(w, zz, b, 1 - g).wait_recv()

    each_other_cell(wait_x)

    step_rows = 64

    def fold(i, carry):
        at = pl.ds(pl.multiple_of(i * step_rows, HALO), step_rows)
        w = [weights[1, at, t * share : (t + 1) * share].astype(F32) for t in range(5)]
        folded[0, at, :share] = (w[0] + w[1]).astype(BF16)
        folded[0, at, share : 2 * share] = (w[2] + w[3]).astype(BF16)
        folded[0, at, 2 * share :] = weights[1, at, 4 * share :]
        folded[1, at, :share] = weights[1, at, :share]
        folded[1, at, share : 2 * share] = (w[1] + w[2]).astype(BF16)
        folded[1, at, 2 * share :] = (w[3] + w[4]).astype(BF16)
        return carry

    lax.fori_loop(0, weights.shape[1] // step_rows, fold, 0)

    contract_rows = (((0,), (0,)), ((), ()))
    contract_last = (((1,), (1,)), ((), ()))
    wide_rows = cell + 2 * HALO
    mid_rows = cell + 2 * EDGE
    window = pl.ds(pl.multiple_of((2 * block * z) // LANES * LANES, LANES), 2 * LANES)
    offset = 2 * block * z - (2 * block * z) // LANES * LANES

    enc_sum[...] = jnp.zeros_like(enc_sum)
    dec_sum[...] = jnp.zeros_like(dec_sum)

    def sums_over_cores():
        for i in range(3):
            total = part[i] + take[i].astype(F32)
            part[i] = total
            rows = pl.ds(pl.multiple_of((1 - y) * chunk, HALO), chunk)
            give_y[i] = part[i, rows, :].astype(BF16)

    give_copy = remote(give, take, give_sem.at[0], take_sem.at[0], to_c)
    give_y_copy = remote(give_y, take_y, give_sem.at[1], take_sem.at[1], to_y)

    def grad_copy(w):
        return remote(
            grad_give.at[w], grad_refs[w].at[:, :, lanes(y, share)], grad_sem.at[0, w], grad_sem.at[1, w], to_y
        )

    def grads(w, who):
        at = pl.ds(pl.multiple_of(offset + who * block, HALO), block)
        if w == 0:
            return [enc_sum[at, t * share : (t + 1) * share].astype(BF16) for t in range(5)]
        e = [dec_sum[0, at, k * share : (k + 1) * share] for k in range(3)]
        o = [dec_sum[1, at, k * share : (k + 1) * share] for k in range(3)]
        both = (e[0] + o[0], e[0] + o[1], e[1] + o[1], e[1] + o[2], e[2] + o[2])
        return [v.astype(BF16) for v in both]

    def give_grads(w):
        for t, value in enumerate(grads(w, 1 - y)):
            grad_give[w, t] = value
        grad_copy(w).start()

    def cell_step(k, carry):
        zz = order(k)

        def slot(when, q):
            @pl.when(when & ((z == 0) | (z == last)) & (q < 3 * (last - 1)))
            def _():
                receive(lax.rem(q, 3), order(2 + q // 3))

        def landed(i):
            for yy in range(2):
                ref = inner_of(i, zz, yy, 1 - c)
                remote(ref, ref, pc_send.at[zz, yy, i], pc_recv.at[zz, yy, i], to_c).wait_recv()

        across(1, zz)
        landed(0)

        base = pl.multiple_of(zz * cell, HALO)
        at = pl.ds(base, wide_rows)
        product = jnp.dot(rows_all[0, at, :], weights[0], preferred_element_type=F32)
        for t in range(5 * tiles):
            z_enc[t] = product[:, t * LANES : (t + 1) * LANES]
        slot(k < 2, 3 * k)

        @pl.when((k < last) | corner)
        def _():
            across(2, zz)

        landed(1)
        product = jnp.dot(rows_all[1, at, :], folded[0], preferred_element_type=F32)
        for t in range(3 * tiles):
            z_dec[t] = product[:, t * LANES : (t + 1) * LANES]
        landed(2)

        piece = mid_rows // 6
        product = jnp.dot(rows_all[2, at, :], folded[1], preferred_element_type=F32)
        for r in range(6):
            start = r * piece
            for q in range(tiles):
                pre = z_enc[q, pl.ds(start + 6, piece), :]
                for t in range(1, 5):
                    pre += z_enc[t * tiles + q, pl.ds(start + 6 + t, piece), :]
                value, up = gelu_and_slope(pre)
                row = lax.broadcasted_iota(jnp.int32, (piece, LANES), 0)
                if r == 0:
                    keep = (row >= EDGE) | (zz > 0)
                    value, up = jnp.where(keep, value, 0.0), jnp.where(keep, up, 0.0)
                if r == 5:
                    keep = (row < piece - EDGE) | (zz < last)
                    value, up = jnp.where(keep, value, 0.0), jnp.where(keep, up, 0.0)
                hid[q, pl.ds(start, piece), :] = value
                slope[q, pl.ds(start, piece), :] = up
        for r in range(cell // LANES):
            for q in range(tiles):
                for t in range(3):
                    moved = hid[q, pl.ds(r * LANES + EDGE - 1 + t, LANES), :]
                    h_taps[r * LANES : (r + 1) * LANES, t * share + q * LANES : t * share + (q + 1) * LANES] = (
                        moved.astype(BF16)
                    )
        for t in range(3 * tiles):
            z_dec[t] += product[:, t * LANES : (t + 1) * LANES]
        slot(k < 2, 3 * k + 1)

        body = pl.ds(base + HALO, cell)
        for i in range(2):
            dec_sum[i] += lax.dot_general(
                rows_all[1 + i, body, window], h_taps[...], contract_rows,
                preferred_element_type=F32,
            )
        for r in range(6):
            start = r * piece
            for q in range(tiles):
                grad = z_dec[q, pl.ds(start + 9, piece), :]
                for t in range(1, 3):
                    grad += z_dec[t * tiles + q, pl.ds(start + 9 - t, piece), :]
                pre_grad[q, pl.ds(start, piece), :] = grad * slope[q, pl.ds(start, piece), :]
        for r in range(cell // LANES):
            for q in range(tiles):
                for t in range(5):
                    moved = pre_grad[q, pl.ds(r * LANES + EDGE + 2 - t, LANES), :]
                    g_taps[r * LANES : (r + 1) * LANES, t * share + q * LANES : t * share + (q + 1) * LANES] = (
                        moved.astype(BF16)
                    )

        @pl.when(k < last)
        def _():
            across(0, order(k + 1))

        @pl.when((k == 1) & middle)
        def _():
            across(2, order(last))

            @pl.when(z * 2 < last)
            def _():
                turned(to_left).start()

            @pl.when(z * 2 > last)
            def _():
                turned(to_right).start()

        @pl.when(k == last)
        def _():
            give_grads(1)

        enc_sum[...] += lax.dot_general(
            rows_all[0, body, window], g_taps[...], contract_rows, preferred_element_type=F32
        )

        @pl.when(k == 0)
        def _():
            for i in range(3):
                for h in range(2):
                    cols = pl.ds(pl.multiple_of((c if h == 0 else 1 - c) * wide, LANES), wide)
                    rhs = weights[0, cols, :] if i == 0 else folded[i - 1, cols, :]
                    lhs = g_taps[...] if i == 0 else h_taps[...]
                    value = lax.dot_general(lhs, rhs, contract_last, preferred_element_type=F32)
                    if h == 0:
                        part[i] = value
                    else:
                        give[i] = value.astype(BF16)
                if i == 0:
                    slot(k == 0, 2)
            give_copy.start()

        slot(k == 1, 5)

        @pl.when(k == 1)
        def _():
            give_copy.wait_recv()
            sums_over_cores()
            give_y_copy.start()

        return carry

    lax.fori_loop(0, last + 1, cell_step, 0)

    give_grads(0)
    for w in range(2):
        for t, value in enumerate(grads(w, y)):
            grad_refs[w][t, :, lanes(y, share)] = value

    give_y_copy.wait_recv()
    for k in range(tiles):
        cols = slice(k * LANES, (k + 1) * LANES)
        even, odd = pl.ds(0, chunk, stride=2), pl.ds(1, chunk, stride=2)
        own = pl.ds(pl.multiple_of(y * chunk, HALO), chunk)
        pool_grad, first, second = [part[i, own, cols] + take_y[i, :, cols].astype(F32) for i in range(3)]
        spread[k, even, :] = first
        spread[k, odd, :] = second
        spread[tiles + k, even, :] = pool_grad
        spread[tiles + k, odd, :] = pool_grad
        mixed_ref[:, cols] = (x_own[:, cols].astype(F32) + spread[k]).astype(BF16)
        in_grad_ref[:, cols] = (cot_ref[:, cols].astype(F32) + 0.5 * spread[tiles + k]).astype(BF16)

    give_copy.wait_send()
    give_y_copy.wait_send()
    for w in range(2):
        for t in range(taps):
            weight_to_y(w, t, g).wait_send()
            weight_to_y(w, t, 1 - g).wait_send()

    @pl.when(has_left)
    def _():
        edge_out(0, to_left).wait_send()
        for i in range(3):
            inner_out(i, 0, to_left).wait_send()
        for w in range(2):
            for b in range(2):
                weight_z(w, z, b, 0, to_left).wait_send()

    @pl.when(has_right)
    def _():
        edge_out(1, to_right).wait_send()
        for i in range(3):
            inner_out(i, 1, to_right).wait_send()
        for w in range(2):
            for b in range(2):
                weight_z(w, z, b, 1, to_right).wait_send()

    def drain(k, carry):
        zz = order(k)
        edge_to_y(zz).wait_send()
        for yy in range(2):
            edge_to_c(zz, yy).wait_send()
        for i in range(3):
            @pl.when(jnp.logical_not(turns(i, zz)))
            def _():
                inner_to_y(i, zz).wait_send()

            for yy in range(2):
                inner_to_c(i, zz, yy).wait_send()

        @pl.when(k > 0)
        def _():
            for w in range(2):
                for b in range(2):
                    weight_x(w, zz, b, g).wait_send()

        @pl.when((zz < z) & has_right)
        def _():
            edge_forward(zz, to_right).wait_send()
            for i in range(3):
                inner_forward(i, zz, to_right).wait_send()
            for w in range(2):
                for b in range(2):
                    weight_z(w, zz, b, 1, to_right).wait_send()

        @pl.when((zz > z) & has_left)
        def _():
            edge_forward(zz, to_left).wait_send()
            for i in range(3):
                inner_forward(i, zz, to_left).wait_send()
            for w in range(2):
                for b in range(2):
                    weight_z(w, zz, b, 0, to_left).wait_send()

        return carry

    lax.fori_loop(0, last + 1, drain, 0)

    @pl.when(middle)
    def _():
        turned(to_y).wait_send()

    for w in range(2):
        grad_copy(w).wait_send()
    for w in range(2):
        grad_arrives = remote(
            grad_give.at[w], grad_refs[w].at[:, :, lanes(1 - y, share)],
            grad_sem.at[0, w], grad_sem.at[1, w], to_y,
        )
        grad_arrives.wait_recv()


def weight_from_y(weights, sources, send, recv, w, t, side, s, y, half, block, share, to_y, lanes):
    other = s + 1 - 2 * y
    row = pl.multiple_of(other * block + side * half, HALO)
    return pltpu.make_async_remote_copy(
        src_ref=sources[w].at[t, pl.ds(pl.multiple_of(side * half, HALO), half), lanes(1 - y, share)],
        dst_ref=weights.at[w, pl.ds(row, half), pl.ds(t * share, share)],
        send_sem=send.at[w, t, side],
        recv_sem=recv.at[w, t, side],
        device_id=to_y,
        device_id_type=pl.DeviceIdType.MESH,
    )


def pair_call(inputs, enc_taps, dec_taps, cotangent, cells):
    rows, wide = cotangent.shape
    chunk = rows // 2
    taps, block, both = enc_taps.shape
    share = both // 2
    cell = 2 * chunk
    vmem = pl.BlockSpec(memory_space=pltpu.VMEM)
    anywhere = pl.BlockSpec(memory_space=pl.ANY)
    dma = pltpu.SemaphoreType.DMA
    tall = cells * cell + 2 * HALO
    width = 2 * wide
    return pl.pallas_call(
        pair_kernel,
        out_shape=[
            jax.ShapeDtypeStruct((rows, wide), BF16),
            jax.ShapeDtypeStruct((rows, wide), BF16),
            jax.ShapeDtypeStruct((taps, block, both), BF16),
            jax.ShapeDtypeStruct((taps, block, both), BF16),
        ],
        in_specs=[anywhere, anywhere, anywhere, vmem],
        out_specs=[vmem] * 4,
        scratch_shapes=[
            pltpu.VMEM((rows, wide), BF16),
            pltpu.VMEM((2 * (wide // LANES), rows, LANES), F32),
            pltpu.VMEM((3, chunk, wide), BF16),
            pltpu.VMEM((3, tall, width), BF16),
            pltpu.VMEM((2, width, taps * share), BF16),
            pltpu.VMEM((2, width, 3 * share), BF16),
            pltpu.VMEM((taps * share // LANES, cell + 2 * HALO, LANES), F32),
            pltpu.VMEM((3 * share // LANES, cell + 2 * HALO, LANES), F32),
            pltpu.VMEM((share // LANES, cell + 2 * EDGE, LANES), F32),
            pltpu.VMEM((share // LANES, cell + 2 * EDGE, LANES), F32),
            pltpu.VMEM((share // LANES, cell + 2 * EDGE, LANES), F32),
            pltpu.VMEM((cell, taps * share), BF16),
            pltpu.VMEM((cell, 3 * share), BF16),
            pltpu.VMEM((2 * LANES, taps * share), F32),
            pltpu.VMEM((2, 2 * LANES, 3 * share), F32),
            pltpu.VMEM((3, cell, wide), F32),
            pltpu.VMEM((3, cell, wide), BF16),
            pltpu.VMEM((3, cell, wide), BF16),
            pltpu.VMEM((3, chunk, wide), BF16),
            pltpu.VMEM((3, chunk, wide), BF16),
            pltpu.VMEM((2, taps, block, share), BF16),
            dma((2, taps + 3)),
            dma((2, taps, 2)), dma((2, taps, 2)),
            dma((2, 2, cells, 2)), dma((2, cells, 2)), dma((2, cells, 2)), dma((2, cells, 2)),
            dma((2,)), dma((cells,)), dma((cells,)), dma((cells, 2)), dma((cells,)), dma((cells,)),
            dma((cells, 2)),
            dma((2, 3)), dma((cells, 3)), dma((cells, 3)), dma((cells, 3)), dma((cells, 3)),
            dma((cells, 2, 3)), dma((cells, 2, 3)),
            dma((2,)), dma((2,)), dma((2, 2)), dma((2,)),
        ],
        compiler_params=pltpu.CompilerParams(
            collective_id=0, has_side_effects=True, vmem_limit_bytes=58 * 2**20
        ),
        cost_estimate=pl.CostEstimate(
            flops=2 * 11 * cells * cell * width * share + 4 * 11 * cells * cell * block * share,
            bytes_accessed=4 * taps * block * both * 2,
            transcendentals=cells * cell * share,
        ),
    )(inputs, enc_taps, dec_taps, cotangent)


def settle_kernel(*refs):
    count = len(refs) // 3
    arrived, left = refs[3 * count :]
    for i in range(count):
        pltpu.make_async_copy(refs[i], refs[2 * count + i], arrived.at[i]).start()
    for i in range(count):
        pltpu.make_async_copy(refs[i], refs[2 * count + i], arrived.at[i]).wait()
        pltpu.make_async_copy(refs[2 * count + i], refs[count + i], left.at[i]).start()
    for i in range(count):
        pltpu.make_async_copy(refs[2 * count + i], refs[count + i], left.at[i]).wait()


def settle(arrays):
    anywhere = pl.BlockSpec(memory_space=pl.ANY)
    return pl.pallas_call(
        settle_kernel,
        out_shape=[jax.ShapeDtypeStruct(a.shape, a.dtype) for a in arrays],
        in_specs=[anywhere] * len(arrays),
        out_specs=[anywhere] * len(arrays),
        scratch_shapes=[pltpu.VMEM(a.shape, a.dtype) for a in arrays]
        + [pltpu.SemaphoreType.DMA((len(arrays),))] * 2,
    )(*arrays)


def shards(inputs, enc_weight, dec_weight, cotangent):
    parts = lax.axis_size("seq")
    cores = lax.axis_size("chan")
    rows, width = inputs.shape
    chunk = rows // 2
    block, taps, share = enc_weight.shape
    wide = cotangent.shape[1]
    fits = parts == 8 and cores == 2 and lax.axis_size("groups") == 2 and taps == 5
    fits = fits and block == 96 and share == 2 * wide and wide % LANES == 0 and chunk == 256
    if not fits:
        return wide_shards(inputs, enc_weight, dec_weight, cotangent)
    found = pair_call(
        inputs, enc_weight.transpose(1, 0, 2), dec_weight.transpose(1, 0, 2), cotangent, parts // 2
    )
    mixed_out, input_grad, enc_grad, dec_grad = settle(found)
    return mixed_out, input_grad, enc_grad.transpose(1, 0, 2), dec_grad.transpose(1, 0, 2)


def solution(mesh):
    return jax.shard_map(
        shards,
        mesh=mesh,
        in_specs=(
            P(("groups", "seq"), None),
            P("seq", None, "chan"),
            P("seq", None, "chan"),
            P(("groups", "seq"), "chan"),
        ),
        out_specs=(
            P(("groups", "seq"), "chan"),
            P(("groups", "seq"), "chan"),
            P(("groups", "seq"), None, "chan"),
            P(("groups", "seq"), None, "chan"),
        ),
        check_vma=False,
    )
```

```python
import functools
import math

import jax
import jax.numpy as jnp
from jax import lax
from jax.experimental import pallas as pl
from jax.experimental.pallas import tpu as pltpu
from jax.sharding import PartitionSpec as P

BF16 = jnp.bfloat16
F32 = jnp.float32


def shift(array, by):
    length = array.shape[0]
    if by == 0:
        return array
    pad = jnp.zeros((abs(by),) + array.shape[1:], array.dtype)
    if by > 0:
        return jnp.concatenate([array[by:], pad], axis=0)
    return jnp.concatenate([pad, array[: length + by]], axis=0)


def to_columns(array, parts):
    rows, cols = array.shape
    blocks = array.reshape(rows, parts, cols // parts).transpose(1, 0, 2)
    return lax.all_to_all(blocks, "seq", 0, 0, tiled=True)


def to_rows(blocks):
    parts, rows, cols = blocks.shape
    got = lax.all_to_all(blocks, "seq", 0, 0, tiled=True)
    return got.transpose(1, 0, 2).reshape(rows, parts * cols)


PIECES = 2


def ring_place(index, n):
    if n != 8:
        return index
    y = lax.rem(index, 2)
    z = index // 2
    return z + y * (n - 1 - 2 * z)


def ring_index(place, n):
    place = lax.rem(place + 2 * n, n)
    if n != 8:
        return place
    back = place // (n // 2)
    return 2 * place + back * (2 * n - 1 - 4 * place)


def gelu_and_slope(v):
    scale = math.sqrt(2.0 / math.pi)
    square = v * v
    th = jnp.tanh(scale * (v + 0.044715 * square * v))
    up = 0.5 * (1.0 + th)
    slope = up + 0.5 * v * (1.0 - th * th) * (scale * (1.0 + 3.0 * 0.044715 * square))
    return v * up, slope


def ring_kernel(
    n, x_ref, y_ref, enc_ref, dec_ref, out_ref, slots, term, mine,
    rs_send, rs_recv, ag_send, ag_recv, local_sem,
):
    me = lax.axis_index("seq")
    place = ring_place(me, n)
    nexts = (ring_index(place + 1, n), ring_index(place - 1, n))
    half = x_ref.shape[1]
    share = enc_ref.shape[1]
    side = half // 2
    piece = side // PIECES

    barrier = pltpu.get_barrier_semaphore()
    for other in nexts:
        pl.semaphore_signal(
            barrier, inc=1, device_id={"seq": other}, device_id_type=pl.DeviceIdType.MESH
        )
    pl.semaphore_wait(barrier, 2)

    def signed(d, steps):
        return place - steps if d == 0 else place + steps

    def own_term(d, steps):
        chunk = ring_index(signed(d, steps), n)
        at = pl.ds(d * side, side)
        a = jnp.dot(x_ref[chunk, at, :], enc_ref[...], preferred_element_type=jnp.float32)
        b = jnp.dot(y_ref[chunk, at, :], dec_ref[...], preferred_element_type=jnp.float32)
        return a, b

    def rs_copy(d, s, q):
        at = pl.ds(q * piece, piece)
        return pltpu.make_async_remote_copy(
            src_ref=slots.at[d, s, at],
            dst_ref=slots.at[d, s + 1, at],
            send_sem=rs_send.at[d, s, q],
            recv_sem=rs_recv.at[d, s, q],
            device_id={"seq": nexts[d]},
            device_id_type=pl.DeviceIdType.MESH,
        )

    def ag_copy(d, s, q, first):
        at = pl.ds(d * side + q * piece, piece)
        owner = ring_index(signed(d, s), n)
        return pltpu.make_async_remote_copy(
            src_ref=mine.at[at] if first else out_ref.at[owner, at],
            dst_ref=out_ref.at[owner, at],
            send_sem=ag_send.at[d, s, q],
            recv_sem=ag_recv.at[d, s, q],
            device_id={"seq": nexts[d]},
            device_id_type=pl.DeviceIdType.MESH,
        )

    for d in range(2):
        a, b = own_term(d, 1)
        slots[d, 0, :, :share] = a.astype(BF16)
        slots[d, 0, :, share:] = b.astype(BF16)
        for q in range(PIECES):
            rs_copy(d, 0, q).start()

    def fill(s):
        for d in range(2):
            a, b = own_term(d, s + 2)
            term[d, :, :share] = a
            term[d, :, share:] = b

    def rs_step(s, carry):
        fill(s)
        for q in range(PIECES):
            at = pl.ds(q * piece, piece)
            for d in range(2):
                rs_copy(d, s, q).wait_recv()
                total = slots[d, s + 1, at, :].astype(F32) + term[d, at, :]
                slots[d, s + 1, at, :] = total.astype(BF16)
                rs_copy(d, s + 1, q).start()
        return carry

    lax.fori_loop(0, n - 2, rs_step, 0)
    fill(n - 2)
    for q in range(PIECES):
        at = pl.ds(q * piece, piece)
        for d in range(2):
            rs_copy(d, n - 2, q).wait_recv()
            rows = pl.ds(d * side + q * piece, piece)
            pre = slots[d, n - 1, at, :share].astype(F32) + term[d, at, :share]
            grad = slots[d, n - 1, at, share:].astype(F32) + term[d, at, share:]
            value, slope = gelu_and_slope(pre)
            mine[rows, :share] = value.astype(BF16)
            mine[rows, share:] = (grad * slope).astype(BF16)
            ag_copy(d, 0, q, True).start()
    local = pltpu.make_async_copy(mine, out_ref.at[me], local_sem)
    local.start()

    def ag_step(s, carry):
        for q in range(PIECES):
            for d in range(2):
                incoming(d, s, q).wait_recv()
                ag_copy(d, s + 1, q, False).start()
        return carry

    def incoming(d, s, q):
        at = pl.ds(d * side + q * piece, piece)
        owner = ring_index(signed(d, s + 1), n)
        return pltpu.make_async_remote_copy(
            src_ref=mine.at[at],
            dst_ref=out_ref.at[owner, at],
            send_sem=ag_send.at[d, s, q],
            recv_sem=ag_recv.at[d, s, q],
            device_id={"seq": nexts[d]},
            device_id_type=pl.DeviceIdType.MESH,
        )

    lax.fori_loop(0, n - 2, ag_step, 0)
    for q in range(PIECES):
        for d in range(2):
            incoming(d, n - 2, q).wait_recv()

    def drain(s, carry):
        for q in range(PIECES):
            for d in range(2):
                rs_copy(d, s, q).wait_send()
                ag_copy(d, s, q, True).wait_send()
        return carry

    lax.fori_loop(0, n - 1, drain, 0)
    local.wait()


def ring(pool_taps, cot_taps, enc_mat, dec_mat, n):
    half = pool_taps.shape[1]
    share = enc_mat.shape[1]
    depth = enc_mat.shape[0]
    vmem = pl.BlockSpec(memory_space=pltpu.VMEM)
    steps = (2, n - 1, PIECES)
    return pl.pallas_call(
        functools.partial(ring_kernel, n),
        out_shape=jax.ShapeDtypeStruct((n, half, 2 * share), BF16),
        in_specs=[vmem] * 4,
        out_specs=pl.BlockSpec(memory_space=pl.ANY),
        scratch_shapes=[
            pltpu.VMEM((2, n, half // 2, 2 * share), BF16),
            pltpu.VMEM((2, half // 2, 2 * share), F32),
            pltpu.VMEM((half, 2 * share), BF16),
            pltpu.SemaphoreType.DMA(steps),
            pltpu.SemaphoreType.DMA(steps),
            pltpu.SemaphoreType.DMA(steps),
            pltpu.SemaphoreType.DMA(steps),
            pltpu.SemaphoreType.DMA,
        ],
        compiler_params=pltpu.CompilerParams(
            collective_id=0, has_side_effects=True, vmem_limit_bytes=48 * 2**20
        ),
        cost_estimate=pl.CostEstimate(
            flops=4 * n * half * depth * share,
            bytes_accessed=4 * n * half * share * 2,
            transcendentals=half * share,
        ),
    )(pool_taps, cot_taps, enc_mat, dec_mat)


def wide_shards(inputs, enc_weight, dec_weight, cotangent):
    parts = lax.axis_size("seq")
    rows, width = inputs.shape
    half = rows // 2
    total = half * parts
    block, taps, share = enc_weight.shape
    half_width = cotangent.shape[1]

    pooled = (inputs.astype(F32).reshape(half, 2, width).sum(axis=1) * 0.5).astype(BF16)
    cot_full = lax.all_gather(cotangent, "chan", axis=1, tiled=True)
    core = lax.axis_index("chan")
    cores = lax.axis_size("chan")
    few = half // cores
    leaving = jnp.concatenate(
        [
            lax.dynamic_slice_in_dim(pooled, core * few, few, 0),
            lax.dynamic_slice_in_dim(cot_full, core * 2 * few, 2 * few, 0),
        ],
        axis=0,
    )
    columns = to_columns(leaving, parts).reshape(parts, 1, 3 * few, block)
    columns = lax.all_gather(columns, "chan", axis=1, tiled=True)
    pool_col = columns[:, :, :few].reshape(total, block)
    cot_col = columns[:, :, few:].reshape(total, 2, block).astype(F32)
    even = cot_col[:, 0]
    odd = cot_col[:, 1]
    pair = (even + odd).astype(BF16)
    cross = (odd + shift(even, 1)).astype(BF16)
    before = jnp.concatenate([even[:1].astype(BF16), cross[:-1]], axis=0)
    pool_taps = jnp.concatenate([shift(pool_col, t - 2) for t in range(taps)], axis=1)
    cot_taps = jnp.concatenate([shift(pair, 1), cross, pair, before, shift(pair, -1)], axis=1)
    enc_mat = enc_weight.transpose(1, 0, 2).reshape(taps * block, share)
    dec_mat = dec_weight.transpose(1, 0, 2).reshape(taps * block, share)

    joint = ring(
        pool_taps.reshape(parts, half, taps * block),
        cot_taps.reshape(parts, half, taps * block),
        enc_mat,
        dec_mat,
        parts,
    ).reshape(total, 2 * share)
    hidden_all = joint[:, :share]
    grad_all = joint[:, share:]

    contract_rows = (((0,), (0,)), ((), ()))
    contract_last = (((1,), (1,)), ((), ()))
    dec_grad = lax.dot_general(cot_taps, hidden_all, contract_rows, preferred_element_type=F32)
    enc_grad = lax.dot_general(pool_taps, grad_all, contract_rows, preferred_element_type=F32)
    dec_grad = dec_grad.astype(BF16).reshape(taps, block, share).transpose(1, 0, 2)
    enc_grad = enc_grad.astype(BF16).reshape(taps, block, share).transpose(1, 0, 2)

    dec_out = lax.dot_general(hidden_all, dec_mat, contract_last, preferred_element_type=F32)
    p0, p1, p2, p3, p4 = [dec_out[:, t * block : (t + 1) * block] for t in range(taps)]
    after4 = shift(p4, 1)
    before0 = shift(p0, -1)
    dec_even = before0 + shift(p1, -1) + p2 + p3 + after4
    dec_odd = before0 + p1 + p2 + shift(p3, 1) + after4
    decoded = jnp.stack([dec_even, dec_odd], axis=1).astype(BF16).reshape(parts, rows, block)
    enc_out = lax.dot_general(grad_all, enc_mat, contract_last, preferred_element_type=F32)
    pool_grad = sum(shift(enc_out[:, t * block : (t + 1) * block], 2 - t) for t in range(taps))
    pool_grad = pool_grad.astype(BF16).reshape(parts, half, block)
    mine = jnp.concatenate([decoded, pool_grad], axis=1)
    mine = lax.psum_scatter(mine, "chan", scatter_dimension=1, tiled=True)
    mine = lax.all_gather(to_rows(mine), "chan", axis=0, tiled=True)
    col_start = core * half_width
    mine = lax.dynamic_slice_in_dim(mine, col_start, half_width, 1).astype(F32)

    skip = lax.dynamic_slice_in_dim(inputs, col_start, half_width, 1)
    mixed_out = (skip.astype(F32) + mine[:rows]).astype(BF16)
    input_grad = (cotangent.astype(F32) + 0.5 * jnp.repeat(mine[rows:], 2, axis=0)).astype(BF16)
    return mixed_out, input_grad, enc_grad, dec_grad


LANES = 128
HALO = 16
EDGE = 8


def pair_kernel(
    x_ref, enc_ref, dec_ref, cot_ref, mixed_ref, in_grad_ref, enc_grad_ref, dec_grad_ref,
    x_own, spread, pc_ref, rows_all, weights, folded, z_enc, z_dec, hid, slope, pre_grad, g_taps, h_taps,
    enc_sum, dec_sum, part, give, take, give_y, take_y, grad_give,
    local_sem, wy_send, wy_recv, wz_send, wz_recv, wx_send, wx_recv,
    edge_send, edge_z, edge_y, edge_c, edge_fwd, edge_ysend, edge_csend,
    own_send, pz_send, pz_recv, py_send, py_recv, pc_send, pc_recv,
    give_sem, take_sem, grad_sem, turn_sem,
):
    g = lax.axis_index("groups")
    s = lax.axis_index("seq")
    c = lax.axis_index("chan")
    z, y = s // 2, lax.rem(s, 2)
    last = lax.axis_size("seq") // 2 - 1
    chunk, wide = pc_ref.shape[1], pc_ref.shape[2]
    cell = 2 * chunk
    taps, block = enc_ref.shape[0], enc_ref.shape[1]
    share = enc_ref.shape[2] // 2
    half = block // 2
    inner = chunk - HALO
    ids = pl.DeviceIdType.MESH
    to_y, to_x, to_c = {"seq": s + 1 - 2 * y}, {"groups": 1 - g}, {"chan": 1 - c}
    to_left, to_right = {"seq": s - 2}, {"seq": s + 2}
    has_left, has_right = z > 0, z < last

    def lanes(index, width):
        return pl.ds(pl.multiple_of(index * width, LANES), width)

    own_x = pltpu.make_async_copy(x_ref.at[:, lanes(c, wide)], x_own, local_sem.at[0, taps + 1])
    own_x.start()
    sources = (enc_ref, dec_ref)
    grad_refs = (enc_grad_ref, dec_grad_ref)

    def own_weight(w, t):
        return pltpu.make_async_copy(
            sources[w].at[t, :, lanes(y, share)],
            weights.at[w, pl.ds(pl.multiple_of(s * block, HALO), block), pl.ds(t * share, share)],
            local_sem.at[w, t],
        )

    for w in range(2):
        for t in range(taps):
            own_weight(w, t).start()

    barrier = pltpu.get_barrier_semaphore()
    for where in (to_y, to_x, to_c):
        pl.semaphore_signal(barrier, inc=1, device_id=where, device_id_type=ids)

    @pl.when(has_left)
    def _():
        pl.semaphore_signal(barrier, inc=1, device_id=to_left, device_id_type=ids)

    @pl.when(has_right)
    def _():
        pl.semaphore_signal(barrier, inc=1, device_id=to_right, device_id_type=ids)

    inside = jnp.where(has_left, 1, 0) + jnp.where(has_right, 1, 0)
    pl.semaphore_wait(barrier, 3 + inside)

    def remote(src, dst, send, recv, where):
        return pltpu.make_async_remote_copy(
            src_ref=src, dst_ref=dst, send_sem=send, recv_sem=recv,
            device_id=where, device_id_type=ids,
        )

    def weight_to_y(w, t, side):
        at = pl.ds(pl.multiple_of(side * half, HALO), half)
        row = pl.multiple_of(s * block + side * half, HALO)
        return remote(
            sources[w].at[t, at, lanes(1 - y, share)],
            weights.at[w, pl.ds(row, half), pl.ds(t * share, share)],
            wy_send.at[w, t, side], wy_recv.at[w, t, side], to_y,
        )

    def slab(w, b, side):
        return weights.at[w, pl.ds(pl.multiple_of(b * block + side * half, HALO), half), :]

    def weight_z(w, zz, b, d, where):
        ref = slab(w, 2 * zz + b, g)
        return remote(ref, ref, wz_send.at[d, w, zz, b], wz_recv.at[w, zz, b], where)

    def weight_x(w, zz, b, side):
        ref = slab(w, 2 * zz + b, side)
        return remote(ref, ref, wx_send.at[w, zz, b], wx_recv.at[w, zz, b], to_x)

    def edge_of(zz, yy, cc):
        at = pl.multiple_of(HALO + (2 * zz + yy) * chunk + yy * inner, HALO)
        return rows_all.at[:, pl.ds(at, HALO), lanes(cc, wide)]

    def inner_of(i, zz, yy, cc):
        at = pl.multiple_of(HALO + (2 * zz + yy) * chunk + (1 - yy) * HALO, HALO)
        return rows_all.at[i, pl.ds(at, inner), lanes(cc, wide)]

    own_edge = pc_ref.at[:, pl.ds(pl.multiple_of(y * inner, HALO), HALO), :]

    def own_inner(i):
        return pc_ref.at[i, pl.ds(pl.multiple_of((1 - y) * HALO, HALO), inner), :]

    local_edge = pltpu.make_async_copy(own_edge, edge_of(z, y, c), local_sem.at[0, taps])
    local_inner = [
        pltpu.make_async_copy(own_inner(i), inner_of(i, z, y, c), local_sem.at[1, taps + i])
        for i in range(3)
    ]

    for w in range(2):
        for t in range(taps):
            weight_to_y(w, t, g).start()

    for w in range(2):
        for t in range(taps):
            own_weight(w, t).wait()

        @pl.when(has_left)
        def _():
            weight_z(w, z, y, 0, to_left).start()

        @pl.when(has_right)
        def _():
            weight_z(w, z, y, 1, to_right).start()

    def edge_out(d, where):
        return remote(own_edge, edge_of(z, y, c), edge_send.at[d], edge_z.at[z], where)

    def edge_forward(zz, where):
        ref = edge_of(zz, y, c)
        return remote(ref, ref, edge_fwd.at[zz], edge_z.at[zz], where)

    def edge_to_y(zz):
        src = edge_of(zz, y, c)
        return remote(src, src, edge_ysend.at[zz], edge_y.at[zz], to_y)

    def edge_to_c(zz, yy):
        ref = edge_of(zz, yy, c)
        return remote(ref, ref, edge_csend.at[zz, yy], edge_c.at[zz, yy], to_c)

    tiles = wide // LANES
    own_x.wait()
    for k in range(tiles):
        cols = slice(k * LANES, (k + 1) * LANES)
        spread[k] = x_own[:, cols].astype(F32)
        spread[tiles + k] = cot_ref[:, cols].astype(F32)
    for k in range(tiles):
        cols = slice(k * LANES, (k + 1) * LANES)
        even, odd = pl.ds(0, chunk, stride=2), pl.ds(1, chunk, stride=2)
        pc_ref[0, :, cols] = ((spread[k, even, :] + spread[k, odd, :]) * 0.5).astype(BF16)
        pc_ref[1, :, cols] = spread[tiles + k, even, :].astype(BF16)
        pc_ref[2, :, cols] = spread[tiles + k, odd, :].astype(BF16)

    local_edge.start()

    @pl.when(has_left)
    def _():
        edge_out(0, to_left).start()

    @pl.when(has_right)
    def _():
        edge_out(1, to_right).start()

    for copy in local_inner:
        copy.start()
    rows_all[:, :HALO, :] = jnp.zeros((3, HALO, 2 * wide), BF16)
    bottom = rows_all.shape[1] - HALO
    rows_all[:, bottom:, :] = jnp.zeros((3, HALO, 2 * wide), BF16)
    local_edge.wait()
    edge_to_y(z).start()
    edge_to_c(z, y).start()

    for w in range(2):
        for t in range(taps):
            weight_from_y(
                weights, sources, wy_send, wy_recv, w, t, g, s, y, half, block, share, to_y, lanes
            ).wait_recv()

        @pl.when(has_left)
        def _():
            weight_z(w, z, 1 - y, 0, to_left).start()

        @pl.when(has_right)
        def _():
            weight_z(w, z, 1 - y, 1, to_right).start()

    for w in range(2):
        for t in range(taps):
            weight_to_y(w, t, 1 - g).start()

    def inner_to_y(i, zz):
        ref = inner_of(i, zz, y, c)
        return remote(ref, ref, py_send.at[zz, i], py_recv.at[zz, i], to_y)

    def inner_to_c(i, zz, yy):
        ref = inner_of(i, zz, yy, c)
        return remote(ref, ref, pc_send.at[zz, yy, i], pc_recv.at[zz, yy, i], to_c)

    def inner_out(i, d, where):
        return remote(own_inner(i), inner_of(i, z, y, c), own_send.at[d, i], pz_recv.at[z, i], where)

    for i in range(3):
        local_inner[i].wait()
        inner_to_y(i, z).start()
        inner_to_c(i, z, y).start()

    def order(k):
        low = jnp.minimum(z, last - z)
        near = jnp.where(low == 0, k, jnp.where(k < 2, 1 - k, k))
        return jnp.where(z * 2 < last, near, last - near)

    def edge_arrives_y(zz):
        ref = edge_of(zz, 1 - y, c)
        return remote(ref, ref, edge_ysend.at[zz], edge_y.at[zz], to_y)

    def send_own_rows(d, where):
        for i in range(3):
            inner_out(i, d, where).start()

    @pl.when(z == 0)
    def _():
        send_own_rows(1, to_right)

    @pl.when(z == last)
    def _():
        send_own_rows(0, to_left)

    def weight_step(k, carry):
        for sign in (-1, 1):
            zz = z + sign * k

            @pl.when((zz >= 0) & (zz <= last))
            def _():
                for w in range(2):
                    for b in range(2):
                        weight_z(w, zz, b, 0, to_y).wait_recv()

                        if sign < 0:
                            @pl.when(has_right)
                            def _():
                                weight_z(w, zz, b, 1, to_right).start()
                        else:
                            @pl.when(has_left)
                            def _():
                                weight_z(w, zz, b, 0, to_left).start()

                        weight_x(w, zz, b, g).start()

                edge_forward(zz, to_y).wait_recv()
                if sign < 0:
                    @pl.when(has_right)
                    def _():
                        edge_forward(zz, to_right).start()
                else:
                    @pl.when(has_left)
                    def _():
                        edge_forward(zz, to_left).start()

                edge_to_y(zz).start()
                edge_to_c(zz, y).start()

        @pl.when((z == k) & has_right)
        def _():
            send_own_rows(1, to_right)

        @pl.when((last - z == k) & has_left)
        def _():
            send_own_rows(0, to_left)

        return carry

    lax.fori_loop(1, last + 1, weight_step, 0)

    def inner_forward(i, zz, where):
        ref = inner_of(i, zz, y, c)
        return remote(ref, ref, pz_send.at[zz, i], pz_recv.at[zz, i], where)

    def receive(i, zz):
        inner_forward(i, zz, to_y).wait_recv()

        @pl.when((zz < z) & has_right)
        def _():
            inner_forward(i, zz, to_right).start()

        @pl.when((zz > z) & has_left)
        def _():
            inner_forward(i, zz, to_left).start()

        @pl.when(jnp.logical_not(turns(i, zz)))
        def _():
            inner_to_y(i, zz).start()

        inner_to_c(i, zz, y).start()

    def edge_end(zz, carry):
        edge_arrives_y(zz).wait_recv()
        edge_to_c(zz, 1 - y).start()
        return carry

    lax.fori_loop(0, last + 1, edge_end, 0)

    corner = (z == 0) | (z == last)

    def turned(where):
        ref = inner_of(2, order(last), 1 - y, c)
        return remote(ref, ref, turn_sem.at[0], turn_sem.at[1], where)

    def turns(i, zz):
        return corner & (zz == order(last)) & (i == 2)

    def across(i, zz):
        @pl.when(jnp.logical_not(turns(i, zz)))
        def _():
            ref = inner_of(i, zz, 1 - y, c)
            remote(ref, ref, py_send.at[zz, i], py_recv.at[zz, i], to_y).wait_recv()

        if i == 2:
            @pl.when(turns(i, zz))
            def _():
                turned(to_y).wait_recv()

        inner_to_c(i, zz, 1 - y).start()

    across(0, z)
    middle = has_left & has_right

    def receive_step(k, carry):
        for i in range(3):
            receive(i, order(k))
        return carry

    lax.fori_loop(1, jnp.where(middle, last + 1, 2), receive_step, 0)

    for zz in range(last + 1):
        for yy in range(2):
            ref = edge_of(zz, yy, 1 - c)
            remote(ref, ref, edge_csend.at[zz, yy], edge_c.at[zz, yy], to_c).wait_recv()

    def each_other_cell(body):
        def step(k, carry):
            body(order(k))
            return carry

        lax.fori_loop(1, last + 1, step, 0)

    for w in range(2):
        for t in range(taps):
            weight_from_y(
                weights, sources, wy_send, wy_recv, w, t, 1 - g, s, y, half, block, share, to_y, lanes
            ).wait_recv()

    def wait_x(zz):
        for w in range(2):
            for b in range(2):
                weight_x(w, zz, b, 1 - g).wait_recv()

    each_other_cell(wait_x)

    step_rows = 64

    def fold(i, carry):
        at = pl.ds(pl.multiple_of(i * step_rows, HALO), step_rows)
        w = [weights[1, at, t * share : (t + 1) * share].astype(F32) for t in range(5)]
        folded[0, at, :share] = (w[0] + w[1]).astype(BF16)
        folded[0, at, share : 2 * share] = (w[2] + w[3]).astype(BF16)
        folded[0, at, 2 * share :] = weights[1, at, 4 * share :]
        folded[1, at, :share] = weights[1, at, :share]
        folded[1, at, share : 2 * share] = (w[1] + w[2]).astype(BF16)
        folded[1, at, 2 * share :] = (w[3] + w[4]).astype(BF16)
        return carry

    lax.fori_loop(0, weights.shape[1] // step_rows, fold, 0)

    contract_rows = (((0,), (0,)), ((), ()))
    contract_last = (((1,), (1,)), ((), ()))
    wide_rows = cell + 2 * HALO
    mid_rows = cell + 2 * EDGE
    window = pl.ds(pl.multiple_of((2 * block * z) // LANES * LANES, LANES), 2 * LANES)
    offset = 2 * block * z - (2 * block * z) // LANES * LANES

    enc_sum[...] = jnp.zeros_like(enc_sum)
    dec_sum[...] = jnp.zeros_like(dec_sum)

    def sums_over_cores():
        for i in range(3):
            total = part[i] + take[i].astype(F32)
            part[i] = total
            rows = pl.ds(pl.multiple_of((1 - y) * chunk, HALO), chunk)
            give_y[i] = part[i, rows, :].astype(BF16)

    give_copy = remote(give, take, give_sem.at[0], take_sem.at[0], to_c)
    give_y_copy = remote(give_y, take_y, give_sem.at[1], take_sem.at[1], to_y)

    def grad_copy(w):
        return remote(
            grad_give.at[w], grad_refs[w].at[:, :, lanes(y, share)], grad_sem.at[0, w], grad_sem.at[1, w], to_y
        )

    def grads(w, who):
        at = pl.ds(pl.multiple_of(offset + who * block, HALO), block)
        if w == 0:
            return [enc_sum[at, t * share : (t + 1) * share].astype(BF16) for t in range(5)]
        e = [dec_sum[0, at, k * share : (k + 1) * share] for k in range(3)]
        o = [dec_sum[1, at, k * share : (k + 1) * share] for k in range(3)]
        both = (e[0] + o[0], e[0] + o[1], e[1] + o[1], e[1] + o[2], e[2] + o[2])
        return [v.astype(BF16) for v in both]

    def give_grads(w):
        for t, value in enumerate(grads(w, 1 - y)):
            grad_give[w, t] = value
        grad_copy(w).start()

    def cell_step(k, carry):
        zz = order(k)

        def slot(when, q):
            @pl.when(when & ((z == 0) | (z == last)) & (q < 3 * (last - 1)))
            def _():
                receive(lax.rem(q, 3), order(2 + q // 3))

        def landed(i):
            for yy in range(2):
                ref = inner_of(i, zz, yy, 1 - c)
                remote(ref, ref, pc_send.at[zz, yy, i], pc_recv.at[zz, yy, i], to_c).wait_recv()

        across(1, zz)
        landed(0)

        base = pl.multiple_of(zz * cell, HALO)
        at = pl.ds(base, wide_rows)
        product = jnp.dot(rows_all[0, at, :], weights[0], preferred_element_type=F32)
        for t in range(5 * tiles):
            z_enc[t] = product[:, t * LANES : (t + 1) * LANES]
        slot(k < 2, 3 * k)

        @pl.when((k < last) | corner)
        def _():
            across(2, zz)

        landed(1)
        product = jnp.dot(rows_all[1, at, :], folded[0], preferred_element_type=F32)
        for t in range(3 * tiles):
            z_dec[t] = product[:, t * LANES : (t + 1) * LANES]
        landed(2)

        piece = mid_rows // 6
        product = jnp.dot(rows_all[2, at, :], folded[1], preferred_element_type=F32)
        for r in range(6):
            start = r * piece
            for q in range(tiles):
                pre = z_enc[q, pl.ds(start + 6, piece), :]
                for t in range(1, 5):
                    pre += z_enc[t * tiles + q, pl.ds(start + 6 + t, piece), :]
                value, up = gelu_and_slope(pre)
                row = lax.broadcasted_iota(jnp.int32, (piece, LANES), 0)
                if r == 0:
                    keep = (row >= EDGE) | (zz > 0)
                    value, up = jnp.where(keep, value, 0.0), jnp.where(keep, up, 0.0)
                if r == 5:
                    keep = (row < piece - EDGE) | (zz < last)
                    value, up = jnp.where(keep, value, 0.0), jnp.where(keep, up, 0.0)
                hid[q, pl.ds(start, piece), :] = value
                slope[q, pl.ds(start, piece), :] = up
        for r in range(cell // LANES):
            for q in range(tiles):
                for t in range(3):
                    moved = hid[q, pl.ds(r * LANES + EDGE - 1 + t, LANES), :]
                    h_taps[r * LANES : (r + 1) * LANES, t * share + q * LANES : t * share + (q + 1) * LANES] = (
                        moved.astype(BF16)
                    )
        for t in range(3 * tiles):
            z_dec[t] += product[:, t * LANES : (t + 1) * LANES]
        slot(k < 2, 3 * k + 1)

        body = pl.ds(base + HALO, cell)
        for i in range(2):
            dec_sum[i] += lax.dot_general(
                rows_all[1 + i, body, window], h_taps[...], contract_rows,
                preferred_element_type=F32,
            )
        for r in range(6):
            start = r * piece
            for q in range(tiles):
                grad = z_dec[q, pl.ds(start + 9, piece), :]
                for t in range(1, 3):
                    grad += z_dec[t * tiles + q, pl.ds(start + 9 - t, piece), :]
                pre_grad[q, pl.ds(start, piece), :] = grad * slope[q, pl.ds(start, piece), :]
        for r in range(cell // LANES):
            for q in range(tiles):
                for t in range(5):
                    moved = pre_grad[q, pl.ds(r * LANES + EDGE + 2 - t, LANES), :]
                    g_taps[r * LANES : (r + 1) * LANES, t * share + q * LANES : t * share + (q + 1) * LANES] = (
                        moved.astype(BF16)
                    )

        @pl.when(k < last)
        def _():
            across(0, order(k + 1))

        @pl.when((k == 1) & middle)
        def _():
            across(2, order(last))

            @pl.when(z * 2 < last)
            def _():
                turned(to_left).start()

            @pl.when(z * 2 > last)
            def _():
                turned(to_right).start()

        @pl.when(k == last)
        def _():
            give_grads(1)

        enc_sum[...] += lax.dot_general(
            rows_all[0, body, window], g_taps[...], contract_rows, preferred_element_type=F32
        )

        @pl.when(k == 0)
        def _():
            for i in range(3):
                for h in range(2):
                    cols = pl.ds(pl.multiple_of((c if h == 0 else 1 - c) * wide, LANES), wide)
                    rhs = weights[0, cols, :] if i == 0 else folded[i - 1, cols, :]
                    lhs = g_taps[...] if i == 0 else h_taps[...]
                    value = lax.dot_general(lhs, rhs, contract_last, preferred_element_type=F32)
                    if h == 0:
                        part[i] = value
                    else:
                        give[i] = value.astype(BF16)
                if i == 0:
                    slot(k == 0, 2)
            give_copy.start()

        slot(k == 1, 5)

        @pl.when(k == 1)
        def _():
            give_copy.wait_recv()
            sums_over_cores()
            give_y_copy.start()

        return carry

    lax.fori_loop(0, last + 1, cell_step, 0)

    give_grads(0)
    for w in range(2):
        for t, value in enumerate(grads(w, y)):
            grad_refs[w][t, :, lanes(y, share)] = value

    give_y_copy.wait_recv()
    for k in range(tiles):
        cols = slice(k * LANES, (k + 1) * LANES)
        even, odd = pl.ds(0, chunk, stride=2), pl.ds(1, chunk, stride=2)
        own = pl.ds(pl.multiple_of(y * chunk, HALO), chunk)
        pool_grad, first, second = [part[i, own, cols] + take_y[i, :, cols].astype(F32) for i in range(3)]
        spread[k, even, :] = first
        spread[k, odd, :] = second
        spread[tiles + k, even, :] = pool_grad
        spread[tiles + k, odd, :] = pool_grad
        mixed_ref[:, cols] = (x_own[:, cols].astype(F32) + spread[k]).astype(BF16)
        in_grad_ref[:, cols] = (cot_ref[:, cols].astype(F32) + 0.5 * spread[tiles + k]).astype(BF16)

    give_copy.wait_send()
    give_y_copy.wait_send()
    for w in range(2):
        for t in range(taps):
            weight_to_y(w, t, g).wait_send()
            weight_to_y(w, t, 1 - g).wait_send()

    @pl.when(has_left)
    def _():
        edge_out(0, to_left).wait_send()
        for i in range(3):
            inner_out(i, 0, to_left).wait_send()
        for w in range(2):
            for b in range(2):
                weight_z(w, z, b, 0, to_left).wait_send()

    @pl.when(has_right)
    def _():
        edge_out(1, to_right).wait_send()
        for i in range(3):
            inner_out(i, 1, to_right).wait_send()
        for w in range(2):
            for b in range(2):
                weight_z(w, z, b, 1, to_right).wait_send()

    def drain(k, carry):
        zz = order(k)
        edge_to_y(zz).wait_send()
        for yy in range(2):
            edge_to_c(zz, yy).wait_send()
        for i in range(3):
            @pl.when(jnp.logical_not(turns(i, zz)))
            def _():
                inner_to_y(i, zz).wait_send()

            for yy in range(2):
                inner_to_c(i, zz, yy).wait_send()

        @pl.when(k > 0)
        def _():
            for w in range(2):
                for b in range(2):
                    weight_x(w, zz, b, g).wait_send()

        @pl.when((zz < z) & has_right)
        def _():
            edge_forward(zz, to_right).wait_send()
            for i in range(3):
                inner_forward(i, zz, to_right).wait_send()
            for w in range(2):
                for b in range(2):
                    weight_z(w, zz, b, 1, to_right).wait_send()

        @pl.when((zz > z) & has_left)
        def _():
            edge_forward(zz, to_left).wait_send()
            for i in range(3):
                inner_forward(i, zz, to_left).wait_send()
            for w in range(2):
                for b in range(2):
                    weight_z(w, zz, b, 0, to_left).wait_send()

        return carry

    lax.fori_loop(0, last + 1, drain, 0)

    @pl.when(middle)
    def _():
        turned(to_y).wait_send()

    for w in range(2):
        grad_copy(w).wait_send()
    for w in range(2):
        grad_arrives = remote(
            grad_give.at[w], grad_refs[w].at[:, :, lanes(1 - y, share)],
            grad_sem.at[0, w], grad_sem.at[1, w], to_y,
        )
        grad_arrives.wait_recv()


def weight_from_y(weights, sources, send, recv, w, t, side, s, y, half, block, share, to_y, lanes):
    other = s + 1 - 2 * y
    row = pl.multiple_of(other * block + side * half, HALO)
    return pltpu.make_async_remote_copy(
        src_ref=sources[w].at[t, pl.ds(pl.multiple_of(side * half, HALO), half), lanes(1 - y, share)],
        dst_ref=weights.at[w, pl.ds(row, half), pl.ds(t * share, share)],
        send_sem=send.at[w, t, side],
        recv_sem=recv.at[w, t, side],
        device_id=to_y,
        device_id_type=pl.DeviceIdType.MESH,
    )


def pair_call(inputs, enc_taps, dec_taps, cotangent, cells):
    rows, wide = cotangent.shape
    chunk = rows // 2
    taps, block, both = enc_taps.shape
    share = both // 2
    cell = 2 * chunk
    vmem = pl.BlockSpec(memory_space=pltpu.VMEM)
    anywhere = pl.BlockSpec(memory_space=pl.ANY)
    dma = pltpu.SemaphoreType.DMA
    tall = cells * cell + 2 * HALO
    width = 2 * wide
    return pl.pallas_call(
        pair_kernel,
        out_shape=[
            jax.ShapeDtypeStruct((rows, wide), BF16),
            jax.ShapeDtypeStruct((rows, wide), BF16),
            jax.ShapeDtypeStruct((taps, block, both), BF16),
            jax.ShapeDtypeStruct((taps, block, both), BF16),
        ],
        in_specs=[anywhere, anywhere, anywhere, vmem],
        out_specs=[vmem] * 4,
        scratch_shapes=[
            pltpu.VMEM((rows, wide), BF16),
            pltpu.VMEM((2 * (wide // LANES), rows, LANES), F32),
            pltpu.VMEM((3, chunk, wide), BF16),
            pltpu.VMEM((3, tall, width), BF16),
            pltpu.VMEM((2, width, taps * share), BF16),
            pltpu.VMEM((2, width, 3 * share), BF16),
            pltpu.VMEM((taps * share // LANES, cell + 2 * HALO, LANES), F32),
            pltpu.VMEM((3 * share // LANES, cell + 2 * HALO, LANES), F32),
            pltpu.VMEM((share // LANES, cell + 2 * EDGE, LANES), F32),
            pltpu.VMEM((share // LANES, cell + 2 * EDGE, LANES), F32),
            pltpu.VMEM((share // LANES, cell + 2 * EDGE, LANES), F32),
            pltpu.VMEM((cell, taps * share), BF16),
            pltpu.VMEM((cell, 3 * share), BF16),
            pltpu.VMEM((2 * LANES, taps * share), F32),
            pltpu.VMEM((2, 2 * LANES, 3 * share), F32),
            pltpu.VMEM((3, cell, wide), F32),
            pltpu.VMEM((3, cell, wide), BF16),
            pltpu.VMEM((3, cell, wide), BF16),
            pltpu.VMEM((3, chunk, wide), BF16),
            pltpu.VMEM((3, chunk, wide), BF16),
            pltpu.VMEM((2, taps, block, share), BF16),
            dma((2, taps + 3)),
            dma((2, taps, 2)), dma((2, taps, 2)),
            dma((2, 2, cells, 2)), dma((2, cells, 2)), dma((2, cells, 2)), dma((2, cells, 2)),
            dma((2,)), dma((cells,)), dma((cells,)), dma((cells, 2)), dma((cells,)), dma((cells,)),
            dma((cells, 2)),
            dma((2, 3)), dma((cells, 3)), dma((cells, 3)), dma((cells, 3)), dma((cells, 3)),
            dma((cells, 2, 3)), dma((cells, 2, 3)),
            dma((2,)), dma((2,)), dma((2, 2)), dma((2,)),
        ],
        compiler_params=pltpu.CompilerParams(
            collective_id=0, has_side_effects=True, vmem_limit_bytes=58 * 2**20
        ),
        cost_estimate=pl.CostEstimate(
            flops=2 * 11 * cells * cell * width * share + 4 * 11 * cells * cell * block * share,
            bytes_accessed=4 * taps * block * both * 2,
            transcendentals=cells * cell * share,
        ),
    )(inputs, enc_taps, dec_taps, cotangent)


def settle_kernel(*refs):
    count = len(refs) // 3
    arrived, left = refs[3 * count :]
    parts = []
    for i in range(count):
        group = (refs[i], refs[2 * count + i], refs[count + i])
        if len(refs[i].shape) == 2:
            parts.append(group)
        else:
            parts += [tuple(r.at[t] for r in group) for t in range(refs[i].shape[0])]
    come = [pltpu.make_async_copy(a, b, arrived.at[j]) for j, (a, b, _) in enumerate(parts)]
    leave = [pltpu.make_async_copy(b, o, left.at[j]) for j, (_, b, o) in enumerate(parts)]
    for copy in come:
        copy.start()
    for first, second in zip(come, leave):
        first.wait()
        second.start()
    for copy in leave:
        copy.wait()


def settle(arrays):
    anywhere = pl.BlockSpec(memory_space=pl.ANY)
    return pl.pallas_call(
        settle_kernel,
        out_shape=[jax.ShapeDtypeStruct(a.shape, a.dtype) for a in arrays],
        in_specs=[anywhere] * len(arrays),
        out_specs=[anywhere] * len(arrays),
        scratch_shapes=[pltpu.VMEM(a.shape, a.dtype) for a in arrays]
        + [pltpu.SemaphoreType.DMA((2 + 2 * arrays[2].shape[0],))] * 2,
    )(*arrays)


def shards(inputs, enc_weight, dec_weight, cotangent):
    parts = lax.axis_size("seq")
    cores = lax.axis_size("chan")
    rows, width = inputs.shape
    chunk = rows // 2
    block, taps, share = enc_weight.shape
    wide = cotangent.shape[1]
    fits = parts == 8 and cores == 2 and lax.axis_size("groups") == 2 and taps == 5
    fits = fits and block == 96 and share == 2 * wide and wide % LANES == 0 and chunk == 256
    if not fits:
        return wide_shards(inputs, enc_weight, dec_weight, cotangent)
    found = pair_call(
        inputs, enc_weight.transpose(1, 0, 2), dec_weight.transpose(1, 0, 2), cotangent, parts // 2
    )
    mixed_out, input_grad, enc_grad, dec_grad = settle(found)
    return mixed_out, input_grad, enc_grad.transpose(1, 0, 2), dec_grad.transpose(1, 0, 2)


def solution(mesh):
    return jax.shard_map(
        shards,
        mesh=mesh,
        in_specs=(
            P(("groups", "seq"), None),
            P("seq", None, "chan"),
            P("seq", None, "chan"),
            P(("groups", "seq"), "chan"),
        ),
        out_specs=(
            P(("groups", "seq"), "chan"),
            P(("groups", "seq"), "chan"),
            P(("groups", "seq"), None, "chan"),
            P(("groups", "seq"), None, "chan"),
        ),
        check_vma=False,
    )
```
